32 devices in a mesh: dp: 8 (over z, x), mp: 4 (over y, core).
Axes of the slice: x: 2, y: 2, z: 4, core: 2. Of those that a mesh axis runs over, the one named last changes fastest.
Arguments:
- patches: bfloat16 [8, 2048, 768], P('dp'), may hold values from -6 to 6
- cotangent: bfloat16 [8, 2048, 768], P('dp'), may hold values from -6 to 6
- keep_mask: int32 [8, 2048], P('dp'), may hold values from 0 to 1, as said below
- segment_ids: int32 [8, 2048], P('dp'), may hold values from 0 to 7, never falling along the last dimension, each value on 1 to 512 neighbouring positions
- step_count: int32 [1], replicated, may hold values from 2 to 8
- qkv_weight: float32 [3, 768, 768], P(None, None, 'mp'), may hold values from -0.21875 to 0.21875
- qkv_first: float32 [3, 768, 768], P(None, 'dp', 'mp'), may hold values from -0.00061035156 to 0.00061035156
- qkv_second: float32 [3, 768, 768], P(None, 'dp', 'mp'), may hold values from 7.4315953e-09 to 2.9669868e-08
- out_weight: float32 [768, 768], P('mp'), may hold values from -1.75 to 1.75
- out_first: float32 [768, 768], P('mp', 'dp'), may hold values from -0.00061035156 to 0.00061035156
- out_second: float32 [768, 768], P('mp', 'dp'), may hold values from 7.4315953e-09 to 2.9669868e-08
- up_weight: float32 [768, 3072], P(None, 'mp'), may hold values from -0.21875 to 0.21875
- up_first: float32 [768, 3072], P('dp', 'mp'), may hold values from -0.00061035156 to 0.00061035156
- up_second: float32 [768, 3072], P('dp', 'mp'), may hold values from 7.4315953e-09 to 2.9669868e-08
- down_weight: float32 [3072, 768], P('mp'), may hold values from -0.109375 to 0.109375
- down_first: float32 [3072, 768], P('mp', 'dp'), may hold values from -0.00061035156 to 0.00061035156
- down_second: float32 [3072, 768], P('mp', 'dp'), may hold values from 7.4315953e-09 to 2.9669868e-08
- head_params: float32 [5, 12, 64], P(None, 'mp'), may hold values from -2 to 2, as said below
- head_first: float32 [5, 12, 64], P(None, 'mp'), may hold values from -0.00061035156 to 0.00061035156
- head_second: float32 [5, 12, 64], P(None, 'mp'), may hold values from 7.4315953e-09 to 2.9669868e-08
- up_bias: float32 [3072], P('mp'), may hold values from -2 to 2
- upb_first: float32 [3072], P('mp'), may hold values from -0.00061035156 to 0.00061035156
- upb_second: float32 [3072], P('mp'), may hold values from 7.4315953e-09 to 2.9669868e-08
- vec_params: float32 [6, 768], replicated, may hold values from -2 to 2, as said below
- vec_first: float32 [6, 768], replicated, may hold values from -0.00061035156 to 0.00061035156
- vec_second: float32 [6, 768], replicated, may hold values from 7.4315953e-09 to 2.9669868e-08
Outputs:
- block_out: bfloat16 [8, 2048, 768], P('dp')
- grad_input: bfloat16 [8, 2048, 768], P('dp')
- new_qkv: float32 [3, 768, 768], P(None, 'dp', 'mp')
- new_qkv_first: float32 [3, 768, 768], P(None, 'dp', 'mp')
- new_qkv_second: float32 [3, 768, 768], P(None, 'dp', 'mp')
- new_out: float32 [768, 768], P('mp', 'dp')
- new_out_first: float32 [768, 768], P('mp', 'dp')
- new_out_second: float32 [768, 768], P('mp', 'dp')
- new_up: float32 [768, 3072], P('dp', 'mp')
- new_up_first: float32 [768, 3072], P('dp', 'mp')
- new_up_second: float32 [768, 3072], P('dp', 'mp')
- new_down: float32 [3072, 768], P('mp', 'dp')
- new_down_first: float32 [3072, 768], P('mp', 'dp')
- new_down_second: float32 [3072, 768], P('mp', 'dp')
- new_head: float32 [5, 12, 64], P(None, 'mp')
- new_head_first: float32 [5, 12, 64], P(None, 'mp')
- new_head_second: float32 [5, 12, 64], P(None, 'mp')
- new_upb: float32 [3072], P('mp')
- new_upb_first: float32 [3072], P('mp')
- new_upb_second: float32 [3072], P('mp')
- new_vec: float32 [6, 768], replicated
- new_vec_first: float32 [6, 768], replicated
- new_vec_second: float32 [6, 768], replicated
- grad_norm: float32 [1], replicated
- rms_stats: float32 [2], replicated
The draws below stay inside these ranges and needn't reach their ends.
Inputs may be any that keep to these rules, and one draw needn't show every extreme that they name: `keep_mask`: per sequence each patch is kept with a chance from one half to all; the chance rises with the sequence index. `segment_ids`: within a row ids never fall; each image covers 1 to 512 consecutive slots, one exactly that many. `head_params`: rows 0 to 2 are biases, rows 3 and 4 gains. `vec_params`: rows 0 and 2 are gains, the others biases.
All inputs are finite; a program needn't handle non-finite values.
Results may differ from the reference program's by a relative error of at most 0.012.
Values sent between devices are 32-bit elements; how exact they have to be, the bound alone decides.
No kernel may reach another device: no remote copies, remote signals or barrier semaphores. Data moves between devices by JAX's collectives and lax.ppermute only.
A program may use at most 256 MiB of HBM per device.

```python
import math
import jax
import jax.numpy as jnp
import numpy as np
from jax import lax

D = 768
H = 12
HD = 64
FF = 3072
SEQ = 2048
GROUPS = 8


def draw_keep_mask(key, part):
    groups = lax.broadcasted_iota(jnp.int32, (GROUPS, SEQ), 0)
    share = 50 + 50 * groups // max(GROUPS - 1, 1)
    rolls = jax.random.randint(key, (GROUPS, SEQ), 0, 100)
    return (rolls < share).astype(jnp.int32)


def draw_head_params(key, part):
    first_key, second_key = jax.random.split(key)
    rows = lax.broadcasted_iota(jnp.int32, (5, H, HD), 0)
    biases = jnp.clip(0.3 * jax.random.normal(first_key, (5, H, HD), jnp.float32), -2.0, 2.0)
    gains = jax.random.uniform(second_key, (5, H, HD), jnp.float32, 0.7, 1.3)
    return jnp.where(rows < 3, biases, gains)


def draw_vec_params(key, part):
    first_key, second_key = jax.random.split(key)
    rows = lax.broadcasted_iota(jnp.int32, (6, D), 0)
    biases = jnp.clip(0.3 * jax.random.normal(first_key, (6, D), jnp.float32), -2.0, 2.0)
    gains = jax.random.uniform(second_key, (6, D), jnp.float32, 0.7, 1.3)
    return jnp.where((rows == 0) | (rows == 2), gains, biases)


def block_scale(rng, dims, pieces, least, top_value):
    level, own = 1.0, jax.random.fold_in(rng, 6)
    for dim, blocks in pieces:
        steps = jnp.exp(jax.random.uniform(jax.random.fold_in(own, dim), (blocks,), jnp.float32, least / len(pieces), top_value / len(pieces)))
        level = level * jnp.repeat(steps, dims[dim] // blocks).reshape([-1 if axis == dim else 1 for axis in range(len(dims))])
    return level


def split_up(number_of, total, bound, lean):
    loads = [(1 << 20) // math.isqrt(grade ** lean) + 1 for grade in range(2, number_of + 1)]
    rest, holding = total - bound - (number_of - 1), [1] * (number_of - 1)
    while rest > 0:
        candidates = [i for i in range(number_of - 1) if holding[i] < bound]
        whole, left = sum([loads[i] for i in candidates]), rest
        for i in candidates:
            addition = min(bound - holding[i], max(1, left * loads[i] // whole), rest)
            holding[i] = holding[i] + addition
            rest = rest - addition
    return np.array([bound] + holding)


def uneven_parts(own_key, count, total, bound, lean):
    if count == 2:
        one = jax.random.randint(own_key, (), max(1, total - bound), min(bound, total - 1) + 1)
        return jnp.stack([one, total - one])
    tallies = jnp.asarray(split_up(count, total, bound, lean), jnp.int32)
    twos = (count - 1) // 2
    giver, receiver = tallies[1:1 + 2 * twos:2], tallies[2:2 + 2 * twos:2]
    room = jnp.minimum(giver - 1, bound - receiver)
    shifted = jax.random.randint(jax.random.fold_in(own_key, 1), (twos,), 0, 1 << 20) % (room + 1)
    tallies = tallies.at[1:1 + 2 * twos:2].set(giver - shifted).at[2:2 + 2 * twos:2].set(receiver + shifted)
    return tallies[jax.random.permutation(jax.random.fold_in(own_key, 2), count)]


def gaussian(own_key, shape, deviation, limit, cuts=(), held_as=jnp.bfloat16):
    drawn = deviation * jax.random.normal(own_key, shape, jnp.float32)
    if cuts:
        drawn = drawn * block_scale(own_key, shape, cuts, -0.22, 0.18)
    return jnp.clip(drawn, -limit, limit).astype(held_as)


def setup_inputs(seed: int = 0) -> dict:
    arg_keys = jax.random.split(jax.random.key(seed), 27)
    return {
        "patches": gaussian(arg_keys[0], (GROUPS, SEQ, D), 1.0, 6.0, ((0, 8),)),
        "cotangent": gaussian(arg_keys[1], (GROUPS, SEQ, D), 1.0, 6.0, ((0, 8),)),
        "keep_mask": draw_keep_mask(jax.random.fold_in(arg_keys[26], 71), 0),
        "segment_ids": jax.vmap(lambda own: jnp.searchsorted(jnp.cumsum(uneven_parts(own, 8, SEQ, SEQ // 4, 2)), jnp.arange(SEQ), side="right"))(jax.random.split(arg_keys[3], GROUPS)).reshape((GROUPS, SEQ)).astype(jnp.int32),
        "step_count": jax.random.randint(arg_keys[4], (1,), 2, 9).astype(jnp.int32),
        "qkv_weight": gaussian(arg_keys[5], (3, D, D), D ** -0.5, 0.21875, ((2, 4),), jnp.float32),
        "qkv_first": gaussian(arg_keys[6], (3, D, D), (0.11 * (12 * D * D) ** -0.5), 0.00061035156, ((1, 8), (2, 4)), jnp.float32),
        "qkv_second": jnp.clip(jnp.exp(math.log(2.9669868339965433e-08) - 1.3843914 * jax.random.uniform(arg_keys[7], (3, D, D), jnp.float32) ** block_scale(arg_keys[7], (3, D, D), ((1, 8), (2, 4)), -0.2, 0.2)), 7.431595339113528e-09, 2.9669868339965433e-08),
        "out_weight": gaussian(arg_keys[8], (D, D), (max(D // 64, 4)) ** -0.5, 1.75, ((0, 4),), jnp.float32),
        "out_first": gaussian(arg_keys[9], (D, D), (0.11 * (12 * D * D) ** -0.5), 0.00061035156, ((0, 4), (1, 8)), jnp.float32),
        "out_second": jnp.clip(jnp.exp(math.log(2.9669868339965433e-08) - 1.3843914 * jax.random.uniform(arg_keys[10], (D, D), jnp.float32) ** block_scale(arg_keys[10], (D, D), ((0, 4), (1, 8)), -0.2, 0.2)), 7.431595339113528e-09, 2.9669868339965433e-08),
        "up_weight": gaussian(arg_keys[11], (D, FF), D ** -0.5, 0.21875, ((1, 4),), jnp.float32),
        "up_first": gaussian(arg_keys[12], (D, FF), (0.11 * (12 * D * D) ** -0.5), 0.00061035156, ((0, 8), (1, 4)), jnp.float32),
        "up_second": jnp.clip(jnp.exp(math.log(2.9669868339965433e-08) - 1.3843914 * jax.random.uniform(arg_keys[13], (D, FF), jnp.float32) ** block_scale(arg_keys[13], (D, FF), ((0, 8), (1, 4)), -0.2, 0.2)), 7.431595339113528e-09, 2.9669868339965433e-08),
        "down_weight": gaussian(arg_keys[14], (FF, D), FF ** -0.5, 0.109375, ((0, 4),), jnp.float32),
        "down_first": gaussian(arg_keys[15], (FF, D), (0.11 * (12 * D * D) ** -0.5), 0.00061035156, ((0, 4), (1, 8)), jnp.float32),
        "down_second": jnp.clip(jnp.exp(math.log(2.9669868339965433e-08) - 1.3843914 * jax.random.uniform(arg_keys[16], (FF, D), jnp.float32) ** block_scale(arg_keys[16], (FF, D), ((0, 4), (1, 8)), -0.2, 0.2)), 7.431595339113528e-09, 2.9669868339965433e-08),
        "head_params": draw_head_params(jax.random.fold_in(arg_keys[26], 71), 0),
        "head_first": gaussian(arg_keys[18], (5, H, HD), (0.11 * (12 * D * D) ** -0.5), 0.00061035156, ((1, 4),), jnp.float32),
        "head_second": jnp.clip(jnp.exp(math.log(2.9669868339965433e-08) - 1.3843914 * jax.random.uniform(arg_keys[19], (5, H, HD), jnp.float32) ** block_scale(arg_keys[19], (5, H, HD), ((1, 4),), -0.2, 0.2)), 7.431595339113528e-09, 2.9669868339965433e-08),
        "up_bias": gaussian(arg_keys[20], (FF,), 0.3, 2.0, ((0, 4),), jnp.float32),
        "upb_first": gaussian(arg_keys[21], (FF,), (0.11 * (12 * D * D) ** -0.5), 0.00061035156, ((0, 4),), jnp.float32),
        "upb_second": jnp.clip(jnp.exp(math.log(2.9669868339965433e-08) - 1.3843914 * jax.random.uniform(arg_keys[22], (FF,), jnp.float32) ** block_scale(arg_keys[22], (FF,), ((0, 4),), -0.2, 0.2)), 7.431595339113528e-09, 2.9669868339965433e-08),
        "vec_params": draw_vec_params(jax.random.fold_in(arg_keys[26], 71), 0),
        "vec_first": gaussian(arg_keys[24], (6, D), (0.11 * (12 * D * D) ** -0.5), 0.00061035156, (), jnp.float32),
        "vec_second": jnp.clip(jnp.exp(jax.random.uniform(arg_keys[25], (6, D), jnp.float32, math.log(7.431595339113528e-09), math.log(2.9669868339965433e-08))), 7.431595339113528e-09, 2.9669868339965433e-08),
    }


@jax.custom_vjp
def low(v):
    return lax.optimization_barrier(v.astype(jnp.bfloat16)).astype(jnp.float32)

@jax.custom_vjp
def low_back(v):
    return v

def low_keep(v):
    return (low(v), None)

def low_pass(kept, grad):
    return (grad,)

def back_keep(v):
    return (v, None)

def back_low(kept, grad):
    return (low(grad),)
low.defvjp(low_keep, low_pass)
low_back.defvjp(back_keep, back_low)
PRECISE = lax.Precision.HIGHEST
NORM_EPS = 1e-06
CLIP_LIMIT = 1.0
LEARN_RATE = 0.1
BETA_ONE = 0.9
BETA_TWO = 0.95
ADAM_EPS = 1e-08
WEIGHT_DECAY = 0.1

def standardize(values):
    center = values - lax.optimization_barrier(jnp.mean(values, axis=-1, keepdims=True))
    spread = lax.optimization_barrier(jnp.mean(center * center, axis=-1, keepdims=True))
    return center * lax.rsqrt(spread + NORM_EPS)

def sequence(params, inputs, seg_row, keep_row):
    qkv_w, out_w, up_w, down_w, head_p, up_b, vec_p = params
    a_first = low(standardize(inputs) * vec_p[0] + vec_p[1])
    raw = jnp.einsum('sd,kde->kse', a_first, low(qkv_w), precision=PRECISE) + head_p[0:3].reshape(3, 1, D)
    raw = low_back(raw)
    query = raw[0].reshape(SEQ, H, HD)
    key_raw = raw[1].reshape(SEQ, H, HD)
    value = raw[2].reshape(SEQ, H, HD)
    q_in = low(standardize(query) * head_p[3] * HD ** (-0.5))
    k_in = low(standardize(key_raw) * head_p[4])
    v_in = low(value)
    scores = low_back(jnp.einsum('qhd,khd->hqk', q_in, k_in, precision=PRECISE))
    places = jnp.arange(SEQ)
    allowed = (seg_row[:, None] == seg_row[None, :]) & ((keep_row[None, :] == 1) | (places[:, None] == places[None, :]))
    scores = jnp.where(allowed[None], scores, -1e+30)
    probs = low(jax.nn.softmax(scores, axis=-1))
    mixed = jnp.einsum('hqk,khd->qhd', probs, v_in, precision=PRECISE).reshape(SEQ, D)
    mixed = low(low_back(mixed))
    attn = low_back(jnp.dot(mixed, low(out_w), precision=PRECISE) + vec_p[4])
    hidden = inputs + attn
    a_second = low(standardize(hidden) * vec_p[2] + vec_p[3])
    upper = low_back(jnp.dot(a_second, low(up_w), precision=PRECISE) + up_b)
    gated = low(jax.nn.gelu(upper, approximate=False))
    mlp = low_back(jnp.dot(gated, low(down_w), precision=PRECISE) + vec_p[5])
    result = hidden + mlp
    keep_f = keep_row.astype(jnp.float32)
    stats = jnp.stack([jnp.sum(keep_f), jnp.sum(keep_f[:, None] * attn * attn), jnp.sum(keep_f[:, None] * mlp * mlp)])
    return (result, stats)

def adam_step(weight, grad, first, second, factor, corr_one, corr_two, decay):
    grad = factor * grad
    first = BETA_ONE * first + (1.0 - BETA_ONE) * grad
    second = BETA_TWO * second + (1.0 - BETA_TWO) * grad * grad
    update = first / corr_one / (jnp.sqrt(second / corr_two) + ADAM_EPS)
    return (weight - LEARN_RATE * (update + decay * weight), first, second)

def reference(patches, cotangent, keep_mask, segment_ids, step_count, qkv_weight, qkv_first, qkv_second, out_weight, out_first, out_second, up_weight, up_first, up_second, down_weight, down_first, down_second, head_params, head_first, head_second, up_bias, upb_first, upb_second, vec_params, vec_first, vec_second):
    params = (qkv_weight, out_weight, up_weight, down_weight, head_params, up_bias, vec_params)
    checked = jax.checkpoint(sequence)

    def whole(params, inputs):
        return lax.map(lambda item: checked(params, item[0], item[1], item[2]), (inputs, segment_ids, keep_mask))
    inputs = patches.astype(jnp.float32)
    outputs, pullback, stats = jax.vjp(whole, params, inputs, has_aux=True)
    incoming = cotangent.astype(jnp.float32) * keep_mask.astype(jnp.float32)[:, :, None]
    grads, grad_in = pullback(incoming)
    count = jnp.sum(stats[:, 0])
    scale = GROUPS * SEQ / count
    raw_sq = sum((jnp.sum(g * g) for g in grads))
    grad_norm = scale * jnp.sqrt(raw_sq)
    factor = jnp.minimum(1.0, CLIP_LIMIT / (grad_norm + 1e-06)) * scale
    steps_f = step_count[0].astype(jnp.float32)
    corr_one = 1.0 - BETA_ONE ** steps_f
    corr_two = 1.0 - BETA_TWO ** steps_f
    firsts = (qkv_first, out_first, up_first, down_first, head_first, upb_first, vec_first)
    seconds = (qkv_second, out_second, up_second, down_second, head_second, upb_second, vec_second)
    decays = (WEIGHT_DECAY, WEIGHT_DECAY, WEIGHT_DECAY, WEIGHT_DECAY, 0.0, 0.0, 0.0)
    updated = [adam_step(params[i], grads[i], firsts[i], seconds[i], factor, corr_one, corr_two, decays[i]) for i in range(7)]
    rms = jnp.sqrt(jnp.stack([jnp.sum(stats[:, 1]), jnp.sum(stats[:, 2])]) / (count * D))
    return (outputs.astype(jnp.bfloat16), (grad_in * scale).astype(jnp.bfloat16), updated[0][0], updated[0][1], updated[0][2], updated[1][0], updated[1][1], updated[1][2], updated[2][0], updated[2][1], updated[2][2], updated[3][0], updated[3][1], updated[3][2], updated[4][0], updated[4][1], updated[4][2], updated[5][0], updated[5][1], updated[5][2], updated[6][0], updated[6][1], updated[6][2], grad_norm.reshape(1), rms)
```

```python
import functools

import jax
import jax.numpy as jnp
from jax import lax
from jax.experimental import pallas as pl
from jax.experimental.pallas import tpu as pltpu
from jax.sharding import PartitionSpec as P

NORM_EPS = 1e-06
CLIP_LIMIT = 1.0
LEARN_RATE = 0.1
BETA_ONE = 0.9
BETA_TWO = 0.95
ADAM_EPS = 1e-08
WEIGHT_DECAY = 0.1
SEG_BOUND = 512
BLOCK = 256
LANES = 128
F32 = jnp.float32
BF16 = jnp.bfloat16


def adam_step(weight, grad, first, second, factor, corr_one, corr_two, decay):
    grad = factor * grad
    first = BETA_ONE * first + (1.0 - BETA_ONE) * grad
    second = BETA_TWO * second + (1.0 - BETA_TWO) * grad * grad
    update = first / corr_one / (jnp.sqrt(second / corr_two) + ADAM_EPS)
    return (weight - LEARN_RATE * (update + decay * weight), first, second)


def dot(left, right, left_dim, right_dim):
    return lax.dot_general(
        left, right, (((left_dim,), (right_dim,)), ((), ())), preferred_element_type=F32
    )


class Links:
    def __init__(self):
        self.dp_size = lax.axis_size("dp")
        self.mp_size = lax.axis_size("mp")
        self.bits = self.dp_size.bit_length() - 1
        self.dp = lax.axis_index("dp")
        self.mp = lax.axis_index("mp")

    def core(self, array):
        return lax.ppermute(array, "mp", [(i, i ^ 1) for i in range(self.mp_size)])

    def half(self, array):
        return lax.ppermute(array, "mp", [(i, i ^ 2) for i in range(self.mp_size)])

    def data(self, array, bit):
        return lax.ppermute(array, "dp", [(i, i ^ (1 << bit)) for i in range(self.dp_size)])

    def bit(self, bit):
        return (self.dp >> bit) & 1

    def sum_all(self, array):
        array = array + self.core(array)
        array = array + self.half(array)
        return self.sum_data(array)

    def sum_data(self, array):
        for bit in range(self.bits):
            array = array + self.data(array, bit)
        return array


def hold(value, *after):
    return lax.optimization_barrier((value, *after))[0]


def quarter_of(links, weight, axis):
    rows = weight.shape[axis] // 4
    return lax.dynamic_slice_in_dim(weight, (links.dp & 3) * rows, rows, axis)


def quarter_spots(links):
    return jnp.stack([(links.dp & 3) ^ change for change in range(4)])


class Reduction:
    def __init__(self, links, grad):
        self.links = links
        self.left = list(range(links.bits - 1, -1, -1))
        self.array = grad.reshape((2,) * links.bits + (grad.shape[0] >> links.bits, grad.shape[1]))

    def send(self, step):
        if step == "half":
            own = self.array.shape[-1] // 2
            self.kept = self.array[..., :own]
            return self.array[..., own:]
        axis = self.left.index(step)
        self.left.remove(step)
        mine = self.links.bit(step)
        self.kept = lax.dynamic_index_in_dim(self.array, mine, axis, keepdims=False)
        return lax.dynamic_index_in_dim(self.array, 1 - mine, axis, keepdims=False)

    def take(self, arrived):
        self.array = self.kept + arrived

    def step(self, step, *after):
        sent = self.send(step)
        sent = hold(sent, *after) if after else sent
        self.take(self.links.half(sent) if step == "half" else self.links.data(sent, step))


def vmem_specs(count):
    return [pl.BlockSpec(memory_space=pltpu.VMEM)] * count


def smem_specs(count):
    return [pl.BlockSpec(memory_space=pltpu.SMEM)] * count


def cost(flops, bytes_accessed, transcendentals=0):
    return pl.CostEstimate(
        flops=int(flops), bytes_accessed=int(bytes_accessed), transcendentals=int(transcendentals)
    )


def normed(values, axis):
    scale = 1.0 / values.shape[axis]
    center = values - jnp.sum(values, axis=axis, keepdims=True) * scale
    spread = jnp.sum(center * center, axis=axis, keepdims=True) * scale
    factor = lax.rsqrt(spread + NORM_EPS)
    return center * factor, factor


def normed_back(grad_hat, hat, factor, axis):
    scale = 1.0 / hat.shape[axis]
    mean = jnp.sum(grad_hat, axis=axis, keepdims=True) * scale
    along = jnp.sum(grad_hat * hat, axis=axis, keepdims=True) * scale
    return factor * (grad_hat - mean - hat * along)


def fold_rows(values):
    return jnp.sum(values.reshape(values.shape[0] // 8, 8, values.shape[1]), axis=0)


def fold_lanes(values):
    total = values[:, :LANES]
    for start in range(LANES, values.shape[1], LANES):
        total = total + values[:, start : start + LANES]
    return total


def column(row, count):
    return jnp.transpose(jnp.broadcast_to(row, (count, row.shape[1])))


def plan_kernel(window, half_ref, seg_ref, keep_ref, plan_ref, qseg_ref, kcode_ref, kept_ref):
    seq_len = seg_ref.shape[1]
    seg = seg_ref[...]
    half = half_ref[0]
    places = lax.broadcasted_iota(jnp.int32, (1, seq_len), 1)
    starts = (seg != pltpu.roll(seg, 1, 1)) & (places > 0)
    ranking = jnp.where(starts, jnp.abs(places - seq_len // 2) * (4 * seq_len) + places, 1 << 30)
    parting = lax.rem(jnp.min(ranking), 4 * seq_len)
    start = pl.multiple_of(half * (seq_len - window), LANES)
    low_valid = jnp.where(half == 0, 0, parting - start)
    high_valid = jnp.where(half == 0, parting, window)
    seg_win = seg_ref[:, pl.ds(start, window)]
    keep_win = keep_ref[:, pl.ds(start, window)]
    spots = lax.broadcasted_iota(jnp.int32, (1, window), 1)
    valid = (spots >= low_valid) & (spots < high_valid)
    qseg_ref[...] = jnp.broadcast_to(seg_win, (8, window))
    kcode_ref[...] = column(jnp.where(keep_win == 1, seg_win, -1), LANES)
    kept_ref[...] = column(jnp.where(valid & (keep_win == 1), 1.0, 0.0), LANES)
    segs = jnp.broadcast_to(seg_win, (8, window))
    lanes = lax.broadcasted_iota(jnp.int32, (8, window), 1)
    block = lax.broadcasted_iota(jnp.int32, (8, window), 0) * BLOCK

    def total(values):
        return jnp.sum(values, axis=1, keepdims=True)

    first_seg = total(jnp.where(lanes == block, segs, 0))
    last_seg = total(jnp.where(lanes == block + (BLOCK - 1), segs, 0))
    low = total(jnp.where(segs < first_seg, 1, 0))
    high = total(jnp.where(segs <= last_seg, 1, 0))
    block_first = block[:, :1]
    low = jnp.maximum(low, low_valid)
    high = jnp.minimum(high, high_valid) + (BLOCK - 1)
    shift = BLOCK.bit_length() - 1
    low, high = low >> shift, high >> shift
    live = (block_first < high_valid) & (block_first + BLOCK > low_valid)
    high = jnp.where(live, high, low)
    lane = lax.broadcasted_iota(jnp.int32, (8, LANES), 1)
    plan = jnp.where(lane == 0, low, jnp.where(lane == 1, high, parting))
    plan_ref[...] = plan


def make_plan(links, seg_row, keep_row, window):
    half = jnp.full((1,), links.mp // 2, jnp.int32)
    return pl.pallas_call(
        functools.partial(plan_kernel, window),
        out_shape=(
            jax.ShapeDtypeStruct((8, LANES), jnp.int32),
            jax.ShapeDtypeStruct((8, window), jnp.int32),
            jax.ShapeDtypeStruct((window, LANES), jnp.int32),
            jax.ShapeDtypeStruct((window, LANES), F32),
        ),
        in_specs=smem_specs(1) + vmem_specs(2),
        out_specs=tuple(vmem_specs(4)),
        cost_estimate=cost(0, window * 1100),
        name="plan_window",
    )(half, seg_row, keep_row)


def allowed_block(kcode_ref, qseg_ref, key_start, query_start):
    codes = kcode_ref[pl.ds(key_start, BLOCK), :]
    codes = jnp.concatenate([codes] * (BLOCK // LANES), axis=1)
    segs = qseg_ref[0:1, pl.ds(query_start, BLOCK)]
    rows = lax.broadcasted_iota(jnp.int32, (BLOCK, BLOCK), 0)
    cols = lax.broadcasted_iota(jnp.int32, (BLOCK, BLOCK), 1)
    return (codes == segs) | (rows - cols == query_start - key_start)


def project_heads(heads, dim, weight, a_ref, params_ref, qkv_refs, hat_refs, factor_ref):
    tokens = a_ref.shape[0]
    group = heads * dim

    def block(tb, carry):
        ts = pl.multiple_of(tb * BLOCK, BLOCK)
        here = pl.ds(ts, BLOCK)
        rows = a_ref[here, :]
        for which in range(3):
            raw = dot(weight[which][...], rows, 1, 1) + params_ref[:, which : which + 1]
            if which == 2:
                qkv_refs[2][:, here] = raw.astype(BF16)
                continue
            hat, factor = normed(raw.reshape(heads, dim, BLOCK), 1)
            hat = hat.reshape(group, BLOCK)
            gained = hat * params_ref[:, 3 + which : 4 + which]
            if which == 0:
                gained = gained * dim ** (-0.5)
            qkv_refs[which][:, here] = gained.astype(BF16)
            hat_refs[which][:, here] = hat.astype(BF16)
            for head in range(heads):
                spot = (which * heads + head) * 8
                factor_ref[pl.ds(spot, 8), here] = jnp.broadcast_to(factor[head], (8, BLOCK))
        return carry

    lax.fori_loop(0, tokens // BLOCK, block, 0)


def attend(heads, dim, plan_ref, q_ref, k_ref, v_ref, kcode_ref, qseg_ref, o_ref, inv_ref, acc, tot):
    tokens = q_ref.shape[1]

    def query_block(qb, carry):
        qs = pl.multiple_of(qb * BLOCK, BLOCK)
        acc[...] = jnp.zeros_like(acc)
        tot[...] = jnp.zeros_like(tot)

        def key_block(kb, carry):
            ks = pl.multiple_of(kb * BLOCK, BLOCK)
            allowed = allowed_block(kcode_ref, qseg_ref, ks, qs)
            for head in range(heads):
                rows = pl.ds(head * dim, dim)
                scores = dot(k_ref[rows, pl.ds(ks, BLOCK)], q_ref[rows, pl.ds(qs, BLOCK)], 0, 0)
                expo = jnp.where(allowed, jnp.exp(scores), 0.0)
                tot[pl.ds(head * 8, 8), :] += fold_rows(expo)
                acc[rows, :] += dot(v_ref[rows, pl.ds(ks, BLOCK)], expo.astype(BF16), 1, 0)
            return carry

        lax.fori_loop(plan_ref[qb, 0], plan_ref[qb, 1], key_block, 0)
        for head in range(heads):
            rows = pl.ds(head * dim, dim)
            total = jnp.sum(tot[pl.ds(head * 8, 8), :], axis=0, keepdims=True)
            inverse = jnp.where(total > 0.0, 1.0 / total, 0.0)
            o_ref[rows, pl.ds(qs, BLOCK)] = (acc[rows, :] * inverse).astype(BF16)
            inv_ref[pl.ds(head * 8, 8), pl.ds(qs, BLOCK)] = jnp.broadcast_to(inverse, (8, BLOCK))
        return carry

    lax.fori_loop(0, tokens // BLOCK, query_block, 0)


def own_heads_kernel(
    heads, dim, x_ref, vec_ref, weight_ref, params_ref,
    a_ref, q_ref, k_ref, v_ref, qh_ref, kh_ref, factor_ref, weight,
):
    weight[...] = weight_ref[...].astype(BF16)
    tokens = x_ref.shape[0]

    def norm_block(tb, carry):
        here = pl.ds(pl.multiple_of(tb * BLOCK, BLOCK), BLOCK)
        hat, _ = normed(x_ref[here, :].astype(F32), 1)
        a_ref[here, :] = (hat * vec_ref[0:1, :] + vec_ref[1:2, :]).astype(BF16)
        return carry

    lax.fori_loop(0, tokens // BLOCK, norm_block, 0)
    project_heads(
        heads, dim, [weight.at[k] for k in range(3)], a_ref, params_ref, (q_ref, k_ref, v_ref),
        (qh_ref, kh_ref), factor_ref,
    )


def other_heads_kernel(
    heads, dim, spots_ref, a_ref, own_ref, p0, p1, p2, p3, params_ref,
    q_ref, k_ref, v_ref, qh_ref, kh_ref, factor_ref, qk_ref, value_ref,
):
    group = heads * dim
    places = [
        (qk_ref.at[pl.ds(0, group)], qk_ref.at[pl.ds(2 * group, group)]),
        (qk_ref.at[pl.ds(group, group)], qk_ref.at[pl.ds(3 * group, group)]),
        (value_ref.at[pl.ds(0, group)], value_ref.at[pl.ds(group, group)]),
    ]
    for which, (own_place, place) in enumerate(places):
        own_place[...] = own_ref[which].astype(BF16)
        for index, piece in enumerate((p0, p1, p2, p3)):
            count = piece.shape[1]
            spot = pl.multiple_of(spots_ref[index] * count, 16)
            place[pl.ds(spot, count), :] = piece[which].astype(BF16)
    project_heads(
        heads, dim, [place for _, place in places], a_ref, params_ref, (q_ref, k_ref, v_ref), (qh_ref, kh_ref), factor_ref
    )


def attention_kernel(
    heads, dim, plan_ref, q_ref, k_ref, v_ref, kcode_ref, qseg_ref, o_ref, inv_ref, acc, tot
):
    attend(heads, dim, plan_ref, q_ref, k_ref, v_ref, kcode_ref, qseg_ref, o_ref, inv_ref, acc, tot)


def out_kernel(o_own_ref, o_other_ref, own_ref, other_ref, part_ref, weight, o_cat):
    group = own_ref.shape[0]

    @pl.when(pl.program_id(0) == 0)
    def _():
        weight[pl.ds(0, group), :] = own_ref[...].astype(BF16)
        weight[pl.ds(group, group), :] = other_ref[...].astype(BF16)

    o_cat[pl.ds(0, group), :] = o_own_ref[...]
    o_cat[pl.ds(group, group), :] = o_other_ref[...]
    part_ref[...] = dot(o_cat[...], weight[...], 0, 0)


def head_shapes(group, heads, tokens):
    narrow = jax.ShapeDtypeStruct((group, tokens), BF16)
    return [*(narrow,) * 5, jax.ShapeDtypeStruct((heads * 16, tokens), F32)]


def o_shapes(group, heads, tokens):
    return [
        jax.ShapeDtypeStruct((group, tokens), BF16),
        jax.ShapeDtypeStruct((heads * 8, tokens), F32),
    ]


def own_heads(x_win, vec_params, weight, params, heads, dim):
    tokens, width = x_win.shape
    group = heads * dim
    return pl.pallas_call(
        functools.partial(own_heads_kernel, heads, dim),
        out_shape=[
            jax.ShapeDtypeStruct((tokens, width), BF16),
            *head_shapes(group, heads, tokens),
        ],
        in_specs=vmem_specs(4),
        out_specs=vmem_specs(7),
        scratch_shapes=[pltpu.VMEM((3, group, width), BF16)],
        cost_estimate=cost(tokens * width * group * 6, tokens * width * 8),
        name="heads_own",
    )(x_win, vec_params, weight, params)


def other_heads(spots, a_first, own_weight, pieces, params, heads, dim):
    tokens, width = a_first.shape
    group = heads * dim
    return pl.pallas_call(
        functools.partial(other_heads_kernel, heads, dim),
        out_shape=[
            *head_shapes(group, heads, tokens),
            jax.ShapeDtypeStruct((4 * group, width), BF16),
            jax.ShapeDtypeStruct((2 * group, width), BF16),
        ],
        in_specs=smem_specs(1) + vmem_specs(7),
        out_specs=vmem_specs(8),
        cost_estimate=cost(tokens * width * group * 6, tokens * width * 8),
        name="heads_other",
    )(spots, a_first, own_weight, *pieces, params)


def attention(plan, query, key, value, kcode, qseg, heads, dim):
    group, tokens = query.shape
    pairs = heads * tokens * 3 * BLOCK
    return pl.pallas_call(
        functools.partial(attention_kernel, heads, dim),
        out_shape=o_shapes(group, heads, tokens),
        in_specs=smem_specs(1) + vmem_specs(5),
        out_specs=vmem_specs(2),
        scratch_shapes=[pltpu.VMEM((group, BLOCK), F32), pltpu.VMEM((heads * 8, BLOCK), F32)],
        cost_estimate=cost(pairs * dim * 4, group * tokens * 8, pairs),
        name="attention",
    )(plan, query, key, value, kcode, qseg)


def out_project(o_own, o_other, out_own, out_other):
    group, tokens = o_own.shape
    width = out_own.shape[1]
    cols = pl.BlockSpec((group, BLOCK), lambda i: (0, i))
    return pl.pallas_call(
        out_kernel,
        grid=(tokens // BLOCK,),
        out_shape=jax.ShapeDtypeStruct((tokens, width), F32),
        in_specs=[cols, cols, whole_spec(out_own.shape), whole_spec(out_other.shape)],
        out_specs=rows_spec(width),
        scratch_shapes=[
            pltpu.VMEM((2 * group, width), BF16),
            pltpu.VMEM((2 * group, BLOCK), BF16),
        ],
        cost_estimate=cost(tokens * width * group * 4, tokens * width * 6),
        name="out_project",
    )(o_own, o_other, out_own, out_other)


def attention_back_kernel(
    heads, dim, plan_ref, q_ref, k_ref, v_ref, qh_ref, kh_ref, factor_ref, o_ref, inv_ref, do_ref,
    params_ref, kcode_ref, qseg_ref, *rest,
):
    draw_qk_ref, draw_v_ref = rest[-7:-5]
    out_sums_ref, dq_ref, dk_ref, dv_ref, sums_ref = rest[-5:]
    group, tokens = q_ref.shape
    for ref in (dq_ref, dk_ref, dv_ref, sums_ref):
        ref[...] = jnp.zeros_like(ref)

    def query_block(qb, carry):
        qs = pl.multiple_of(qb * BLOCK, BLOCK)
        here = pl.ds(qs, BLOCK)
        deltas = []
        inverses = []
        for head in range(heads):
            rows = pl.ds(head * dim, dim)
            products = do_ref[rows, here].astype(F32) * o_ref[rows, here].astype(F32)
            deltas.append(jnp.sum(products, axis=0, keepdims=True))
            inverses.append(inv_ref[pl.ds(head * 8, 1), here])

        def key_block(kb, carry):
            ks = pl.multiple_of(kb * BLOCK, BLOCK)
            there = pl.ds(ks, BLOCK)
            allowed = allowed_block(kcode_ref, qseg_ref, ks, qs)
            for head in range(heads):
                rows = pl.ds(head * dim, dim)
                query, key = q_ref[rows, here], k_ref[rows, there]
                grad_o = do_ref[rows, here]
                scores = dot(key, query, 0, 0)
                probs = jnp.where(allowed, jnp.exp(scores), 0.0) * inverses[head]
                grad_probs = dot(v_ref[rows, there], grad_o, 0, 0)
                grad_scores = (probs * (grad_probs - deltas[head])).astype(BF16)
                dv_ref[rows, there] += dot(grad_o, probs.astype(BF16), 1, 1)
                dk_ref[rows, there] += dot(query, grad_scores, 1, 1)
                dq_ref[rows, here] += dot(key, grad_scores, 1, 0)
            return carry

        lax.fori_loop(plan_ref[qb, 0], plan_ref[qb, 1], key_block, 0)
        return carry

    lax.fori_loop(0, tokens // BLOCK, query_block, 0)

    def token_block(tb, carry):
        here = pl.ds(pl.multiple_of(tb * BLOCK, BLOCK), BLOCK)
        for which, (grad_ref, hat_ref) in enumerate(((dq_ref, qh_ref), (dk_ref, kh_ref), (dv_ref, None))):
            rows = pl.ds(which * group, group)
            grad = grad_ref[:, here]
            if hat_ref is not None:
                if which == 0:
                    grad = grad * dim ** (-0.5)
                hat = hat_ref[:, here].astype(F32)
                sums_ref[pl.ds((3 + which) * group, group), :] += fold_lanes(grad * hat)
                grad = grad * params_ref[:, 3 + which : 4 + which]
                parts = []
                for head in range(heads):
                    lines = slice(head * dim, (head + 1) * dim)
                    factor = factor_ref[pl.ds((which * heads + head) * 8, 1), here]
                    parts.append(normed_back(grad[lines], hat[lines], factor, 0))
                grad = jnp.concatenate(parts, axis=0)
            rounded = grad.astype(BF16)
            if which < 2:
                draw_qk_ref[rows, here] = rounded
            else:
                draw_v_ref[:, here] = rounded
            sums_ref[rows, :] += fold_lanes(rounded.astype(F32))
        return carry

    lax.fori_loop(0, tokens // BLOCK, token_block, 0)
    out_sums_ref[...] = jnp.sum(jnp.transpose(sums_ref[...]), axis=0, keepdims=True)


def attention_back(plan, saved, grad_o, params, kcode, qseg, heads, dim, draws=None):
    group, tokens = saved[0].shape
    pairs = heads * tokens * 3 * BLOCK
    which = 0 if draws is None else 1
    sums = -(-5 * group // LANES) * LANES
    inputs = [*saved, grad_o, params, kcode, qseg]
    in_specs = smem_specs(1) + [whole_spec(x.shape) for x in inputs]
    aliases = {}
    if draws is not None:
        aliases = {1 + len(inputs) + k: k for k in range(2)}
        inputs += draws
        in_specs += [pl.BlockSpec(memory_space=pl.ANY)] * 2
    return pl.pallas_call(
        functools.partial(attention_back_kernel, heads, dim),
        grid=(1,),
        out_shape=[
            jax.ShapeDtypeStruct((4 * group, tokens), BF16),
            jax.ShapeDtypeStruct((2 * group, tokens), BF16),
            jax.ShapeDtypeStruct((1, sums), F32),
        ],
        in_specs=in_specs,
        out_specs=[
            pl.BlockSpec((2 * group, tokens), lambda i: (which, 0)),
            pl.BlockSpec((group, tokens), lambda i: (which, 0)),
            whole_spec((1, sums)),
        ],
        scratch_shapes=[
            *(pltpu.VMEM((group, tokens), F32),) * 3,
            pltpu.VMEM((sums, LANES), F32),
        ],
        input_output_aliases=aliases,
        cost_estimate=cost(pairs * dim * 10, group * tokens * 30, pairs),
        name="attention_back",
    )(plan, *inputs)


ERFC_TERMS = (
    0.16918800576031592, 0.17071521752915575, 0.14833923939584578, 0.2149257797248009,
    -0.09465005158893602, 0.5477190245253036, -0.5122771874066157, 0.4855627631921905,
    -0.1295228107166713,
)


def gelu_and_slope(values):
    t = 1.0 / (1.0 + (0.3 * 0.5**0.5) * jnp.abs(values))
    poly = ERFC_TERMS[-1]
    for term in ERFC_TERMS[-2::-1]:
        poly = poly * t + term
    bell = jnp.exp(values * values * -0.5)
    low_tail = 0.5 * (t * poly) * bell
    below = jnp.where(values > 0.0, 1.0 - low_tail, low_tail)
    return values * below, below + values * bell * 0.3989422804014327


def mlp_half(a, dmlp, up, down, bias):
    upper = dot(a, up, 1, 0) + bias
    gated, slope = gelu_and_slope(upper)
    gated = gated.astype(BF16)
    grad_gated = dot(dmlp, down, 1, 1)
    grad_upper = (grad_gated * slope).astype(BF16)
    return gated, grad_upper, dot(gated, down, 1, 0), dot(grad_upper, up, 1, 1)


def own_mlp_kernel(
    x_ref, mine_ref, peer_ref, cot_ref, kept_ref, vec_ref, up_ref, down_ref, bias_ref,
    hidden_ref, a_ref, dmlp_ref, g_ref, du_ref, mlp_ref, da_ref, bias_out, attn_out, up, down, bias_sums, attn_sums,
):
    @pl.when(pl.program_id(0) == 0)
    def _():
        up[...] = up_ref[...].astype(BF16)
        down[...] = down_ref[...].astype(BF16)
        bias_sums[...] = jnp.zeros_like(bias_sums)
        attn_sums[...] = jnp.zeros_like(attn_sums)

    kept = kept_ref[:, 0:1]
    attn = mine_ref[...] + peer_ref[...] + vec_ref[4:5, :]
    attn_sums[...] += fold_rows(kept * attn * attn)
    hidden = x_ref[...].astype(F32) + attn
    hidden_ref[...] = hidden
    hat, _ = normed(hidden, 1)
    a = (hat * vec_ref[2:3, :] + vec_ref[3:4, :]).astype(BF16)
    a_ref[...] = a
    dmlp = (cot_ref[...].astype(F32) * kept).astype(BF16)
    dmlp_ref[...] = dmlp
    gated, grad_upper, mlp, da = mlp_half(a, dmlp, up[...], down[...], bias_ref[...])
    g_ref[...] = gated
    du_ref[...] = grad_upper
    mlp_ref[...] = mlp
    da_ref[...] = da
    bias_sums[...] += fold_rows(grad_upper.astype(F32))

    @pl.when(pl.program_id(0) == pl.num_programs(0) - 1)
    def _():
        bias_out[...] = jnp.sum(bias_sums[...], axis=0, keepdims=True)
        attn_out[...] = jnp.sum(attn_sums[...], axis=0, keepdims=True)


def other_mlp_kernel(
    spots_ref, a_ref, dmlp_ref, mlp_in_ref, da_in_ref, base, near_a, near_b, far_a, far_b, bias_ref, g_in, du_in,
    g_ref, du_ref, mlp_ref, da_ref, bias_out, up, down, bias_sums,
):
    @pl.when(pl.program_id(0) == 0)
    def _():
        count = near_a.shape[1]
        for change, first, second in (
            (0, base.at[:, pl.ds(0, count)], base.at[:, pl.ds(count, count)]),
            (1, near_a, far_b.at[0]),
            (2, far_a.at[0], near_b),
            (3, far_a.at[1], far_b.at[1]),
        ):
            for which, piece in enumerate((first, second)):
                spot = pl.multiple_of((spots_ref[change] * 2 + which) * count, 16)
                up[pl.ds(spot, count), :] = piece[0].astype(BF16)
                down[pl.ds(spot, count), :] = piece[1].astype(BF16)
        bias_sums[...] = jnp.zeros_like(bias_sums)

    gated, grad_upper, mlp, da = mlp_half(
        a_ref[...], dmlp_ref[...], up[...], down[...], bias_ref[...]
    )
    g_ref[...] = gated
    du_ref[...] = grad_upper
    mlp_ref[...] = mlp_in_ref[...] + mlp
    da_ref[...] = da_in_ref[...] + da
    bias_sums[...] += fold_rows(grad_upper.astype(F32))

    @pl.when(pl.program_id(0) == pl.num_programs(0) - 1)
    def _():
        bias_out[...] = jnp.sum(bias_sums[...], axis=0, keepdims=True)


def rows_spec(width):
    return pl.BlockSpec((BLOCK, width), lambda i: (i, 0))


def whole_spec(shape):
    return pl.BlockSpec(shape, lambda *_: (0,) * len(shape), pipeline_mode=pl.Buffered(1))


def sums_spec(rows, width):
    return pl.BlockSpec((rows, width), lambda *_: (0, 0))


def own_mlp(x_win, mine, peer, cot, kept, vec_params, up_weight, down_weight, bias):
    tokens, width = x_win.shape
    units = up_weight.shape[1]
    wide = rows_spec(width)
    struct = jax.ShapeDtypeStruct
    return pl.pallas_call(
        own_mlp_kernel,
        grid=(tokens // BLOCK,),
        out_shape=[
            struct((tokens, width), F32),
            struct((tokens, width), BF16),
            struct((tokens, width), BF16),
            struct((tokens, 2 * units), BF16),
            struct((tokens, 2 * units), BF16),
            struct((tokens, width), F32),
            struct((tokens, width), F32),
            struct((1, units), F32),
            struct((1, width), F32),
        ],
        in_specs=[
            wide, wide, wide, wide, rows_spec(LANES), whole_spec(vec_params.shape),
            whole_spec(up_weight.shape), whole_spec(down_weight.shape), whole_spec(bias.shape),
        ],
        out_specs=[
            wide, wide, wide, rows_spec(units), rows_spec(units), wide, wide,
            sums_spec(1, units), sums_spec(1, width),
        ],
        scratch_shapes=[
            pltpu.VMEM(up_weight.shape, BF16),
            pltpu.VMEM(down_weight.shape, BF16),
            pltpu.VMEM((8, units), F32),
            pltpu.VMEM((8, width), F32),
        ],
        cost_estimate=cost(8 * tokens * width * units, tokens * width * 40, tokens * units * 2),
        name="mlp_own",
    )(x_win, mine, peer, cot, kept, vec_params, up_weight, down_weight, bias)


def other_mlp(spots, a_second, dmlp, mlp_part, da_part, pieces, bias, activations):
    tokens, width = a_second.shape
    units = bias.shape[1]
    wide = rows_spec(width)
    later = pl.BlockSpec((BLOCK, units), lambda i: (i, 1))
    struct = jax.ShapeDtypeStruct
    return pl.pallas_call(
        other_mlp_kernel,
        grid=(tokens // BLOCK,),
        out_shape=[
            struct((tokens, 2 * units), BF16),
            struct((tokens, 2 * units), BF16),
            struct((tokens, width), F32),
            struct((tokens, width), F32),
            struct((1, units), F32),
        ],
        in_specs=[
            *smem_specs(1), wide, wide, wide, wide,
            *(whole_spec(piece.shape) for piece in pieces), whole_spec(bias.shape),
            *(pl.BlockSpec(memory_space=pl.ANY),) * 2,
        ],
        out_specs=[later, later, wide, wide, sums_spec(1, units)],
        input_output_aliases={3: 2, 4: 3, 6 + len(pieces): 0, 7 + len(pieces): 1},
        scratch_shapes=[
            pltpu.VMEM((width, units), BF16),
            pltpu.VMEM((units, width), BF16),
            pltpu.VMEM((8, units), F32),
        ],
        cost_estimate=cost(8 * tokens * width * units, tokens * width * 28, tokens * units * 2),
        name="mlp_other",
    )(spots, a_second, dmlp, mlp_part, da_part, *pieces, bias, *activations)


def hidden_back_kernel(
    group, hidden_ref, mine_ref, peer_ref, cot_ref, kept_ref, vec_ref, out_own_ref, out_other_ref,
    dh_ref, dattn_ref, do_own_ref, do_other_ref, sums_out, out_weight, sums_ref,
):
    @pl.when(pl.program_id(0) == 0)
    def _():
        out_weight[pl.ds(0, group), :] = out_own_ref[...].astype(BF16)
        out_weight[pl.ds(group, group), :] = out_other_ref[...].astype(BF16)
        sums_ref[...] = jnp.zeros_like(sums_ref)

    hat, factor = normed(hidden_ref[...], 1)
    da = mine_ref[...] + peer_ref[...]
    dy = cot_ref[...].astype(F32) * kept_ref[:, 0:1]
    dh = dy + normed_back(da * vec_ref[2:3, :], hat, factor, 1)
    dh_ref[...] = dh
    dattn = dh.astype(BF16)
    dattn_ref[...] = dattn
    grads = dot(out_weight[...], dattn, 1, 1).astype(BF16)
    do_own_ref[...] = grads[:group]
    do_other_ref[...] = grads[group:]
    sums_ref[0:8, :] += fold_rows(da * hat)
    sums_ref[8:16, :] += fold_rows(da)
    sums_ref[16:24, :] += fold_rows(dattn.astype(F32))
    sums_ref[24:32, :] += fold_rows(dy.astype(BF16).astype(F32))

    @pl.when(pl.program_id(0) == pl.num_programs(0) - 1)
    def _():
        for row in range(4):
            total = jnp.sum(sums_ref[8 * row : 8 * row + 8, :], axis=0, keepdims=True)
            sums_out[row : row + 1, :] = total


def hidden_back(hidden, mine, peer, cot, kept, vec_params, out_own, out_other):
    tokens, width = hidden.shape
    group = out_own.shape[0]
    wide = rows_spec(width)
    cols = pl.BlockSpec((group, BLOCK), lambda i: (0, i))
    struct = jax.ShapeDtypeStruct
    return pl.pallas_call(
        functools.partial(hidden_back_kernel, group),
        grid=(tokens // BLOCK,),
        out_shape=[
            struct((tokens, width), F32),
            struct((tokens, width), BF16),
            struct((group, tokens), BF16),
            struct((group, tokens), BF16),
            struct((4, width), F32),
        ],
        in_specs=[
            wide, wide, wide, wide, rows_spec(LANES), whole_spec(vec_params.shape),
            whole_spec(out_own.shape), whole_spec(out_other.shape),
        ],
        out_specs=[wide, wide, cols, cols, sums_spec(4, width)],
        scratch_shapes=[pltpu.VMEM((2 * group, width), BF16), pltpu.VMEM((32, width), F32)],
        cost_estimate=cost(4 * tokens * width * group, tokens * width * 22),
        name="hidden_back",
    )(hidden, mine, peer, cot, kept, vec_params, out_own, out_other)


def input_back_kernel(
    core_ref, mine_ref, peer_ref, x_ref, dh_ref, vec_ref, out_ref, sums_out, sums_ref
):
    @pl.when(pl.program_id(0) == 0)
    def _():
        sums_ref[...] = jnp.zeros_like(sums_ref)

    hat, factor = normed(x_ref[...].astype(F32), 1)
    da = mine_ref[...] + peer_ref[...]
    out_ref[...] = dh_ref[...] + normed_back(da * vec_ref[0:1, :], hat, factor, 1)
    sums_ref[0:8, :] += fold_rows(da * hat)
    sums_ref[8:16, :] += fold_rows(da)

    @pl.when(pl.program_id(0) == pl.num_programs(0) - 1)
    def _():
        for row in range(2):
            total = jnp.sum(sums_ref[8 * row : 8 * row + 8, :], axis=0, keepdims=True)
            sums_out[row : row + 1, :] = total


def input_back(core, mine, peer, x_win, dh, vec_params):
    half_rows, width = peer.shape
    step = LANES
    count = half_rows // step
    near = pl.BlockSpec((step, width), lambda i, core_ref: (i, 0))
    window = pl.BlockSpec((step, width), lambda i, core_ref: (core_ref[0] * count + i, 0))
    struct = jax.ShapeDtypeStruct
    return pl.pallas_call(
        input_back_kernel,
        grid_spec=pltpu.PrefetchScalarGridSpec(
            num_scalar_prefetch=1,
            grid=(count,),
            in_specs=[window, near, window, window, whole_spec(vec_params.shape)],
            out_specs=[near, sums_spec(2, width)],
            scratch_shapes=[pltpu.VMEM((16, width), F32)],
        ),
        out_shape=[struct((half_rows, width), F32), struct((2, width), F32)],
        cost_estimate=cost(0, half_rows * width * 18),
        name="input_back",
    )(core, mine, peer, x_win, dh, vec_params)


def join_kernel(half_rows, window, info_ref, factor_ref, shift_ref, mine_ref, near_ref, far_ref, far_near_ref, out_ref):
    seq_len = out_ref.shape[1]
    core, half, parting = info_ref[0], info_ref[1], info_ref[2]
    factor = factor_ref[0]
    step = LANES

    def rows_of(which, row):
        from_core = row // half_rows
        spot = pl.ds(row % half_rows, step)
        own = half == which
        same = core == from_core
        return jnp.where(
            own,
            jnp.where(same, mine_ref[spot, :], near_ref[spot, :]),
            jnp.where(same, far_ref[spot, :], far_near_ref[spot, :]),
        )

    offset = seq_len - window
    for row in range(0, seq_len, step):
        if row + step <= offset:
            values = rows_of(0, row)
        elif row >= window:
            values = rows_of(1, row - offset)
        else:
            places = row + lax.broadcasted_iota(jnp.int32, (step, 1), 0)
            values = jnp.where(places < parting, rows_of(0, row), rows_of(1, row - offset))
        out_ref[0, pl.ds(row, step), :] = (values * factor + shift_ref[...]).astype(BF16)


def join_sequence(links, mine, near, far, far_near, parting, seq_len, window, factor, shift):
    half_rows, width = mine.shape
    info = jnp.stack([links.mp % 2, links.mp // 2, parting]).astype(jnp.int32)
    return pl.pallas_call(
        functools.partial(join_kernel, half_rows, window),
        out_shape=jax.ShapeDtypeStruct((1, seq_len, width), BF16),
        in_specs=smem_specs(2) + vmem_specs(5),
        out_specs=pl.BlockSpec(memory_space=pltpu.VMEM),
        cost_estimate=cost(0, half_rows * width * 16 + seq_len * width * 2),
        name="join_sequence",
    )(info, factor, shift, mine, near, far, far_near)


def last_gradients_kernel(
    group, a_ref, dattn_ref, qk_ref, v_ref, o_own_ref, o_other_ref, qk_own_out, qk_other_out, vo_out
):
    a, dattn = a_ref[...], dattn_ref[...]
    query_key = jnp.transpose(dot(qk_ref[...], a, 1, 0))
    qk_own_out[...] = query_key[:, : 2 * group]
    qk_other_out[...] = query_key[:, 2 * group :]
    value = dot(v_ref[...], a, 1, 0)
    own, other = dot(o_own_ref[...], dattn, 1, 0), dot(o_other_ref[...], dattn, 1, 0)
    rows = jnp.concatenate([value[:group], own, value[group:], other], axis=0)
    vo_out[...] = jnp.transpose(rows)


def last_gradients(a_first, dattn, draw_qk, draw_v, o_own, o_other):
    tokens, width = a_first.shape
    group = o_own.shape[0]
    cols = pl.BlockSpec((tokens, BLOCK), lambda i: (0, i))
    narrow, wide = rows_spec(2 * group), rows_spec(4 * group)
    struct = jax.ShapeDtypeStruct
    inputs = (draw_qk, draw_v, o_own, o_other)
    return pl.pallas_call(
        functools.partial(last_gradients_kernel, group),
        grid=(width // BLOCK,),
        out_shape=[
            struct((width, 2 * group), F32),
            struct((width, 2 * group), F32),
            struct((width, 4 * group), F32),
        ],
        in_specs=[cols, cols, *(whole_spec(x.shape) for x in inputs)],
        out_specs=[narrow, narrow, wide],
        cost_estimate=cost(16 * tokens * width * group, tokens * width * 12),
        name="last_gradients",
    )(a_first, dattn, *inputs)


def pack_kernel(
    core_ref, first_ref, second_ref, kept_ref, attn_ref, mlp_ref,
    own_ref, other_ref, own_bias_ref, other_bias_ref, mine_ref, away_ref,
):
    width = mine_ref.shape[1]
    once = jnp.where(core_ref[0] == 0, 1.0, 0.0)
    count = jnp.sum(kept_ref[...]) * (once / kept_ref.shape[1])
    attn = jnp.sum(attn_ref[...]) * once
    lane = lax.broadcasted_iota(jnp.int32, (1, width), 1)
    stats = jnp.where(lane == 0, count, jnp.where(lane == 1, attn, jnp.where(lane == 2, mlp_ref[0], 0.0)))
    sums, units = own_ref.shape[1], own_bias_ref.shape[1]
    for ref, head, bias in ((mine_ref, own_ref, own_bias_ref), (away_ref, other_ref, other_bias_ref)):
        ref[...] = jnp.zeros_like(ref)
        ref[0:2, :] = first_ref[...]
        ref[2:6, :] = second_ref[...] * once
        ref[6:7, :] = stats
        row = 8
        for source, size in ((head, sums), (bias, units)):
            for start in range(0, size, width):
                length = min(width, size - start)
                ref[row : row + 1, :length] = source[:, start : start + length]
                row += 1


def pack_small(core, first, second, kept, attn, mlp_sq, own, other, own_bias, other_bias):
    width = first.shape[1]
    inputs = (first, second, kept, attn)
    more = (own, other, own_bias, other_bias)
    rows = 8 + -(-own.shape[1] // width) + -(-own_bias.shape[1] // width)
    struct = jax.ShapeDtypeStruct((-(-rows // 8) * 8, width), F32)
    return pl.pallas_call(
        pack_kernel,
        out_shape=[struct, struct],
        in_specs=smem_specs(1) + vmem_specs(4) + smem_specs(1) + vmem_specs(4),
        out_specs=vmem_specs(2),
        cost_estimate=cost(0, kept.size * 4),
        name="pack_small",
    )(core, *inputs, mlp_sq, *more)


def update_kernel(decays, *refs):
    scalars, count = refs[0], len(decays)
    inputs, outputs = refs[1 : 1 + 4 * count], refs[1 + 4 * count :]
    factor, corr_one, corr_two = scalars[0], scalars[1], scalars[2]
    for index, decay in enumerate(decays):
        weight, grad, first, second = (ref[...] for ref in inputs[4 * index : 4 * index + 4])
        results = adam_step(weight, grad, first, second, factor, corr_one, corr_two, decay)
        for ref, value in zip(outputs[3 * index : 3 * index + 3], results):
            ref[...] = value


def update(scalars, groups, decays):
    inputs = [array for group in groups for array in group]
    shapes = [
        jax.ShapeDtypeStruct(group[0].shape, F32) for group in groups for _ in range(3)
    ]
    results = pl.pallas_call(
        functools.partial(update_kernel, decays),
        out_shape=shapes,
        in_specs=smem_specs(1) + vmem_specs(len(inputs)),
        out_specs=vmem_specs(len(shapes)),
        cost_estimate=cost(0, sum(28 * group[0].size for group in groups)),
        name="update",
    )(scalars, *inputs)
    return [results[3 * k : 3 * k + 3] for k in range(len(groups))]


def local(
    patches, cotangent, keep_mask, segment_ids, step_count,
    qkv_weight, qkv_first, qkv_second,
    out_weight, out_first, out_second,
    up_weight, up_first, up_second,
    down_weight, down_first, down_second,
    head_params, head_first, head_second,
    up_bias, upb_first, upb_second,
    vec_params, vec_first, vec_second,
):
    links = Links()
    seq_len, width = patches.shape[1:]
    heads, dim = head_params.shape[1:]
    group = heads * dim
    units = up_weight.shape[1]
    window = seq_len // 2 + SEG_BOUND // 2
    half_rows = window // 2
    core = links.mp % 2
    start = (links.mp // 2) * (seq_len - window)

    qkv_flip = jnp.swapaxes(qkv_weight, 1, 2)
    qkv_base = links.half(quarter_of(links, qkv_flip, 1))
    small = jnp.concatenate([head_params.reshape(-1), up_bias])
    small_other = links.half(small)
    head_other = small_other[: head_params.size].reshape(head_params.shape)

    def columns(params):
        return jnp.pad(params.reshape(params.shape[0], group).T, ((0, 0), (0, 3)))

    head_cols = columns(head_params)
    other_cols = columns(head_other)
    upb_own = up_bias.reshape(1, units)
    upb_other = small_other[head_params.size :].reshape(1, units)

    plan, qseg, kcode, kept = make_plan(links, segment_ids, keep_mask, window)
    parting = plan[0, 2]
    x_win = lax.dynamic_slice_in_dim(patches[0], start, window, 0)
    cot_win = lax.dynamic_slice_in_dim(cotangent[0], start, window, 0)
    a_first, *own = own_heads(x_win, vec_params, qkv_flip, head_cols, heads, dim)

    qkv_base = hold(qkv_base, own[0])
    qkv_pieces = [qkv_base, links.data(qkv_base, 0), links.data(qkv_base, 1)]
    both = [(i, i ^ 3) for i in range(links.dp_size)]
    qkv_pieces.append(lax.ppermute(qkv_base, "dp", both))
    spots = quarter_spots(links)
    up_down = quarter_of(links, jnp.stack([up_weight, down_weight]), 1)
    mlp_base = links.half(hold(up_down, qkv_base, small_other))
    own += attention(plan, hold(own[0], qkv_base), own[1], own[2], kcode, qseg, heads, dim)

    qkv_pieces = list(lax.optimization_barrier((*qkv_pieces, own[6]))[:4])
    *other, qk_cat, value_cat = other_heads(
        spots, a_first, qkv_flip, qkv_pieces, other_cols, heads, dim
    )
    mlp_base = hold(mlp_base, other[0])
    out_other = links.half(hold(out_weight, own[6]))
    eighth = mlp_base.shape[1] // 2
    part_a, part_b = mlp_base[:, :eighth], mlp_base[:, eighth:]
    near_a, near_b = links.data(part_a, 0), links.data(part_b, 1)
    other += attention(plan, hold(other[0], mlp_base), other[1], other[2], kcode, qseg, heads, dim)
    o_other, near_a, near_b = lax.optimization_barrier((other[6], near_a, near_b))
    attn_part = out_project(own[6], o_other, out_weight, out_other)
    pair_a, pair_b = jnp.stack([part_a, near_a]), jnp.stack([part_b, near_b])
    far_a, far_b = links.data(pair_a, 1), links.data(pair_b, 0)
    attn_peer = links.core(attn_part)
    hidden, a_second, dmlp, gated, grad_upper, mlp_part, da_part, upb_sums, attn_sums = own_mlp(
        x_win, attn_part, attn_peer, cot_win, kept, vec_params, up_weight, down_weight, upb_own
    )
    gated, grad_upper, mlp_part, da_part, upb_sums_other = other_mlp(
        spots, a_second, dmlp, mlp_part, da_part, (mlp_base, near_a, near_b, far_a, far_b), upb_other,
        (gated, grad_upper),
    )
    da_peer = links.core(da_part)
    down = Reduction(links, dot(dmlp, gated, 0, 0))
    up = Reduction(links, dot(a_second, grad_upper, 0, 0))
    down_sent, up_sent = down.send(0), up.send(1)
    down_got, up_got = links.data(down_sent, 0), links.data(up_sent, 1)
    dh, dattn, do_own, do_other, row_sums = hidden_back(
        hold(hidden, down_sent, up_sent), da_part, da_peer, cot_win, kept, vec_params,
        out_weight, out_other,
    )

    def my_rows(array):
        return lax.dynamic_slice_in_dim(array, core * half_rows, half_rows, 0)

    def peer_rows(array):
        return lax.dynamic_slice_in_dim(array, (1 - core) * half_rows, half_rows, 0)

    mlp_sum = my_rows(mlp_part) + links.core(peer_rows(mlp_part))
    result_mine = my_rows(hidden) + mlp_sum
    result_far, result_near = links.half(result_mine), links.core(result_mine)
    mlp_mine = mlp_sum + vec_params[5]
    mlp_sq = jnp.sum(my_rows(kept[:, :1]) * mlp_mine * mlp_mine)
    *draws, own_sums = attention_back(
        plan, own, hold(do_own, result_mine), head_cols, kcode, qseg, heads, dim
    )
    down.take(hold(down_got, draws[1]))
    up.take(hold(up_got, draws[1]))
    down_sent, up_sent = down.send("half"), up.send(0)
    down_got, up_got = links.half(down_sent), links.data(up_sent, 0)
    *draws, other_sums = attention_back(
        plan, other, hold(do_other, down_sent, up_sent, result_far, result_near), other_cols, kcode,
        qseg, heads, dim, draws,
    )
    result_far_near = links.core(result_far)
    down.take(hold(down_got, draws[1]))
    up.take(hold(up_got, draws[1]))
    down_sent, up_sent = down.send(1), up.send("half")
    down_got, up_got = links.data(down_sent, 1), links.half(up_sent)
    draws = lax.optimization_barrier((*draws, down_sent, up_sent, result_far_near))[:2]
    qk_own, qk_other, value_out = last_gradients(a_first, dattn, *draws, own[6], other[6])
    value_out = Reduction(links, value_out)
    value_out_sent = value_out.send(0)
    qk_got, value_out_got = links.half(qk_other), links.data(value_out_sent, 0)
    da1_part = dot(draws[0], qk_cat, 0, 0) + dot(draws[1], value_cat, 0, 0)
    da1_sent = peer_rows(da1_part)
    da1_peer = links.core(da1_sent)
    down.take(hold(down_got, da1_sent))
    up.take(hold(up_got, da1_sent))
    mlp = Reduction(links, jnp.zeros((width, 1), F32))
    mlp.left, mlp.array = list(down.left), jnp.concatenate([down.array, up.array], axis=-1)
    last_bits = list(mlp.left)
    mlp_sent = mlp.send(last_bits[0])
    mlp_got = links.data(mlp_sent, last_bits[0])
    grad_mine, first_sums = input_back(
        jnp.full((1,), core, jnp.int32), hold(da1_part, mlp_sent), da1_peer, x_win, dh, vec_params
    )
    grad_near = links.core(grad_mine)

    value_out.take(hold(value_out_got, grad_mine))
    value_out_sent = value_out.send(1)
    value_out_got = links.data(value_out_sent, 1)
    query_key = Reduction(links, qk_own + hold(qk_got, value_out_sent))
    query_key_sent = query_key.send(0)
    query_key_got = links.data(query_key_sent, 0)
    value_out.take(hold(value_out_got, query_key_sent, mlp_got))
    value_out_sent = value_out.send("half")
    value_out_got = links.half(value_out_sent)
    query_key.take(query_key_got)
    query_key_sent = query_key.send(1)
    query_key_got = links.data(query_key_sent, 1)
    value_out_got = hold(value_out_got, query_key_sent)
    value_out.take(value_out_got)
    grad_far = links.half(hold(grad_mine, value_out_got))
    query_key.take(query_key_got)
    last = Reduction(links, jnp.zeros((width, 1), F32))
    last.left = list(last_bits)
    last.array = jnp.concatenate([query_key.array, value_out.array], axis=-1)
    last_sent = last.send(last_bits[0])
    last_got = links.data(last_sent, last_bits[0])
    mlp.take(mlp_got)
    for bit in last_bits[1:]:
        mlp.step(bit)
    down_share, up_share = mlp.array[:, :units], mlp.array[:, units:]
    one = jnp.ones((1,), F32)
    result = join_sequence(
        links, hold(result_mine, grad_mine), result_near, result_far, result_far_near, parting, seq_len,
        window, one, vec_params[5:6],
    )
    last.take(hold(last_got, result))
    while last.left:
        last.step(last.left[0])
    last_share = last.array

    core_index = jnp.full((1,), core, jnp.int32)
    mine, away = pack_small(
        core_index, first_sums, row_sums, kept, attn_sums, mlp_sq.reshape(1), own_sums, other_sums,
        upb_sums, upb_sums_other,
    )
    summed = mine + links.half(away)
    shared = summed[:8]
    shared = shared + links.core(shared)
    summed = links.sum_data(jnp.concatenate([shared, summed[8:]], axis=0))
    vec_grad = summed[:6]
    stats = summed[6, :3]
    tail = summed[8:].reshape(-1)
    head_grad = tail[: head_params.size].reshape(head_params.shape)
    head_rows = -(-own_sums.shape[1] // width)
    bup_grad = tail[head_rows * width : head_rows * width + units]
    count = stats[0]
    scale = seq_len * links.dp_size / count
    rows = width // links.dp_size
    first_row = links.dp * rows
    shares = (
        jnp.stack([last_share[:, k * group : (k + 1) * group] for k in range(3)]),
        last_share[:, 3 * group :].T,
        up_share,
        down_share,
    )
    old_shares = (
        lax.dynamic_slice_in_dim(qkv_weight, first_row, rows, 1),
        lax.dynamic_slice_in_dim(out_weight, first_row, rows, 1),
        lax.dynamic_slice_in_dim(up_weight, first_row, rows, 0),
        lax.dynamic_slice_in_dim(down_weight, first_row, rows, 1).T,
    )
    first_dp = links.dp == 0
    first_mp = links.mp == 0
    big_sq = jnp.sum(last_share * last_share) + jnp.sum(mlp.array * mlp.array)
    split_sq = jnp.sum(head_grad * head_grad) + jnp.sum(bup_grad * bup_grad)
    whole_sq = jnp.sum(vec_grad * vec_grad)
    raw_sq = (
        big_sq + jnp.where(first_dp, split_sq, 0.0) + jnp.where(first_dp & first_mp, whole_sq, 0.0)
    )
    sq_total = links.sum_all(raw_sq)
    grad_norm = scale * jnp.sqrt(sq_total)
    factor = jnp.minimum(1.0, CLIP_LIMIT / (grad_norm + 1e-06)) * scale
    steps_f = step_count[0].astype(F32)
    corr_one = 1.0 - BETA_ONE**steps_f
    corr_two = 1.0 - BETA_TWO**steps_f
    grad_far = hold(grad_far, sq_total)
    grad_input = join_sequence(
        links, grad_mine, grad_near, grad_far, links.core(grad_far), parting, seq_len, window, scale.reshape(1), jnp.zeros((1, width), F32)
    )
    new_qkv, new_out, new_up, new_down, new_head, new_upb, new_vec = update(
        jnp.stack([factor, corr_one, corr_two]),
        [
            (old_shares[0], shares[0], qkv_first, qkv_second),
            (old_shares[1], shares[1], out_first, out_second),
            (old_shares[2], shares[2], up_first, up_second),
            (old_shares[3], shares[3], down_first.T, down_second.T),
            (head_params, head_grad, head_first, head_second),
            [x.reshape(1, units) for x in (up_bias, bup_grad, upb_first, upb_second)],
            (vec_params, vec_grad, vec_first, vec_second),
        ],
        (WEIGHT_DECAY,) * 4 + (0.0,) * 3,
    )
    new_down = [array.T for array in new_down]
    new_upb = [array.reshape(units) for array in new_upb]
    rms = jnp.sqrt(stats[1:] / (count * width))
    return (
        result, grad_input, *new_qkv, *new_out, *new_up, *new_down, *new_head, *new_upb, *new_vec,
        grad_norm.reshape(1), rms,
    )


def solution(mesh):
    seq = P("dp", None, None)
    row = P("dp", None)
    qkv = P(None, "dp", "mp")
    out = P("mp", "dp")
    up = P("dp", "mp")
    head = P(None, "mp", None)
    unit = P("mp")
    whole = P()
    return jax.shard_map(
        local,
        mesh=mesh,
        in_specs=(
            *(seq, seq, row, row, whole),
            *(P(None, None, "mp"), qkv, qkv),
            *(P("mp", None), out, out),
            *(P(None, "mp"), up, up),
            *(P("mp", None), out, out),
            *(head, head, head),
            *(unit, unit, unit),
            *(whole, whole, whole),
        ),
        out_specs=(
            *(seq, seq),
            *(qkv, qkv, qkv),
            *(out, out, out),
            *(up, up, up),
            *(out, out, out),
            *(head, head, head),
            *(unit, unit, unit),
            *(whole, whole, whole),
            *(whole, whole),
        ),
        check_vma=False,
    )
```

```python
import functools

import jax
import jax.numpy as jnp
from jax import lax
from jax.experimental import pallas as pl
from jax.experimental.pallas import tpu as pltpu
from jax.sharding import PartitionSpec as P

NORM_EPS = 1e-06
CLIP_LIMIT = 1.0
LEARN_RATE = 0.1
BETA_ONE = 0.9
BETA_TWO = 0.95
ADAM_EPS = 1e-08
WEIGHT_DECAY = 0.1
SEG_BOUND = 512
BLOCK = 256
LANES = 128
F32 = jnp.float32
BF16 = jnp.bfloat16


def adam_step(weight, grad, first, second, factor, corr_one, corr_two, decay):
    grad = factor * grad
    first = BETA_ONE * first + (1.0 - BETA_ONE) * grad
    second = BETA_TWO * second + (1.0 - BETA_TWO) * grad * grad
    update = first / corr_one / (jnp.sqrt(second / corr_two) + ADAM_EPS)
    return (weight - LEARN_RATE * (update + decay * weight), first, second)


def dot(left, right, left_dim, right_dim):
    return lax.dot_general(
        left, right, (((left_dim,), (right_dim,)), ((), ())), preferred_element_type=F32
    )


class Links:
    def __init__(self):
        self.dp_size = lax.axis_size("dp")
        self.mp_size = lax.axis_size("mp")
        self.bits = self.dp_size.bit_length() - 1
        self.dp = lax.axis_index("dp")
        self.mp = lax.axis_index("mp")

    def core(self, array):
        return lax.ppermute(array, "mp", [(i, i ^ 1) for i in range(self.mp_size)])

    def half(self, array):
        return lax.ppermute(array, "mp", [(i, i ^ 2) for i in range(self.mp_size)])

    def data(self, array, bit):
        return lax.ppermute(array, "dp", [(i, i ^ (1 << bit)) for i in range(self.dp_size)])

    def bit(self, bit):
        return (self.dp >> bit) & 1

    def sum_all(self, array):
        array = array + self.core(array)
        array = array + self.half(array)
        return self.sum_data(array)

    def sum_data(self, array):
        for bit in range(self.bits):
            array = array + self.data(array, bit)
        return array


def hold(value, *after):
    return lax.optimization_barrier((value, *after))[0]


def quarter_of(links, weight, axis):
    rows = weight.shape[axis] // 4
    return lax.dynamic_slice_in_dim(weight, (links.dp & 3) * rows, rows, axis)


def quarter_spots(links):
    return jnp.stack([(links.dp & 3) ^ change for change in range(4)])


class Reduction:
    def __init__(self, links, grad):
        self.links = links
        self.left = list(range(links.bits - 1, -1, -1))
        self.array = grad.reshape((2,) * links.bits + (grad.shape[0] >> links.bits, grad.shape[1]))

    def send(self, step):
        if step == "half":
            own = self.array.shape[-1] // 2
            self.kept = self.array[..., :own]
            return self.array[..., own:]
        axis = self.left.index(step)
        self.left.remove(step)
        mine = self.links.bit(step)
        self.kept = lax.dynamic_index_in_dim(self.array, mine, axis, keepdims=False)
        return lax.dynamic_index_in_dim(self.array, 1 - mine, axis, keepdims=False)

    def take(self, arrived):
        self.array = self.kept + arrived

    def step(self, step, *after):
        sent = self.send(step)
        sent = hold(sent, *after) if after else sent
        self.take(self.links.half(sent) if step == "half" else self.links.data(sent, step))


def vmem_specs(count):
    return [pl.BlockSpec(memory_space=pltpu.VMEM)] * count


def smem_specs(count):
    return [pl.BlockSpec(memory_space=pltpu.SMEM)] * count


def cost(flops, bytes_accessed, transcendentals=0):
    return pl.CostEstimate(
        flops=int(flops), bytes_accessed=int(bytes_accessed), transcendentals=int(transcendentals)
    )


def normed(values, axis):
    scale = 1.0 / values.shape[axis]
    center = values - jnp.sum(values, axis=axis, keepdims=True) * scale
    spread = jnp.sum(center * center, axis=axis, keepdims=True) * scale
    factor = lax.rsqrt(spread + NORM_EPS)
    return center * factor, factor


def normed_back(grad_hat, hat, factor, axis):
    scale = 1.0 / hat.shape[axis]
    mean = jnp.sum(grad_hat, axis=axis, keepdims=True) * scale
    along = jnp.sum(grad_hat * hat, axis=axis, keepdims=True) * scale
    return factor * (grad_hat - mean - hat * along)


def fold_rows(values):
    return jnp.sum(values.reshape(values.shape[0] // 8, 8, values.shape[1]), axis=0)


def fold_lanes(values):
    total = values[:, :LANES]
    for start in range(LANES, values.shape[1], LANES):
        total = total + values[:, start : start + LANES]
    return total


def column(row, count):
    return jnp.transpose(jnp.broadcast_to(row, (count, row.shape[1])))


def plan_kernel(window, half_ref, seg_ref, keep_ref, plan_ref, qseg_ref, kcode_ref, kept_ref):
    seq_len = seg_ref.shape[1]
    seg = seg_ref[...]
    half = half_ref[0]
    places = lax.broadcasted_iota(jnp.int32, (1, seq_len), 1)
    starts = (seg != pltpu.roll(seg, 1, 1)) & (places > 0)
    ranking = jnp.where(starts, jnp.abs(places - seq_len // 2) * (4 * seq_len) + places, 1 << 30)
    parting = lax.rem(jnp.min(ranking), 4 * seq_len)
    start = pl.multiple_of(half * (seq_len - window), LANES)
    low_valid = jnp.where(half == 0, 0, parting - start)
    high_valid = jnp.where(half == 0, parting, window)
    seg_win = seg_ref[:, pl.ds(start, window)]
    keep_win = keep_ref[:, pl.ds(start, window)]
    spots = lax.broadcasted_iota(jnp.int32, (1, window), 1)
    valid = (spots >= low_valid) & (spots < high_valid)
    qseg_ref[...] = jnp.broadcast_to(seg_win, (8, window))
    kcode_ref[...] = column(jnp.where(keep_win == 1, seg_win, -1), LANES)
    kept_ref[...] = column(jnp.where(valid & (keep_win == 1), 1.0, 0.0), LANES)
    segs = jnp.broadcast_to(seg_win, (8, window))
    lanes = lax.broadcasted_iota(jnp.int32, (8, window), 1)
    block = lax.broadcasted_iota(jnp.int32, (8, window), 0) * BLOCK

    def total(values):
        return jnp.sum(values, axis=1, keepdims=True)

    first_seg = total(jnp.where(lanes == block, segs, 0))
    last_seg = total(jnp.where(lanes == block + (BLOCK - 1), segs, 0))
    low = total(jnp.where(segs < first_seg, 1, 0))
    high = total(jnp.where(segs <= last_seg, 1, 0))
    block_first = block[:, :1]
    low = jnp.maximum(low, low_valid)
    high = jnp.minimum(high, high_valid) + (BLOCK - 1)
    shift = BLOCK.bit_length() - 1
    low, high = low >> shift, high >> shift
    live = (block_first < high_valid) & (block_first + BLOCK > low_valid)
    high = jnp.where(live, high, low)
    lane = lax.broadcasted_iota(jnp.int32, (8, LANES), 1)
    plan = jnp.where(lane == 0, low, jnp.where(lane == 1, high, parting))
    plan_ref[...] = plan


def make_plan(links, seg_row, keep_row, window):
    half = jnp.full((1,), links.mp // 2, jnp.int32)
    return pl.pallas_call(
        functools.partial(plan_kernel, window),
        out_shape=(
            jax.ShapeDtypeStruct((8, LANES), jnp.int32),
            jax.ShapeDtypeStruct((8, window), jnp.int32),
            jax.ShapeDtypeStruct((window, LANES), jnp.int32),
            jax.ShapeDtypeStruct((window, LANES), F32),
        ),
        in_specs=smem_specs(1) + vmem_specs(2),
        out_specs=tuple(vmem_specs(4)),
        compiler_params=pltpu.CompilerParams(vmem_limit_bytes=6 << 20),
        cost_estimate=cost(0, window * 1100),
        name="plan_window",
    )(half, seg_row, keep_row)


def allowed_block(kcode_ref, qseg_ref, key_start, query_start):
    codes = kcode_ref[pl.ds(key_start, BLOCK), :]
    codes = jnp.concatenate([codes] * (BLOCK // LANES), axis=1)
    segs = qseg_ref[0:1, pl.ds(query_start, BLOCK)]
    rows = lax.broadcasted_iota(jnp.int32, (BLOCK, BLOCK), 0)
    cols = lax.broadcasted_iota(jnp.int32, (BLOCK, BLOCK), 1)
    return (codes == segs) | (rows - cols == query_start - key_start)


def project_heads(heads, dim, weight, a_ref, params_ref, qkv_refs, hat_refs, factor_ref):
    tokens = a_ref.shape[0]
    group = heads * dim

    def block(tb, carry):
        ts = pl.multiple_of(tb * BLOCK, BLOCK)
        here = pl.ds(ts, BLOCK)
        rows = a_ref[here, :]
        for which in range(3):
            raw = dot(weight[which][...], rows, 1, 1) + params_ref[:, which : which + 1]
            if which == 2:
                qkv_refs[2][:, here] = raw.astype(BF16)
                continue
            hat, factor = normed(raw.reshape(heads, dim, BLOCK), 1)
            hat = hat.reshape(group, BLOCK)
            gained = hat * params_ref[:, 3 + which : 4 + which]
            if which == 0:
                gained = gained * dim ** (-0.5)
            qkv_refs[which][:, here] = gained.astype(BF16)
            hat_refs[which][:, here] = hat.astype(BF16)
            for head in range(heads):
                spot = (which * heads + head) * 8
                factor_ref[pl.ds(spot, 8), here] = jnp.broadcast_to(factor[head], (8, BLOCK))
        return carry

    lax.fori_loop(0, tokens // BLOCK, block, 0)


def attend(heads, dim, plan_ref, q_ref, k_ref, v_ref, kcode_ref, qseg_ref, o_ref, inv_ref, acc, tot):
    tokens = q_ref.shape[1]

    def query_block(qb, carry):
        qs = pl.multiple_of(qb * BLOCK, BLOCK)
        acc[...] = jnp.zeros_like(acc)
        tot[...] = jnp.zeros_like(tot)

        def key_block(kb, carry):
            ks = pl.multiple_of(kb * BLOCK, BLOCK)
            allowed = allowed_block(kcode_ref, qseg_ref, ks, qs)
            lines = [pl.ds(head * dim, dim) for head in range(heads)]
            scores = [dot(k_ref[rows, pl.ds(ks, BLOCK)], q_ref[rows, pl.ds(qs, BLOCK)], 0, 0) for rows in lines]
            expos = [jnp.where(allowed, jnp.exp(score), 0.0) for score in scores]
            more = [dot(v_ref[rows, pl.ds(ks, BLOCK)], expo.astype(BF16), 1, 0) for rows, expo in zip(lines, expos)]
            for head, rows in enumerate(lines):
                tot[pl.ds(head * 8, 8), :] += fold_rows(expos[head])
                acc[rows, :] += more[head]
            return carry

        lax.fori_loop(plan_ref[qb, 0], plan_ref[qb, 1], key_block, 0)
        for head in range(heads):
            rows = pl.ds(head * dim, dim)
            total = jnp.sum(tot[pl.ds(head * 8, 8), :], axis=0, keepdims=True)
            inverse = jnp.where(total > 0.0, 1.0 / total, 0.0)
            o_ref[rows, pl.ds(qs, BLOCK)] = (acc[rows, :] * inverse).astype(BF16)
            inv_ref[pl.ds(head * 8, 8), pl.ds(qs, BLOCK)] = jnp.broadcast_to(inverse, (8, BLOCK))
        return carry

    lax.fori_loop(0, tokens // BLOCK, query_block, 0)


def own_heads_kernel(
    heads, dim, x_ref, vec_ref, weight_ref, params_ref,
    a_ref, q_ref, k_ref, v_ref, qh_ref, kh_ref, factor_ref, weight,
):
    weight[...] = weight_ref[...].astype(BF16)
    tokens = x_ref.shape[0]

    def norm_block(tb, carry):
        here = pl.ds(pl.multiple_of(tb * BLOCK, BLOCK), BLOCK)
        hat, _ = normed(x_ref[here, :].astype(F32), 1)
        a_ref[here, :] = (hat * vec_ref[0:1, :] + vec_ref[1:2, :]).astype(BF16)
        return carry

    lax.fori_loop(0, tokens // BLOCK, norm_block, 0)
    project_heads(
        heads, dim, [weight.at[k] for k in range(3)], a_ref, params_ref, (q_ref, k_ref, v_ref),
        (qh_ref, kh_ref), factor_ref,
    )


def other_heads_kernel(
    heads, dim, spots_ref, a_ref, own_ref, p0, p1, p2, p3, params_ref,
    q_ref, k_ref, v_ref, qh_ref, kh_ref, factor_ref, qk_ref, value_ref,
):
    group = heads * dim
    places = [
        (qk_ref.at[pl.ds(0, group)], qk_ref.at[pl.ds(2 * group, group)]),
        (qk_ref.at[pl.ds(group, group)], qk_ref.at[pl.ds(3 * group, group)]),
        (value_ref.at[pl.ds(0, group)], value_ref.at[pl.ds(group, group)]),
    ]
    for which, (own_place, place) in enumerate(places):
        own_place[...] = own_ref[which].astype(BF16)
        for index, piece in enumerate((p0, p1, p2, p3)):
            count = piece.shape[1]
            spot = pl.multiple_of(spots_ref[index] * count, 16)
            place[pl.ds(spot, count), :] = piece[which].astype(BF16)
    project_heads(
        heads, dim, [place for _, place in places], a_ref, params_ref, (q_ref, k_ref, v_ref), (qh_ref, kh_ref), factor_ref
    )


def attention_kernel(
    heads, dim, plan_ref, q_ref, k_ref, v_ref, kcode_ref, qseg_ref, o_ref, inv_ref, acc, tot
):
    attend(heads, dim, plan_ref, q_ref, k_ref, v_ref, kcode_ref, qseg_ref, o_ref, inv_ref, acc, tot)


def out_kernel(o_own_ref, o_other_ref, own_ref, other_ref, part_ref, weight, o_cat):
    group = own_ref.shape[0]

    @pl.when(pl.program_id(0) == 0)
    def _():
        weight[pl.ds(0, group), :] = own_ref[...].astype(BF16)
        weight[pl.ds(group, group), :] = other_ref[...].astype(BF16)

    o_cat[pl.ds(0, group), :] = o_own_ref[...]
    o_cat[pl.ds(group, group), :] = o_other_ref[...]
    part_ref[...] = dot(o_cat[...], weight[...], 0, 0)


def head_shapes(group, heads, tokens):
    narrow = jax.ShapeDtypeStruct((group, tokens), BF16)
    return [*(narrow,) * 5, jax.ShapeDtypeStruct((heads * 16, tokens), F32)]


def o_shapes(group, heads, tokens):
    return [
        jax.ShapeDtypeStruct((group, tokens), BF16),
        jax.ShapeDtypeStruct((heads * 8, tokens), F32),
    ]


def own_heads(x_win, vec_params, weight, params, heads, dim):
    tokens, width = x_win.shape
    group = heads * dim
    return pl.pallas_call(
        functools.partial(own_heads_kernel, heads, dim),
        out_shape=[
            jax.ShapeDtypeStruct((tokens, width), BF16),
            *head_shapes(group, heads, tokens),
        ],
        in_specs=vmem_specs(4),
        out_specs=vmem_specs(7),
        scratch_shapes=[pltpu.VMEM((3, group, width), BF16)],
        cost_estimate=cost(tokens * width * group * 6, tokens * width * 8),
        name="heads_own",
    )(x_win, vec_params, weight, params)


def other_heads(spots, a_first, own_weight, pieces, params, heads, dim):
    tokens, width = a_first.shape
    group = heads * dim
    return pl.pallas_call(
        functools.partial(other_heads_kernel, heads, dim),
        out_shape=[
            *head_shapes(group, heads, tokens),
            jax.ShapeDtypeStruct((4 * group, width), BF16),
            jax.ShapeDtypeStruct((2 * group, width), BF16),
        ],
        in_specs=smem_specs(1) + vmem_specs(7),
        out_specs=vmem_specs(8),
        cost_estimate=cost(tokens * width * group * 6, tokens * width * 8),
        name="heads_other",
    )(spots, a_first, own_weight, *pieces, params)


def attention(plan, query, key, value, kcode, qseg, heads, dim):
    group, tokens = query.shape
    pairs = heads * tokens * 3 * BLOCK
    return pl.pallas_call(
        functools.partial(attention_kernel, heads, dim),
        out_shape=o_shapes(group, heads, tokens),
        in_specs=smem_specs(1) + vmem_specs(5),
        out_specs=vmem_specs(2),
        scratch_shapes=[pltpu.VMEM((group, BLOCK), F32), pltpu.VMEM((heads * 8, BLOCK), F32)],
        cost_estimate=cost(pairs * dim * 4, group * tokens * 8, pairs),
        name="attention",
    )(plan, query, key, value, kcode, qseg)


def out_project(o_own, o_other, out_own, out_other):
    group, tokens = o_own.shape
    width = out_own.shape[1]
    cols = pl.BlockSpec((group, BLOCK), lambda i: (0, i))
    return pl.pallas_call(
        out_kernel,
        grid=(tokens // BLOCK,),
        out_shape=jax.ShapeDtypeStruct((tokens, width), F32),
        in_specs=[cols, cols, whole_spec(out_own.shape), whole_spec(out_other.shape)],
        out_specs=rows_spec(width),
        scratch_shapes=[
            pltpu.VMEM((2 * group, width), BF16),
            pltpu.VMEM((2 * group, BLOCK), BF16),
        ],
        compiler_params=pltpu.CompilerParams(vmem_limit_bytes=12 << 20),
        cost_estimate=cost(tokens * width * group * 4, tokens * width * 6),
        name="out_project",
    )(o_own, o_other, out_own, out_other)


def attention_back_kernel(
    heads, dim, plan_ref, q_ref, k_ref, v_ref, qh_ref, kh_ref, factor_ref, o_ref, inv_ref, do_ref,
    params_ref, kcode_ref, qseg_ref, *rest,
):
    draw_qk_ref, draw_v_ref = rest[-7:-5]
    out_sums_ref, dq_ref, dk_ref, dv_ref, sums_ref = rest[-5:]
    group, tokens = q_ref.shape
    for ref in (dq_ref, dk_ref, dv_ref, sums_ref):
        ref[...] = jnp.zeros_like(ref)

    def query_block(qb, carry):
        qs = pl.multiple_of(qb * BLOCK, BLOCK)
        here = pl.ds(qs, BLOCK)
        deltas = []
        inverses = []
        for head in range(heads):
            rows = pl.ds(head * dim, dim)
            products = do_ref[rows, here].astype(F32) * o_ref[rows, here].astype(F32)
            deltas.append(jnp.sum(products, axis=0, keepdims=True))
            inverses.append(inv_ref[pl.ds(head * 8, 1), here])

        def key_block(kb, carry):
            ks = pl.multiple_of(kb * BLOCK, BLOCK)
            there = pl.ds(ks, BLOCK)
            allowed = allowed_block(kcode_ref, qseg_ref, ks, qs)
            lines = [pl.ds(head * dim, dim) for head in range(heads)]
            keys = [k_ref[rows, there] for rows in lines]
            queries = [q_ref[rows, here] for rows in lines]
            grads = [do_ref[rows, here] for rows in lines]
            scores = [dot(key, query, 0, 0) for key, query in zip(keys, queries)]
            grad_probs = [dot(v_ref[rows, there], grad, 0, 0) for rows, grad in zip(lines, grads)]
            added = []
            for head in range(heads):
                probs = jnp.where(allowed, jnp.exp(scores[head]), 0.0) * inverses[head]
                grad_scores = (probs * (grad_probs[head] - deltas[head])).astype(BF16)
                added.append((
                    dot(grads[head], probs.astype(BF16), 1, 1),
                    dot(queries[head], grad_scores, 1, 1),
                    dot(keys[head], grad_scores, 1, 0),
                ))
            for rows, (more_v, more_k, more_q) in zip(lines, added):
                dv_ref[rows, there] += more_v
                dk_ref[rows, there] += more_k
                dq_ref[rows, here] += more_q
            return carry

        lax.fori_loop(plan_ref[qb, 0], plan_ref[qb, 1], key_block, 0)
        return carry

    lax.fori_loop(0, tokens // BLOCK, query_block, 0)

    def token_block(tb, carry):
        here = pl.ds(pl.multiple_of(tb * BLOCK, BLOCK), BLOCK)
        for which, (grad_ref, hat_ref) in enumerate(((dq_ref, qh_ref), (dk_ref, kh_ref), (dv_ref, None))):
            rows = pl.ds(which * group, group)
            grad = grad_ref[:, here]
            if hat_ref is not None:
                if which == 0:
                    grad = grad * dim ** (-0.5)
                hat = hat_ref[:, here].astype(F32)
                sums_ref[pl.ds((3 + which) * group, group), :] += fold_lanes(grad * hat)
                grad = grad * params_ref[:, 3 + which : 4 + which]
                parts = []
                for head in range(heads):
                    lines = slice(head * dim, (head + 1) * dim)
                    factor = factor_ref[pl.ds((which * heads + head) * 8, 1), here]
                    parts.append(normed_back(grad[lines], hat[lines], factor, 0))
                grad = jnp.concatenate(parts, axis=0)
            rounded = grad.astype(BF16)
            if which < 2:
                draw_qk_ref[rows, here] = rounded
            else:
                draw_v_ref[:, here] = rounded
            sums_ref[rows, :] += fold_lanes(rounded.astype(F32))
        return carry

    lax.fori_loop(0, tokens // BLOCK, token_block, 0)
    out_sums_ref[...] = jnp.sum(jnp.transpose(sums_ref[...]), axis=0, keepdims=True)


def attention_back(plan, saved, grad_o, params, kcode, qseg, heads, dim, draws=None):
    group, tokens = saved[0].shape
    pairs = heads * tokens * 3 * BLOCK
    which = 0 if draws is None else 1
    sums = -(-5 * group // LANES) * LANES
    inputs = [*saved, grad_o, params, kcode, qseg]
    in_specs = smem_specs(1) + [whole_spec(x.shape) for x in inputs]
    aliases = {}
    if draws is not None:
        aliases = {1 + len(inputs) + k: k for k in range(2)}
        inputs += draws
        in_specs += [pl.BlockSpec(memory_space=pl.ANY)] * 2
    return pl.pallas_call(
        functools.partial(attention_back_kernel, heads, dim),
        grid=(1,),
        out_shape=[
            jax.ShapeDtypeStruct((4 * group, tokens), BF16),
            jax.ShapeDtypeStruct((2 * group, tokens), BF16),
            jax.ShapeDtypeStruct((1, sums), F32),
        ],
        in_specs=in_specs,
        out_specs=[
            pl.BlockSpec((2 * group, tokens), lambda i: (which, 0)),
            pl.BlockSpec((group, tokens), lambda i: (which, 0)),
            whole_spec((1, sums)),
        ],
        scratch_shapes=[
            *(pltpu.VMEM((group, tokens), F32),) * 3,
            pltpu.VMEM((sums, LANES), F32),
        ],
        input_output_aliases=aliases,
        compiler_params=pltpu.CompilerParams(vmem_limit_bytes=16 << 20),
        cost_estimate=cost(pairs * dim * 10, group * tokens * 30, pairs),
        name="attention_back",
    )(plan, *inputs)


ERFC_TERMS = (
    0.16918800576031592, 0.17071521752915575, 0.14833923939584578, 0.2149257797248009,
    -0.09465005158893602, 0.5477190245253036, -0.5122771874066157, 0.4855627631921905,
    -0.1295228107166713,
)


def gelu_and_slope(values):
    t = 1.0 / (1.0 + (0.3 * 0.5**0.5) * jnp.abs(values))
    poly = ERFC_TERMS[-1]
    for term in ERFC_TERMS[-2::-1]:
        poly = poly * t + term
    bell = jnp.exp(values * values * -0.5)
    low_tail = 0.5 * (t * poly) * bell
    below = jnp.where(values > 0.0, 1.0 - low_tail, low_tail)
    return values * below, below + values * bell * 0.3989422804014327


def mlp_half(a, dmlp, up, down, bias):
    upper = dot(a, up, 1, 0) + bias
    gated, slope = gelu_and_slope(upper)
    gated = gated.astype(BF16)
    grad_gated = dot(dmlp, down, 1, 1)
    grad_upper = (grad_gated * slope).astype(BF16)
    return gated, grad_upper, dot(gated, down, 1, 0), dot(grad_upper, up, 1, 1)


def own_mlp_kernel(
    x_ref, mine_ref, peer_ref, cot_ref, kept_ref, vec_ref, up_ref, down_ref, bias_ref,
    hidden_ref, a_ref, dmlp_ref, g_ref, du_ref, mlp_ref, da_ref, bias_out, attn_out, up, down, bias_sums, attn_sums,
):
    @pl.when(pl.program_id(0) == 0)
    def _():
        up[...] = up_ref[...].astype(BF16)
        down[...] = down_ref[...].astype(BF16)
        bias_sums[...] = jnp.zeros_like(bias_sums)
        attn_sums[...] = jnp.zeros_like(attn_sums)

    kept = kept_ref[:, 0:1]
    attn = mine_ref[...] + peer_ref[...] + vec_ref[4:5, :]
    attn_sums[...] += fold_rows(kept * attn * attn)
    hidden = x_ref[...].astype(F32) + attn
    hidden_ref[...] = hidden
    hat, _ = normed(hidden, 1)
    a = (hat * vec_ref[2:3, :] + vec_ref[3:4, :]).astype(BF16)
    a_ref[...] = a
    dmlp = (cot_ref[...].astype(F32) * kept).astype(BF16)
    dmlp_ref[...] = dmlp
    gated, grad_upper, mlp, da = mlp_half(a, dmlp, up[...], down[...], bias_ref[...])
    g_ref[...] = gated
    du_ref[...] = grad_upper
    mlp_ref[...] = mlp
    da_ref[...] = da
    bias_sums[...] += fold_rows(grad_upper.astype(F32))

    @pl.when(pl.program_id(0) == pl.num_programs(0) - 1)
    def _():
        bias_out[...] = jnp.sum(bias_sums[...], axis=0, keepdims=True)
        attn_out[...] = jnp.sum(attn_sums[...], axis=0, keepdims=True)


def other_mlp_kernel(
    spots_ref, a_ref, dmlp_ref, mlp_in_ref, da_in_ref, base, near_a, near_b, far_a, far_b, bias_ref,
    g_ref, du_ref, mlp_ref, da_left_ref, da_right_ref, bias_out, up, down, bias_sums,
):
    @pl.when(pl.program_id(0) == 0)
    def _():
        count = near_a.shape[1]
        for change, first, second in (
            (0, base.at[:, pl.ds(0, count)], base.at[:, pl.ds(count, count)]),
            (1, near_a, far_b.at[0]),
            (2, far_a.at[0], near_b),
            (3, far_a.at[1], far_b.at[1]),
        ):
            for which, piece in enumerate((first, second)):
                spot = pl.multiple_of((spots_ref[change] * 2 + which) * count, 16)
                up[pl.ds(spot, count), :] = piece[0].astype(BF16)
                down[pl.ds(spot, count), :] = piece[1].astype(BF16)
        bias_sums[...] = jnp.zeros_like(bias_sums)

    gated, grad_upper, mlp, da = mlp_half(
        a_ref[...], dmlp_ref[...], up[...], down[...], bias_ref[...]
    )
    g_ref[...] = gated
    du_ref[...] = grad_upper
    mlp_ref[...] = mlp_in_ref[...] + mlp
    da = da_in_ref[...] + da
    cut = da_left_ref.shape[1]
    da_left_ref[...], da_right_ref[...] = da[:, :cut], da[:, cut:]
    bias_sums[...] += fold_rows(grad_upper.astype(F32))

    @pl.when(pl.program_id(0) == pl.num_programs(0) - 1)
    def _():
        bias_out[...] = jnp.sum(bias_sums[...], axis=0, keepdims=True)


def rows_spec(width):
    return pl.BlockSpec((BLOCK, width), lambda i: (i, 0))


def whole_spec(shape):
    return pl.BlockSpec(shape, lambda *_: (0,) * len(shape), pipeline_mode=pl.Buffered(1))


def sums_spec(rows, width):
    return pl.BlockSpec((rows, width), lambda *_: (0, 0))


def own_mlp(x_win, mine, peer, cot, kept, vec_params, up_weight, down_weight, bias):
    tokens, width = x_win.shape
    units = up_weight.shape[1]
    wide = rows_spec(width)
    struct = jax.ShapeDtypeStruct
    return pl.pallas_call(
        own_mlp_kernel,
        grid=(tokens // BLOCK,),
        out_shape=[
            struct((tokens, width), F32),
            struct((tokens, width), BF16),
            struct((tokens, width), BF16),
            struct((tokens, units), BF16),
            struct((tokens, units), BF16),
            struct((tokens, width), F32),
            struct((tokens, width), F32),
            struct((1, units), F32),
            struct((1, width), F32),
        ],
        in_specs=[
            wide, wide, wide, wide, rows_spec(LANES), whole_spec(vec_params.shape),
            whole_spec(up_weight.shape), whole_spec(down_weight.shape), whole_spec(bias.shape),
        ],
        out_specs=[
            wide, wide, wide, rows_spec(units), rows_spec(units), wide, wide,
            sums_spec(1, units), sums_spec(1, width),
        ],
        scratch_shapes=[
            pltpu.VMEM(up_weight.shape, BF16),
            pltpu.VMEM(down_weight.shape, BF16),
            pltpu.VMEM((8, units), F32),
            pltpu.VMEM((8, width), F32),
        ],
        cost_estimate=cost(8 * tokens * width * units, tokens * width * 40, tokens * units * 2),
        name="mlp_own",
    )(x_win, mine, peer, cot, kept, vec_params, up_weight, down_weight, bias)


def other_mlp(spots, a_second, dmlp, mlp_part, da_part, pieces, bias):
    tokens, width = a_second.shape
    units = bias.shape[1]
    wide = rows_spec(width)
    struct = jax.ShapeDtypeStruct
    return pl.pallas_call(
        other_mlp_kernel,
        grid=(tokens // BLOCK,),
        out_shape=[
            struct((tokens, units), BF16),
            struct((tokens, units), BF16),
            struct((tokens, width), F32),
            struct((tokens, width // 2), F32),
            struct((tokens, width // 2), F32),
            struct((1, units), F32),
        ],
        in_specs=[
            *smem_specs(1), wide, wide, wide, wide,
            *(whole_spec(piece.shape) for piece in pieces), whole_spec(bias.shape),
        ],
        out_specs=[
            rows_spec(units), rows_spec(units), wide, *(rows_spec(width // 2),) * 2, sums_spec(1, units),
        ],
        input_output_aliases={3: 2},
        scratch_shapes=[
            pltpu.VMEM((width, units), BF16),
            pltpu.VMEM((units, width), BF16),
            pltpu.VMEM((8, units), F32),
        ],
        cost_estimate=cost(8 * tokens * width * units, tokens * width * 28, tokens * units * 2),
        name="mlp_other",
    )(spots, a_second, dmlp, mlp_part, da_part, *pieces, bias)


def hidden_back_kernel(
    group, hidden_ref, mine_left, mine_right, peer_left, peer_right, cot_ref, kept_ref, vec_ref, out_own_ref, out_other_ref,
    dh_ref, dattn_ref, do_own_ref, do_other_ref, sums_out, out_weight, sums_ref,
):
    @pl.when(pl.program_id(0) == 0)
    def _():
        out_weight[pl.ds(0, group), :] = out_own_ref[...].astype(BF16)
        out_weight[pl.ds(group, group), :] = out_other_ref[...].astype(BF16)
        sums_ref[...] = jnp.zeros_like(sums_ref)

    hat, factor = normed(hidden_ref[...], 1)
    da = jnp.concatenate(
        [mine_left[...] + peer_left[...], mine_right[...] + peer_right[...]], axis=1
    )
    dy = cot_ref[...].astype(F32) * kept_ref[:, 0:1]
    dh = dy + normed_back(da * vec_ref[2:3, :], hat, factor, 1)
    dh_ref[...] = dh
    dattn = dh.astype(BF16)
    dattn_ref[...] = dattn
    grads = dot(out_weight[...], dattn, 1, 1).astype(BF16)
    do_own_ref[...] = grads[:group]
    do_other_ref[...] = grads[group:]
    sums_ref[0:8, :] += fold_rows(da * hat)
    sums_ref[8:16, :] += fold_rows(da)
    sums_ref[16:24, :] += fold_rows(dattn.astype(F32))
    sums_ref[24:32, :] += fold_rows(dy.astype(BF16).astype(F32))

    @pl.when(pl.program_id(0) == pl.num_programs(0) - 1)
    def _():
        for row in range(4):
            total = jnp.sum(sums_ref[8 * row : 8 * row + 8, :], axis=0, keepdims=True)
            sums_out[row : row + 1, :] = total


def hidden_back(hidden, mine, peer, cot, kept, vec_params, out_own, out_other):
    tokens, width = hidden.shape
    group = out_own.shape[0]
    wide = rows_spec(width)
    cols = pl.BlockSpec((group, BLOCK), lambda i: (0, i))
    struct = jax.ShapeDtypeStruct
    return pl.pallas_call(
        functools.partial(hidden_back_kernel, group),
        grid=(tokens // BLOCK,),
        out_shape=[
            struct((tokens, width), F32),
            struct((tokens, width), BF16),
            struct((group, tokens), BF16),
            struct((group, tokens), BF16),
            struct((4, width), F32),
        ],
        in_specs=[
            wide, *(rows_spec(width // 2),) * 4, wide, rows_spec(LANES), whole_spec(vec_params.shape),
            whole_spec(out_own.shape), whole_spec(out_other.shape),
        ],
        out_specs=[wide, wide, cols, cols, sums_spec(4, width)],
        scratch_shapes=[pltpu.VMEM((2 * group, width), BF16), pltpu.VMEM((32, width), F32)],
        compiler_params=pltpu.CompilerParams(vmem_limit_bytes=22 << 20),
        cost_estimate=cost(4 * tokens * width * group, tokens * width * 22),
        name="hidden_back",
    )(hidden, *mine, *peer, cot, kept, vec_params, out_own, out_other)


def input_back_kernel(
    core_ref, mine_ref, peer_ref, x_ref, dh_ref, vec_ref, out_ref, sums_out, sums_ref
):
    @pl.when(pl.program_id(0) == 0)
    def _():
        sums_ref[...] = jnp.zeros_like(sums_ref)

    hat, factor = normed(x_ref[...].astype(F32), 1)
    da = mine_ref[...] + peer_ref[...]
    out_ref[...] = dh_ref[...] + normed_back(da * vec_ref[0:1, :], hat, factor, 1)
    sums_ref[0:8, :] += fold_rows(da * hat)
    sums_ref[8:16, :] += fold_rows(da)

    @pl.when(pl.program_id(0) == pl.num_programs(0) - 1)
    def _():
        for row in range(2):
            total = jnp.sum(sums_ref[8 * row : 8 * row + 8, :], axis=0, keepdims=True)
            sums_out[row : row + 1, :] = total


def input_back(core, mine, peer, x_win, dh, vec_params):
    half_rows, width = peer.shape
    step = LANES
    count = half_rows // step
    near = pl.BlockSpec((step, width), lambda i, core_ref: (i, 0))
    window = pl.BlockSpec((step, width), lambda i, core_ref: (core_ref[0] * count + i, 0))
    struct = jax.ShapeDtypeStruct
    return pl.pallas_call(
        input_back_kernel,
        grid_spec=pltpu.PrefetchScalarGridSpec(
            num_scalar_prefetch=1,
            grid=(count,),
            in_specs=[window, near, window, window, whole_spec(vec_params.shape)],
            out_specs=[near, sums_spec(2, width)],
            scratch_shapes=[pltpu.VMEM((16, width), F32)],
        ),
        out_shape=[struct((half_rows, width), F32), struct((2, width), F32)],
        cost_estimate=cost(0, half_rows * width * 18),
        name="input_back",
    )(core, mine, peer, x_win, dh, vec_params)


def join_kernel(half_rows, window, info_ref, factor_ref, shift_ref, mine_ref, near_ref, far_ref, far_near_ref, out_ref):
    seq_len = out_ref.shape[1]
    core, half, parting = info_ref[0], info_ref[1], info_ref[2]
    factor = factor_ref[0]
    step = LANES

    def rows_of(which, row):
        from_core = row // half_rows
        spot = pl.ds(row % half_rows, step)
        own = half == which
        same = core == from_core
        return jnp.where(
            own,
            jnp.where(same, mine_ref[spot, :], near_ref[spot, :]),
            jnp.where(same, far_ref[spot, :], far_near_ref[spot, :]),
        )

    offset = seq_len - window
    for row in range(0, seq_len, step):
        if row + step <= offset:
            values = rows_of(0, row)
        elif row >= window:
            values = rows_of(1, row - offset)
        else:
            places = row + lax.broadcasted_iota(jnp.int32, (step, 1), 0)
            values = jnp.where(places < parting, rows_of(0, row), rows_of(1, row - offset))
        out_ref[0, pl.ds(row, step), :] = (values * factor + shift_ref[...]).astype(BF16)


def join_sequence(links, mine, near, far, far_near, parting, seq_len, window, factor, shift):
    half_rows, width = mine.shape
    info = jnp.stack([links.mp % 2, links.mp // 2, parting]).astype(jnp.int32)
    return pl.pallas_call(
        functools.partial(join_kernel, half_rows, window),
        out_shape=jax.ShapeDtypeStruct((1, seq_len, width), BF16),
        in_specs=smem_specs(2) + vmem_specs(5),
        out_specs=pl.BlockSpec(memory_space=pltpu.VMEM),
        cost_estimate=cost(0, half_rows * width * 16 + seq_len * width * 2),
        name="join_sequence",
    )(info, factor, shift, mine, near, far, far_near)


def last_gradients_kernel(
    group, a_ref, dattn_ref, qk_ref, v_ref, o_own_ref, o_other_ref, qk_own_out, qk_other_out, vo_out
):
    a, dattn = a_ref[...], dattn_ref[...]
    query_key = jnp.transpose(dot(qk_ref[...], a, 1, 0))
    qk_own_out[...] = query_key[:, : 2 * group]
    qk_other_out[...] = query_key[:, 2 * group :]
    value = dot(v_ref[...], a, 1, 0)
    own, other = dot(o_own_ref[...], dattn, 1, 0), dot(o_other_ref[...], dattn, 1, 0)
    rows = jnp.concatenate([value[:group], own, value[group:], other], axis=0)
    vo_out[...] = jnp.transpose(rows)


def last_gradients(a_first, dattn, draw_qk, draw_v, o_own, o_other):
    tokens, width = a_first.shape
    group = o_own.shape[0]
    cols = pl.BlockSpec((tokens, BLOCK), lambda i: (0, i))
    narrow, wide = rows_spec(2 * group), rows_spec(4 * group)
    struct = jax.ShapeDtypeStruct
    inputs = (draw_qk, draw_v, o_own, o_other)
    return pl.pallas_call(
        functools.partial(last_gradients_kernel, group),
        grid=(width // BLOCK,),
        out_shape=[
            struct((width, 2 * group), F32),
            struct((width, 2 * group), F32),
            struct((width, 4 * group), F32),
        ],
        in_specs=[cols, cols, *(whole_spec(x.shape) for x in inputs)],
        out_specs=[narrow, narrow, wide],
        compiler_params=pltpu.CompilerParams(vmem_limit_bytes=20 << 20),
        cost_estimate=cost(16 * tokens * width * group, tokens * width * 12),
        name="last_gradients",
    )(a_first, dattn, *inputs)


def pack_kernel(
    core_ref, first_ref, second_ref, kept_ref, attn_ref, mlp_ref,
    own_ref, other_ref, own_bias_ref, other_bias_ref, mine_ref, away_ref,
):
    width = mine_ref.shape[1]
    once = jnp.where(core_ref[0] == 0, 1.0, 0.0)
    count = jnp.sum(kept_ref[...]) * (once / kept_ref.shape[1])
    attn = jnp.sum(attn_ref[...]) * once
    lane = lax.broadcasted_iota(jnp.int32, (1, width), 1)
    stats = jnp.where(lane == 0, count, jnp.where(lane == 1, attn, jnp.where(lane == 2, mlp_ref[0], 0.0)))
    sums, units = own_ref.shape[1], own_bias_ref.shape[1]
    for ref, head, bias in ((mine_ref, own_ref, own_bias_ref), (away_ref, other_ref, other_bias_ref)):
        ref[...] = jnp.zeros_like(ref)
        ref[0:2, :] = first_ref[...]
        ref[2:6, :] = second_ref[...] * once
        ref[6:7, :] = stats
        row = 8
        for source, size in ((head, sums), (bias, units)):
            for start in range(0, size, width):
                length = min(width, size - start)
                ref[row : row + 1, :length] = source[:, start : start + length]
                row += 1


def pack_small(core, first, second, kept, attn, mlp_sq, own, other, own_bias, other_bias):
    width = first.shape[1]
    inputs = (first, second, kept, attn)
    more = (own, other, own_bias, other_bias)
    rows = 8 + -(-own.shape[1] // width) + -(-own_bias.shape[1] // width)
    struct = jax.ShapeDtypeStruct((-(-rows // 8) * 8, width), F32)
    return pl.pallas_call(
        pack_kernel,
        out_shape=[struct, struct],
        in_specs=smem_specs(1) + vmem_specs(4) + smem_specs(1) + vmem_specs(4),
        out_specs=vmem_specs(2),
        compiler_params=pltpu.CompilerParams(vmem_limit_bytes=6 << 20),
        cost_estimate=cost(0, kept.size * 4),
        name="pack_small",
    )(core, *inputs, mlp_sq, *more)


def update_kernel(decays, *refs):
    scalars, count = refs[0], len(decays)
    inputs, outputs = refs[1 : 1 + 4 * count], refs[1 + 4 * count :]
    factor, corr_one, corr_two = scalars[0], scalars[1], scalars[2]
    for index, decay in enumerate(decays):
        weight_ref, grad_ref, first_ref, second_ref = inputs[4 * index : 4 * index + 4]
        shape = weight_ref.shape
        if index == 0:
            size = shape[2]
            spots = [(k, grad_ref[:, k * size : (k + 1) * size]) for k in range(shape[0])]
        elif index == 1:
            spots = [(slice(None), jnp.transpose(grad_ref[:, grad_ref.shape[1] - shape[0] :]))]
        elif index == 2:
            spots = [(slice(None), grad_ref[:, grad_ref.shape[1] - shape[1] :])]
        elif index == 3:
            spots = [(slice(None), grad_ref[:, : shape[1]])]
        else:
            spots = [(slice(None), grad_ref[...])]
        for spot, grad in spots:
            results = adam_step(
                weight_ref[spot], grad, first_ref[spot], second_ref[spot], factor, corr_one, corr_two, decay
            )
            for ref, value in zip(outputs[3 * index : 3 * index + 3], results):
                ref[spot] = value


def update(scalars, groups, decays):
    inputs = [array for group in groups for array in group]
    shapes = [
        jax.ShapeDtypeStruct(group[0].shape, F32) for group in groups for _ in range(3)
    ]
    results = pl.pallas_call(
        functools.partial(update_kernel, decays),
        out_shape=shapes,
        in_specs=smem_specs(1) + vmem_specs(len(inputs)),
        out_specs=vmem_specs(len(shapes)),
        cost_estimate=cost(0, sum(28 * group[0].size for group in groups)),
        name="update",
    )(scalars, *inputs)
    return [results[3 * k : 3 * k + 3] for k in range(len(groups))]


def local(
    patches, cotangent, keep_mask, segment_ids, step_count,
    qkv_weight, qkv_first, qkv_second,
    out_weight, out_first, out_second,
    up_weight, up_first, up_second,
    down_weight, down_first, down_second,
    head_params, head_first, head_second,
    up_bias, upb_first, upb_second,
    vec_params, vec_first, vec_second,
):
    links = Links()
    seq_len, width = patches.shape[1:]
    heads, dim = head_params.shape[1:]
    group = heads * dim
    units = up_weight.shape[1]
    window = seq_len // 2 + SEG_BOUND // 2
    half_rows = window // 2
    core = links.mp % 2
    start = (links.mp // 2) * (seq_len - window)

    qkv_flip = jnp.swapaxes(qkv_weight, 1, 2)
    qkv_base = links.half(quarter_of(links, qkv_flip, 1))
    small = jnp.concatenate([head_params.reshape(-1), up_bias])
    small_other = links.half(small)
    head_other = small_other[: head_params.size].reshape(head_params.shape)

    def columns(params):
        return jnp.pad(params.reshape(params.shape[0], group).T, ((0, 0), (0, 3)))

    head_cols = columns(head_params)
    other_cols = columns(head_other)
    upb_own = up_bias.reshape(1, units)
    upb_other = small_other[head_params.size :].reshape(1, units)

    plan, qseg, kcode, kept = make_plan(links, segment_ids, keep_mask, window)
    parting = plan[0, 2]
    x_win = lax.dynamic_slice_in_dim(patches[0], start, window, 0)
    cot_win = lax.dynamic_slice_in_dim(cotangent[0], start, window, 0)
    a_first, *own = own_heads(x_win, vec_params, qkv_flip, head_cols, heads, dim)

    qkv_base = hold(qkv_base, own[0])
    qkv_pieces = [qkv_base, links.data(qkv_base, 0), links.data(qkv_base, 1)]
    both = [(i, i ^ 3) for i in range(links.dp_size)]
    qkv_pieces.append(lax.ppermute(qkv_base, "dp", both))
    spots = quarter_spots(links)
    up_down = quarter_of(links, jnp.stack([up_weight, down_weight]), 1)
    mlp_base = links.half(hold(up_down, qkv_base, small_other))
    own += attention(plan, hold(own[0], qkv_base), own[1], own[2], kcode, qseg, heads, dim)

    qkv_pieces = list(lax.optimization_barrier((*qkv_pieces, own[6]))[:4])
    *other, qk_cat, value_cat = other_heads(
        spots, a_first, qkv_flip, qkv_pieces, other_cols, heads, dim
    )
    mlp_base = hold(mlp_base, other[0])
    out_other = links.half(hold(out_weight, own[6]))
    eighth = mlp_base.shape[1] // 2
    part_a, part_b = mlp_base[:, :eighth], mlp_base[:, eighth:]
    near_a, near_b = links.data(part_a, 0), links.data(part_b, 1)
    other += attention(plan, hold(other[0], mlp_base), other[1], other[2], kcode, qseg, heads, dim)
    o_other, near_a, near_b = lax.optimization_barrier((other[6], near_a, near_b))
    attn_part = out_project(own[6], o_other, out_weight, out_other)
    pair_a, pair_b = jnp.stack([part_a, near_a]), jnp.stack([part_b, near_b])
    far_a, far_b = links.data(pair_a, 1), links.data(pair_b, 0)
    attn_peer = links.core(attn_part)
    hidden, a_second, dmlp, gated, grad_upper, mlp_part, da_part, upb_sums, attn_sums = own_mlp(
        x_win, attn_part, attn_peer, cot_win, kept, vec_params, up_weight, down_weight, upb_own
    )
    down, up = Reduction(links, dot(dmlp, gated, 0, 0)), Reduction(links, dot(a_second, grad_upper, 0, 0))
    down_sent, up_sent = down.send(0), up.send(1)
    down_got, up_got = links.data(down_sent, 0), links.data(up_sent, 1)
    gated, grad_upper, mlp_part, *da_parts, upb_sums_other = other_mlp(
        spots, hold(a_second, down_sent, up_sent), dmlp, mlp_part, da_part,
        (mlp_base, near_a, near_b, far_a, far_b), upb_other,
    )
    da_peers = [links.core(part) for part in da_parts]
    gated, grad_upper, down_got, up_got = lax.optimization_barrier(
        (gated, grad_upper, down_got, up_got)
    )
    down.take(down_got)
    up.take(up_got)
    down_other = Reduction(links, dot(dmlp, gated, 0, 0))
    up_other = Reduction(links, dot(a_second, grad_upper, 0, 0))
    down_sent, up_sent = down_other.send(0), up_other.send(1)
    down_got, up_got = links.data(down_sent, 0), links.data(up_sent, 1)
    def my_rows(array):
        return lax.dynamic_slice_in_dim(array, core * half_rows, half_rows, 0)

    def peer_rows(array):
        return lax.dynamic_slice_in_dim(array, (1 - core) * half_rows, half_rows, 0)

    mlp_sum = my_rows(mlp_part) + links.core(peer_rows(mlp_part))
    result_mine = my_rows(hidden) + mlp_sum
    result_far = links.half(result_mine)
    mlp_mine = mlp_sum + vec_params[5]
    mlp_sq = jnp.sum(my_rows(kept[:, :1]) * mlp_mine * mlp_mine)
    dh, dattn, do_own, do_other, row_sums = hidden_back(
        hold(hidden, down_sent, up_sent, result_mine), da_parts, da_peers, cot_win, kept, vec_params,
        out_weight, out_other,
    )

    *draws, own_sums = attention_back(plan, own, do_own, head_cols, kcode, qseg, heads, dim)
    down_other.take(hold(down_got, draws[1]))
    up_other.take(hold(up_got, draws[1]))
    down.array = jnp.concatenate([down.array, down_other.array], axis=-1)
    up.array = jnp.concatenate([up.array, up_other.array], axis=-1)
    down_sent, up_sent = down.send(1), up.send(0)
    down_got, up_got = links.data(down_sent, 1), links.data(up_sent, 0)
    result_near = links.core(result_mine)
    *draws, other_sums = attention_back(
        plan, other, hold(do_other, down_sent, up_sent, result_far, result_near), other_cols, kcode,
        qseg, heads, dim, draws,
    )
    down.take(hold(down_got, draws[1]))
    up.take(hold(up_got, draws[1]))
    mlp = Reduction(links, jnp.zeros((width, 1), F32))
    mlp.left = list(down.left)
    mlp_sent = jnp.concatenate([down.array[..., units:], up.array[..., units:]], axis=-1)
    mlp.kept = jnp.concatenate([down.array[..., :units], up.array[..., :units]], axis=-1)
    mlp_got = links.half(mlp_sent)
    result_far_near = links.core(hold(result_far, draws[1]))
    draws = lax.optimization_barrier((*draws, mlp_sent))[:2]
    qk_own, qk_other, value_out = last_gradients(a_first, dattn, *draws, own[6], other[6])
    last_bits = list(mlp.left)
    value_out = Reduction(links, value_out)
    value_out_sent = value_out.send(0)
    qk_got, value_out_got = links.half(qk_other), links.data(value_out_sent, 0)
    da1_part = dot(draws[0], qk_cat, 0, 0) + dot(draws[1], value_cat, 0, 0)
    da1_sent = peer_rows(da1_part)
    da1_peer = links.core(da1_sent)
    grad_mine, first_sums = input_back(
        jnp.full((1,), core, jnp.int32), hold(da1_part, result_far_near), da1_peer, x_win, dh, vec_params
    )
    grad_near = links.core(grad_mine)

    mlp.take(hold(mlp_got, grad_mine))
    mlp_sent = mlp.send(last_bits[0])
    mlp_got = links.data(mlp_sent, last_bits[0])
    value_out.take(hold(value_out_got, grad_mine))
    value_out_sent = value_out.send(1)
    value_out_got = links.data(value_out_sent, 1)
    query_key = Reduction(links, qk_own + hold(qk_got, value_out_sent))
    query_key_sent = query_key.send(0)
    query_key_got = links.data(query_key_sent, 0)
    core_index = jnp.full((1,), core, jnp.int32)
    mine, away = pack_small(
        core_index, hold(first_sums, query_key_sent), row_sums, kept, attn_sums, mlp_sq.reshape(1),
        own_sums, other_sums, upb_sums, upb_sums_other,
    )
    summed = mine + links.half(away)
    shared = summed[:8]
    summed = jnp.concatenate([shared + links.core(shared), summed[8:]], axis=0)
    value_out.take(hold(value_out_got, query_key_sent, mlp_got))
    value_out_sent = value_out.send("half")
    value_out_got = links.half(value_out_sent)
    query_key.take(hold(query_key_got, summed))
    query_key_sent = query_key.send(1)
    query_key_got = links.data(query_key_sent, 1)
    summed = hold(summed, query_key_sent)
    summed = summed + links.data(summed, 0)
    value_out_got = hold(value_out_got, query_key_sent)
    value_out.take(value_out_got)
    grad_far = links.half(hold(grad_mine, value_out_got))
    query_key.take(hold(query_key_got, summed))
    last = Reduction(links, jnp.zeros((width, 1), F32))
    last.left = list(last_bits)
    last.array = jnp.concatenate([query_key.array, value_out.array], axis=-1)
    last_sent = last.send(last_bits[0])
    last_got = links.data(last_sent, last_bits[0])
    summed = hold(summed, last_sent)
    for bit in range(1, links.bits):
        summed = summed + links.data(summed, bit)
    mlp.take(mlp_got)
    for bit in last_bits[1:]:
        mlp.step(bit)
    one = jnp.ones((1,), F32)
    result = join_sequence(
        links, hold(result_mine, last_sent), result_near, result_far, result_far_near, parting, seq_len,
        window, one, vec_params[5:6],
    )
    rows = width // links.dp_size
    first_row = links.dp * rows
    qkv_weight, out_weight, up_weight, down_weight, _ = lax.optimization_barrier(
        (qkv_weight, out_weight, up_weight, down_weight, value_out_got)
    )
    old_shares = (
        lax.dynamic_slice_in_dim(qkv_weight, first_row, rows, 1),
        lax.dynamic_slice_in_dim(out_weight, first_row, rows, 1),
        lax.dynamic_slice_in_dim(up_weight, first_row, rows, 0),
        lax.dynamic_slice_in_dim(down_weight, first_row, rows, 1).T,
    )
    last_got, result, summed, *old_shares = lax.optimization_barrier(
        (last_got, result, summed, *old_shares)
    )
    last.take(last_got)
    while last.left:
        last.step(last.left[0])
    last_share = last.array

    vec_grad = summed[:6]
    stats = summed[6, :3]
    tail = summed[8:].reshape(-1)
    head_grad = tail[: head_params.size].reshape(head_params.shape)
    head_rows = -(-own_sums.shape[1] // width)
    bup_grad = tail[head_rows * width : head_rows * width + units]
    count = stats[0]
    scale = seq_len * links.dp_size / count
    shares = (last_share, last_share, mlp.array, mlp.array)
    first_dp = links.dp == 0
    first_mp = links.mp == 0
    big_sq = jnp.sum(last_share * last_share) + jnp.sum(mlp.array * mlp.array)
    split_sq = jnp.sum(head_grad * head_grad) + jnp.sum(bup_grad * bup_grad)
    whole_sq = jnp.sum(vec_grad * vec_grad)
    raw_sq = (
        big_sq + jnp.where(first_dp, split_sq, 0.0) + jnp.where(first_dp & first_mp, whole_sq, 0.0)
    )
    sq_total = links.sum_all(raw_sq)
    grad_norm = scale * jnp.sqrt(sq_total)
    factor = jnp.minimum(1.0, CLIP_LIMIT / (grad_norm + 1e-06)) * scale
    steps_f = step_count[0].astype(F32)
    corr_one = 1.0 - BETA_ONE**steps_f
    corr_two = 1.0 - BETA_TWO**steps_f
    grad_far = hold(grad_far, sq_total)
    grad_input = join_sequence(
        links, grad_mine, grad_near, grad_far, links.core(grad_far), parting, seq_len, window, scale.reshape(1), jnp.zeros((1, width), F32)
    )
    new_qkv, new_out, new_up, new_down, new_head, new_vec = update(
        jnp.stack([factor, corr_one, corr_two]),
        [
            (old_shares[0], shares[0], qkv_first, qkv_second),
            (old_shares[1], shares[1], out_first, out_second),
            (old_shares[2], shares[2], up_first, up_second),
            (old_shares[3], shares[3], down_first.T, down_second.T),
            (head_params, head_grad, head_first, head_second),
            (vec_params, vec_grad, vec_first, vec_second),
        ],
        (WEIGHT_DECAY,) * 4 + (0.0,) * 2,
    )
    new_down = [array.T for array in new_down]
    new_upb = adam_step(
        up_bias, bup_grad, upb_first, upb_second, factor, corr_one, corr_two, 0.0
    )
    rms = jnp.sqrt(stats[1:] / (count * width))
    return (
        result, grad_input, *new_qkv, *new_out, *new_up, *new_down, *new_head, *new_upb, *new_vec,
        grad_norm.reshape(1), rms,
    )


def solution(mesh):
    seq = P("dp", None, None)
    row = P("dp", None)
    qkv = P(None, "dp", "mp")
    out = P("mp", "dp")
    up = P("dp", "mp")
    head = P(None, "mp", None)
    unit = P("mp")
    whole = P()
    return jax.shard_map(
        local,
        mesh=mesh,
        in_specs=(
            *(seq, seq, row, row, whole),
            *(P(None, None, "mp"), qkv, qkv),
            *(P("mp", None), out, out),
            *(P(None, "mp"), up, up),
            *(P("mp", None), out, out),
            *(head, head, head),
            *(unit, unit, unit),
            *(whole, whole, whole),
        ),
        out_specs=(
            *(seq, seq),
            *(qkv, qkv, qkv),
            *(out, out, out),
            *(up, up, up),
            *(out, out, out),
            *(head, head, head),
            *(unit, unit, unit),
            *(whole, whole, whole),
            *(whole, whole),
        ),
        check_vma=False,
    )
```

```python
import functools

import jax
import jax.numpy as jnp
from jax import lax
from jax.experimental import pallas as pl
from jax.experimental.pallas import tpu as pltpu
from jax.sharding import PartitionSpec as P

NORM_EPS = 1e-06
CLIP_LIMIT = 1.0
LEARN_RATE = 0.1
BETA_ONE = 0.9
BETA_TWO = 0.95
ADAM_EPS = 1e-08
WEIGHT_DECAY = 0.1
SEG_BOUND = 512
BLOCK = 256
LANES = 128
F32 = jnp.float32
BF16 = jnp.bfloat16


def adam_step(weight, grad, first, second, factor, corr_one, corr_two, decay):
    grad = factor * grad
    first = BETA_ONE * first + (1.0 - BETA_ONE) * grad
    second = BETA_TWO * second + (1.0 - BETA_TWO) * grad * grad
    update = first / corr_one / (jnp.sqrt(second / corr_two) + ADAM_EPS)
    return (weight - LEARN_RATE * (update + decay * weight), first, second)


def dot(left, right, left_dim, right_dim):
    return lax.dot_general(
        left, right, (((left_dim,), (right_dim,)), ((), ())), preferred_element_type=F32
    )


class Links:
    def __init__(self):
        self.dp_size = lax.axis_size("dp")
        self.mp_size = lax.axis_size("mp")
        self.bits = self.dp_size.bit_length() - 1
        self.dp = lax.axis_index("dp")
        self.mp = lax.axis_index("mp")

    def core(self, array):
        return lax.ppermute(array, "mp", [(i, i ^ 1) for i in range(self.mp_size)])

    def half(self, array):
        return lax.ppermute(array, "mp", [(i, i ^ 2) for i in range(self.mp_size)])

    def data(self, array, bit):
        return lax.ppermute(array, "dp", [(i, i ^ (1 << bit)) for i in range(self.dp_size)])

    def bit(self, bit):
        return (self.dp >> bit) & 1

    def sum_all(self, array):
        array = array + self.core(array)
        array = array + self.half(array)
        return self.sum_data(array)

    def sum_data(self, array):
        for bit in range(self.bits):
            array = array + self.data(array, bit)
        return array


def hold(value, *after):
    return lax.optimization_barrier((value, *after))[0]


def quarter_of(links, weight, axis):
    rows = weight.shape[axis] // 4
    return lax.dynamic_slice_in_dim(weight, (links.dp & 3) * rows, rows, axis)


def quarter_spots(links):
    return jnp.stack([(links.dp & 3) ^ change for change in range(4)])


class Reduction:
    def __init__(self, links, grad):
        self.links = links
        self.left = list(range(links.bits - 1, -1, -1))
        self.array = grad.reshape((2,) * links.bits + (grad.shape[0] >> links.bits, grad.shape[1]))

    def send(self, step):
        if step == "half":
            own = self.array.shape[-1] // 2
            self.kept = self.array[..., :own]
            return self.array[..., own:]
        axis = self.left.index(step)
        self.left.remove(step)
        mine = self.links.bit(step)
        self.kept = lax.dynamic_index_in_dim(self.array, mine, axis, keepdims=False)
        return lax.dynamic_index_in_dim(self.array, 1 - mine, axis, keepdims=False)

    def take(self, arrived):
        self.array = self.kept + arrived

    def step(self, step, *after):
        sent = self.send(step)
        sent = hold(sent, *after) if after else sent
        self.take(self.links.half(sent) if step == "half" else self.links.data(sent, step))


def vmem_specs(count):
    return [pl.BlockSpec(memory_space=pltpu.VMEM)] * count


def smem_specs(count):
    return [pl.BlockSpec(memory_space=pltpu.SMEM)] * count


def cost(flops, bytes_accessed, transcendentals=0):
    return pl.CostEstimate(
        flops=int(flops), bytes_accessed=int(bytes_accessed), transcendentals=int(transcendentals)
    )


def normed(values, axis):
    scale = 1.0 / values.shape[axis]
    center = values - jnp.sum(values, axis=axis, keepdims=True) * scale
    spread = jnp.sum(center * center, axis=axis, keepdims=True) * scale
    factor = lax.rsqrt(spread + NORM_EPS)
    return center * factor, factor


def normed_back(grad_hat, hat, factor, axis):
    scale = 1.0 / hat.shape[axis]
    mean = jnp.sum(grad_hat, axis=axis, keepdims=True) * scale
    along = jnp.sum(grad_hat * hat, axis=axis, keepdims=True) * scale
    return factor * (grad_hat - mean - hat * along)


def fold_rows(values):
    return jnp.sum(values.reshape(values.shape[0] // 8, 8, values.shape[1]), axis=0)


def fold_lanes(values):
    total = values[:, :LANES]
    for start in range(LANES, values.shape[1], LANES):
        total = total + values[:, start : start + LANES]
    return total


def column(row, count):
    return jnp.transpose(jnp.broadcast_to(row, (count, row.shape[1])))


def plan_kernel(window, half_ref, seg_ref, keep_ref, plan_ref, qseg_ref, kcode_ref, kept_ref):
    seq_len = seg_ref.shape[1]
    seg = seg_ref[...]
    half = half_ref[0]
    places = lax.broadcasted_iota(jnp.int32, (1, seq_len), 1)
    starts = (seg != pltpu.roll(seg, 1, 1)) & (places > 0)
    ranking = jnp.where(starts, jnp.abs(places - seq_len // 2) * (4 * seq_len) + places, 1 << 30)
    parting = lax.rem(jnp.min(ranking), 4 * seq_len)
    start = pl.multiple_of(half * (seq_len - window), LANES)
    low_valid = jnp.where(half == 0, 0, parting - start)
    high_valid = jnp.where(half == 0, parting, window)
    seg_win = seg_ref[:, pl.ds(start, window)]
    keep_win = keep_ref[:, pl.ds(start, window)]
    spots = lax.broadcasted_iota(jnp.int32, (1, window), 1)
    valid = (spots >= low_valid) & (spots < high_valid)
    qseg_ref[...] = jnp.broadcast_to(seg_win, (8, window))
    kcode_ref[...] = column(jnp.where(keep_win == 1, seg_win, -1), LANES)
    kept_ref[...] = column(jnp.where(valid & (keep_win == 1), 1.0, 0.0), LANES)
    segs = jnp.broadcast_to(seg_win, (8, window))
    lanes = lax.broadcasted_iota(jnp.int32, (8, window), 1)
    block = lax.broadcasted_iota(jnp.int32, (8, window), 0) * BLOCK

    def total(values):
        return jnp.sum(values, axis=1, keepdims=True)

    first_seg = total(jnp.where(lanes == block, segs, 0))
    last_seg = total(jnp.where(lanes == block + (BLOCK - 1), segs, 0))
    low = total(jnp.where(segs < first_seg, 1, 0))
    high = total(jnp.where(segs <= last_seg, 1, 0))
    block_first = block[:, :1]
    low = jnp.maximum(low, low_valid)
    high = jnp.minimum(high, high_valid) + (BLOCK - 1)
    shift = BLOCK.bit_length() - 1
    low, high = low >> shift, high >> shift
    live = (block_first < high_valid) & (block_first + BLOCK > low_valid)
    high = jnp.where(live, high, low)
    lane = lax.broadcasted_iota(jnp.int32, (8, LANES), 1)
    plan = jnp.where(lane == 0, low, jnp.where(lane == 1, high, parting))
    plan_ref[...] = plan


def make_plan(links, seg_row, keep_row, window):
    half = jnp.full((1,), links.mp // 2, jnp.int32)
    return pl.pallas_call(
        functools.partial(plan_kernel, window),
        out_shape=(
            jax.ShapeDtypeStruct((8, LANES), jnp.int32),
            jax.ShapeDtypeStruct((8, window), jnp.int32),
            jax.ShapeDtypeStruct((window, LANES), jnp.int32),
            jax.ShapeDtypeStruct((window, LANES), F32),
        ),
        in_specs=smem_specs(1) + vmem_specs(2),
        out_specs=tuple(vmem_specs(4)),
        compiler_params=pltpu.CompilerParams(vmem_limit_bytes=6 << 20),
        cost_estimate=cost(0, window * 1100),
        name="plan_window",
    )(half, seg_row, keep_row)


def allowed_block(kcode_ref, qseg_ref, key_start, query_start):
    codes = kcode_ref[pl.ds(key_start, BLOCK), :]
    codes = jnp.concatenate([codes] * (BLOCK // LANES), axis=1)
    segs = qseg_ref[0:1, pl.ds(query_start, BLOCK)]
    rows = lax.broadcasted_iota(jnp.int32, (BLOCK, BLOCK), 0)
    cols = lax.broadcasted_iota(jnp.int32, (BLOCK, BLOCK), 1)
    return (codes == segs) | (rows - cols == query_start - key_start)


def project_heads(heads, dim, weight, a_ref, params_ref, qkv_refs, hat_refs, factor_ref):
    tokens = a_ref.shape[0]
    group = heads * dim

    def block(tb, carry):
        ts = pl.multiple_of(tb * BLOCK, BLOCK)
        here = pl.ds(ts, BLOCK)
        rows = a_ref[here, :]
        for which in range(3):
            raw = dot(weight[which][...], rows, 1, 1) + params_ref[:, which : which + 1]
            if which == 2:
                qkv_refs[2][:, here] = raw.astype(BF16)
                continue
            hat, factor = normed(raw.reshape(heads, dim, BLOCK), 1)
            hat = hat.reshape(group, BLOCK)
            gained = hat * params_ref[:, 3 + which : 4 + which]
            if which == 0:
                gained = gained * dim ** (-0.5)
            qkv_refs[which][:, here] = gained.astype(BF16)
            hat_refs[which][:, here] = hat.astype(BF16)
            for head in range(heads):
                spot = (which * heads + head) * 8
                factor_ref[pl.ds(spot, 8), here] = jnp.broadcast_to(factor[head], (8, BLOCK))
        return carry

    lax.fori_loop(0, tokens // BLOCK, block, 0)


def attend(heads, dim, plan_ref, q_ref, k_ref, v_ref, kcode_ref, qseg_ref, o_ref, inv_ref, acc, tot):
    tokens = q_ref.shape[1]

    def query_block(qb, carry):
        qs = pl.multiple_of(qb * BLOCK, BLOCK)
        acc[...] = jnp.zeros_like(acc)
        tot[...] = jnp.zeros_like(tot)

        def key_block(kb, carry):
            ks = pl.multiple_of(kb * BLOCK, BLOCK)
            allowed = allowed_block(kcode_ref, qseg_ref, ks, qs)
            lines = [pl.ds(head * dim, dim) for head in range(heads)]
            scores = [dot(k_ref[rows, pl.ds(ks, BLOCK)], q_ref[rows, pl.ds(qs, BLOCK)], 0, 0) for rows in lines]
            expos = [jnp.where(allowed, jnp.exp(score), 0.0) for score in scores]
            more = [dot(v_ref[rows, pl.ds(ks, BLOCK)], expo.astype(BF16), 1, 0) for rows, expo in zip(lines, expos)]
            for head, rows in enumerate(lines):
                tot[pl.ds(head * 8, 8), :] += fold_rows(expos[head])
                acc[rows, :] += more[head]
            return carry

        lax.fori_loop(plan_ref[qb, 0], plan_ref[qb, 1], key_block, 0)
        for head in range(heads):
            rows = pl.ds(head * dim, dim)
            total = jnp.sum(tot[pl.ds(head * 8, 8), :], axis=0, keepdims=True)
            inverse = jnp.where(total > 0.0, 1.0 / total, 0.0)
            o_ref[rows, pl.ds(qs, BLOCK)] = (acc[rows, :] * inverse).astype(BF16)
            inv_ref[pl.ds(head * 8, 8), pl.ds(qs, BLOCK)] = jnp.broadcast_to(inverse, (8, BLOCK))
        return carry

    lax.fori_loop(0, tokens // BLOCK, query_block, 0)


def own_heads_kernel(
    heads, dim, x_ref, vec_ref, weight_ref, params_ref,
    a_ref, q_ref, k_ref, v_ref, qh_ref, kh_ref, factor_ref, weight,
):
    weight[...] = weight_ref[...].astype(BF16)
    tokens = x_ref.shape[0]

    def norm_block(tb, carry):
        here = pl.ds(pl.multiple_of(tb * BLOCK, BLOCK), BLOCK)
        hat, _ = normed(x_ref[here, :].astype(F32), 1)
        a_ref[here, :] = (hat * vec_ref[0:1, :] + vec_ref[1:2, :]).astype(BF16)
        return carry

    lax.fori_loop(0, tokens // BLOCK, norm_block, 0)
    project_heads(
        heads, dim, [weight.at[k] for k in range(3)], a_ref, params_ref, (q_ref, k_ref, v_ref),
        (qh_ref, kh_ref), factor_ref,
    )


def other_heads_kernel(
    heads, dim, spots_ref, a_ref, own_ref, p0, p1, p2, p3, params_ref,
    q_ref, k_ref, v_ref, qh_ref, kh_ref, factor_ref, qk_ref, value_ref,
):
    group = heads * dim
    places = [
        (qk_ref.at[pl.ds(0, group)], qk_ref.at[pl.ds(2 * group, group)]),
        (qk_ref.at[pl.ds(group, group)], qk_ref.at[pl.ds(3 * group, group)]),
        (value_ref.at[pl.ds(0, group)], value_ref.at[pl.ds(group, group)]),
    ]
    for which, (own_place, place) in enumerate(places):
        own_place[...] = own_ref[which].astype(BF16)
        for index, piece in enumerate((p0, p1, p2, p3)):
            count = piece.shape[1]
            spot = pl.multiple_of(spots_ref[index] * count, 16)
            place[pl.ds(spot, count), :] = piece[which].astype(BF16)
    project_heads(
        heads, dim, [place for _, place in places], a_ref, params_ref, (q_ref, k_ref, v_ref), (qh_ref, kh_ref), factor_ref
    )


def attention_kernel(
    heads, dim, plan_ref, q_ref, k_ref, v_ref, kcode_ref, qseg_ref, o_ref, inv_ref, acc, tot
):
    attend(heads, dim, plan_ref, q_ref, k_ref, v_ref, kcode_ref, qseg_ref, o_ref, inv_ref, acc, tot)


def out_kernel(o_own_ref, o_other_ref, own_ref, other_ref, part_ref, weight, o_cat):
    group = own_ref.shape[0]

    @pl.when(pl.program_id(0) == 0)
    def _():
        weight[pl.ds(0, group), :] = own_ref[...].astype(BF16)
        weight[pl.ds(group, group), :] = other_ref[...].astype(BF16)

    o_cat[pl.ds(0, group), :] = o_own_ref[...]
    o_cat[pl.ds(group, group), :] = o_other_ref[...]
    part_ref[...] = dot(o_cat[...], weight[...], 0, 0)


def head_shapes(group, heads, tokens):
    narrow = jax.ShapeDtypeStruct((group, tokens), BF16)
    return [*(narrow,) * 5, jax.ShapeDtypeStruct((heads * 16, tokens), F32)]


def o_shapes(group, heads, tokens):
    return [
        jax.ShapeDtypeStruct((group, tokens), BF16),
        jax.ShapeDtypeStruct((heads * 8, tokens), F32),
    ]


def own_heads(x_win, vec_params, weight, params, heads, dim):
    tokens, width = x_win.shape
    group = heads * dim
    return pl.pallas_call(
        functools.partial(own_heads_kernel, heads, dim),
        out_shape=[
            jax.ShapeDtypeStruct((tokens, width), BF16),
            *head_shapes(group, heads, tokens),
        ],
        in_specs=vmem_specs(4),
        out_specs=vmem_specs(7),
        scratch_shapes=[pltpu.VMEM((3, group, width), BF16)],
        cost_estimate=cost(tokens * width * group * 6, tokens * width * 8),
        name="heads_own",
    )(x_win, vec_params, weight, params)


def other_heads(spots, a_first, own_weight, pieces, params, heads, dim):
    tokens, width = a_first.shape
    group = heads * dim
    return pl.pallas_call(
        functools.partial(other_heads_kernel, heads, dim),
        out_shape=[
            *head_shapes(group, heads, tokens),
            jax.ShapeDtypeStruct((4 * group, width), BF16),
            jax.ShapeDtypeStruct((2 * group, width), BF16),
        ],
        in_specs=smem_specs(1) + vmem_specs(7),
        out_specs=vmem_specs(8),
        cost_estimate=cost(tokens * width * group * 6, tokens * width * 8),
        name="heads_other",
    )(spots, a_first, own_weight, *pieces, params)


def attention(plan, query, key, value, kcode, qseg, heads, dim):
    group, tokens = query.shape
    pairs = heads * tokens * 3 * BLOCK
    return pl.pallas_call(
        functools.partial(attention_kernel, heads, dim),
        out_shape=o_shapes(group, heads, tokens),
        in_specs=smem_specs(1) + vmem_specs(5),
        out_specs=vmem_specs(2),
        scratch_shapes=[pltpu.VMEM((group, BLOCK), F32), pltpu.VMEM((heads * 8, BLOCK), F32)],
        cost_estimate=cost(pairs * dim * 4, group * tokens * 8, pairs),
        name="attention",
    )(plan, query, key, value, kcode, qseg)


def out_project(o_own, o_other, out_own, out_other):
    group, tokens = o_own.shape
    width = out_own.shape[1]
    cols = pl.BlockSpec((group, BLOCK), lambda i: (0, i))
    return pl.pallas_call(
        out_kernel,
        grid=(tokens // BLOCK,),
        out_shape=jax.ShapeDtypeStruct((tokens, width), F32),
        in_specs=[cols, cols, whole_spec(out_own.shape), whole_spec(out_other.shape)],
        out_specs=rows_spec(width),
        scratch_shapes=[
            pltpu.VMEM((2 * group, width), BF16),
            pltpu.VMEM((2 * group, BLOCK), BF16),
        ],
        compiler_params=pltpu.CompilerParams(vmem_limit_bytes=12 << 20),
        cost_estimate=cost(tokens * width * group * 4, tokens * width * 6),
        name="out_project",
    )(o_own, o_other, out_own, out_other)


def attention_back_kernel(
    heads, dim, plan_ref, q_ref, k_ref, v_ref, qh_ref, kh_ref, factor_ref, o_ref, inv_ref, do_ref,
    params_ref, kcode_ref, qseg_ref, *rest,
):
    draw_qk_ref, draw_v_ref = rest[-7:-5]
    out_sums_ref, dq_ref, dk_ref, dv_ref, sums_ref = rest[-5:]
    group, tokens = q_ref.shape
    for ref in (dq_ref, dk_ref, dv_ref, sums_ref):
        ref[...] = jnp.zeros_like(ref)

    def query_block(qb, carry):
        qs = pl.multiple_of(qb * BLOCK, BLOCK)
        here = pl.ds(qs, BLOCK)
        deltas = []
        inverses = []
        for head in range(heads):
            rows = pl.ds(head * dim, dim)
            products = do_ref[rows, here].astype(F32) * o_ref[rows, here].astype(F32)
            deltas.append(jnp.sum(products, axis=0, keepdims=True))
            inverses.append(inv_ref[pl.ds(head * 8, 1), here])

        def key_block(kb, carry):
            ks = pl.multiple_of(kb * BLOCK, BLOCK)
            there = pl.ds(ks, BLOCK)
            allowed = allowed_block(kcode_ref, qseg_ref, ks, qs)
            lines = [pl.ds(head * dim, dim) for head in range(heads)]
            keys = [k_ref[rows, there] for rows in lines]
            queries = [q_ref[rows, here] for rows in lines]
            grads = [do_ref[rows, here] for rows in lines]
            scores = [dot(key, query, 0, 0) for key, query in zip(keys, queries)]
            grad_probs = [dot(v_ref[rows, there], grad, 0, 0) for rows, grad in zip(lines, grads)]
            added = []
            for head in range(heads):
                probs = jnp.where(allowed, jnp.exp(scores[head]), 0.0) * inverses[head]
                grad_scores = (probs * (grad_probs[head] - deltas[head])).astype(BF16)
                added.append((
                    dot(grads[head], probs.astype(BF16), 1, 1),
                    dot(queries[head], grad_scores, 1, 1),
                    dot(keys[head], grad_scores, 1, 0),
                ))
            for rows, (more_v, more_k, more_q) in zip(lines, added):
                dv_ref[rows, there] += more_v
                dk_ref[rows, there] += more_k
                dq_ref[rows, here] += more_q
            return carry

        lax.fori_loop(plan_ref[qb, 0], plan_ref[qb, 1], key_block, 0)
        return carry

    lax.fori_loop(0, tokens // BLOCK, query_block, 0)

    def token_block(tb, carry):
        here = pl.ds(pl.multiple_of(tb * BLOCK, BLOCK), BLOCK)
        for which, (grad_ref, hat_ref) in enumerate(((dq_ref, qh_ref), (dk_ref, kh_ref), (dv_ref, None))):
            rows = pl.ds(which * group, group)
            grad = grad_ref[:, here]
            if hat_ref is not None:
                if which == 0:
                    grad = grad * dim ** (-0.5)
                hat = hat_ref[:, here].astype(F32)
                sums_ref[pl.ds((3 + which) * group, group), :] += fold_lanes(grad * hat)
                grad = grad * params_ref[:, 3 + which : 4 + which]
                parts = []
                for head in range(heads):
                    lines = slice(head * dim, (head + 1) * dim)
                    factor = factor_ref[pl.ds((which * heads + head) * 8, 1), here]
                    parts.append(normed_back(grad[lines], hat[lines], factor, 0))
                grad = jnp.concatenate(parts, axis=0)
            rounded = grad.astype(BF16)
            if which < 2:
                draw_qk_ref[rows, here] = rounded
            else:
                draw_v_ref[:, here] = rounded
            sums_ref[rows, :] += fold_lanes(rounded.astype(F32))
        return carry

    lax.fori_loop(0, tokens // BLOCK, token_block, 0)
    out_sums_ref[...] = jnp.sum(jnp.transpose(sums_ref[...]), axis=0, keepdims=True)


def attention_back(plan, saved, grad_o, params, kcode, qseg, heads, dim, draws=None):
    group, tokens = saved[0].shape
    pairs = heads * tokens * 3 * BLOCK
    which = 0 if draws is None else 1
    sums = -(-5 * group // LANES) * LANES
    inputs = [*saved, grad_o, params, kcode, qseg]
    in_specs = smem_specs(1) + [whole_spec(x.shape) for x in inputs]
    aliases = {}
    if draws is not None:
        aliases = {1 + len(inputs) + k: k for k in range(2)}
        inputs += draws
        in_specs += [pl.BlockSpec(memory_space=pl.ANY)] * 2
    return pl.pallas_call(
        functools.partial(attention_back_kernel, heads, dim),
        grid=(1,),
        out_shape=[
            jax.ShapeDtypeStruct((4 * group, tokens), BF16),
            jax.ShapeDtypeStruct((2 * group, tokens), BF16),
            jax.ShapeDtypeStruct((1, sums), F32),
        ],
        in_specs=in_specs,
        out_specs=[
            pl.BlockSpec((2 * group, tokens), lambda i: (which, 0)),
            pl.BlockSpec((group, tokens), lambda i: (which, 0)),
            whole_spec((1, sums)),
        ],
        scratch_shapes=[
            *(pltpu.VMEM((group, tokens), F32),) * 3,
            pltpu.VMEM((sums, LANES), F32),
        ],
        input_output_aliases=aliases,
        compiler_params=pltpu.CompilerParams(vmem_limit_bytes=16 << 20),
        cost_estimate=cost(pairs * dim * 10, group * tokens * 30, pairs),
        name="attention_back",
    )(plan, *inputs)


ERFC_TERMS = (
    0.16918800576031592, 0.17071521752915575, 0.14833923939584578, 0.2149257797248009,
    -0.09465005158893602, 0.5477190245253036, -0.5122771874066157, 0.4855627631921905,
    -0.1295228107166713,
)


def gelu_and_slope(values):
    t = 1.0 / (1.0 + (0.3 * 0.5**0.5) * jnp.abs(values))
    poly = ERFC_TERMS[-1]
    for term in ERFC_TERMS[-2::-1]:
        poly = poly * t + term
    bell = jnp.exp(values * values * -0.5)
    low_tail = 0.5 * (t * poly) * bell
    below = jnp.where(values > 0.0, 1.0 - low_tail, low_tail)
    return values * below, below + values * bell * 0.3989422804014327


def mlp_half(a, dmlp, up, down, bias):
    upper = dot(a, up, 1, 0) + bias
    gated, slope = gelu_and_slope(upper)
    gated = gated.astype(BF16)
    grad_gated = dot(dmlp, down, 1, 1)
    grad_upper = (grad_gated * slope).astype(BF16)
    return gated, grad_upper, dot(gated, down, 1, 0), dot(grad_upper, up, 1, 1)


def own_mlp_kernel(
    x_ref, mine_ref, peer_ref, cot_ref, kept_ref, vec_ref, up_ref, down_ref, bias_ref,
    hidden_ref, a_ref, dmlp_ref, g_ref, du_ref, mlp_ref, da_ref, bias_out, attn_out, up, down, bias_sums, attn_sums,
):
    @pl.when(pl.program_id(0) == 0)
    def _():
        up[...] = up_ref[...].astype(BF16)
        down[...] = down_ref[...].astype(BF16)
        bias_sums[...] = jnp.zeros_like(bias_sums)
        attn_sums[...] = jnp.zeros_like(attn_sums)

    kept = kept_ref[:, 0:1]
    attn = mine_ref[...] + peer_ref[...] + vec_ref[4:5, :]
    attn_sums[...] += fold_rows(kept * attn * attn)
    hidden = x_ref[...].astype(F32) + attn
    hidden_ref[...] = hidden
    hat, _ = normed(hidden, 1)
    a = (hat * vec_ref[2:3, :] + vec_ref[3:4, :]).astype(BF16)
    a_ref[...] = a
    dmlp = (cot_ref[...].astype(F32) * kept).astype(BF16)
    dmlp_ref[...] = dmlp
    gated, grad_upper, mlp, da = mlp_half(a, dmlp, up[...], down[...], bias_ref[...])
    g_ref[...] = gated
    du_ref[...] = grad_upper
    mlp_ref[...] = mlp
    da_ref[...] = da
    bias_sums[...] += fold_rows(grad_upper.astype(F32))

    @pl.when(pl.program_id(0) == pl.num_programs(0) - 1)
    def _():
        bias_out[...] = jnp.sum(bias_sums[...], axis=0, keepdims=True)
        attn_out[...] = jnp.sum(attn_sums[...], axis=0, keepdims=True)


def other_mlp_kernel(
    spots_ref, a_ref, dmlp_ref, mlp_in_ref, da_in_ref, base, near_a, near_b, far_a, far_b, bias_ref,
    g_ref, du_ref, mlp_ref, da_left_ref, da_right_ref, bias_out, up, down, bias_sums,
):
    @pl.when(pl.program_id(0) == 0)
    def _():
        count = near_a.shape[1]
        for change, first, second in (
            (0, base.at[:, pl.ds(0, count)], base.at[:, pl.ds(count, count)]),
            (1, near_a, far_b.at[0]),
            (2, far_a.at[0], near_b),
            (3, far_a.at[1], far_b.at[1]),
        ):
            for which, piece in enumerate((first, second)):
                spot = pl.multiple_of((spots_ref[change] * 2 + which) * count, 16)
                up[pl.ds(spot, count), :] = piece[0].astype(BF16)
                down[pl.ds(spot, count), :] = piece[1].astype(BF16)
        bias_sums[...] = jnp.zeros_like(bias_sums)

    gated, grad_upper, mlp, da = mlp_half(
        a_ref[...], dmlp_ref[...], up[...], down[...], bias_ref[...]
    )
    g_ref[...] = gated
    du_ref[...] = grad_upper
    mlp_ref[...] = mlp_in_ref[...] + mlp
    da = da_in_ref[...] + da
    cut = da_left_ref.shape[1]
    da_left_ref[...], da_right_ref[...] = da[:, :cut], da[:, cut:]
    bias_sums[...] += fold_rows(grad_upper.astype(F32))

    @pl.when(pl.program_id(0) == pl.num_programs(0) - 1)
    def _():
        bias_out[...] = jnp.sum(bias_sums[...], axis=0, keepdims=True)


def rows_spec(width):
    return pl.BlockSpec((BLOCK, width), lambda i: (i, 0))


def whole_spec(shape):
    return pl.BlockSpec(shape, lambda *_: (0,) * len(shape), pipeline_mode=pl.Buffered(1))


def sums_spec(rows, width):
    return pl.BlockSpec((rows, width), lambda *_: (0, 0))


def own_mlp(x_win, mine, peer, cot, kept, vec_params, up_weight, down_weight, bias):
    tokens, width = x_win.shape
    units = up_weight.shape[1]
    wide = rows_spec(width)
    struct = jax.ShapeDtypeStruct
    return pl.pallas_call(
        own_mlp_kernel,
        grid=(tokens // BLOCK,),
        out_shape=[
            struct((tokens, width), F32),
            struct((tokens, width), BF16),
            struct((tokens, width), BF16),
            struct((tokens, units), BF16),
            struct((tokens, units), BF16),
            struct((tokens, width), F32),
            struct((tokens, width), F32),
            struct((1, units), F32),
            struct((1, width), F32),
        ],
        in_specs=[
            wide, wide, wide, wide, rows_spec(LANES), whole_spec(vec_params.shape),
            whole_spec(up_weight.shape), whole_spec(down_weight.shape), whole_spec(bias.shape),
        ],
        out_specs=[
            wide, wide, wide, rows_spec(units), rows_spec(units), wide, wide,
            sums_spec(1, units), sums_spec(1, width),
        ],
        scratch_shapes=[
            pltpu.VMEM(up_weight.shape, BF16),
            pltpu.VMEM(down_weight.shape, BF16),
            pltpu.VMEM((8, units), F32),
            pltpu.VMEM((8, width), F32),
        ],
        cost_estimate=cost(8 * tokens * width * units, tokens * width * 40, tokens * units * 2),
        name="mlp_own",
    )(x_win, mine, peer, cot, kept, vec_params, up_weight, down_weight, bias)


def other_mlp(spots, a_second, dmlp, mlp_part, da_part, pieces, bias):
    tokens, width = a_second.shape
    units = bias.shape[1]
    wide = rows_spec(width)
    struct = jax.ShapeDtypeStruct
    return pl.pallas_call(
        other_mlp_kernel,
        grid=(tokens // BLOCK,),
        out_shape=[
            struct((tokens, units), BF16),
            struct((tokens, units), BF16),
            struct((tokens, width), F32),
            struct((tokens, width // 2), F32),
            struct((tokens, width // 2), F32),
            struct((1, units), F32),
        ],
        in_specs=[
            *smem_specs(1), wide, wide, wide, wide,
            *(whole_spec(piece.shape) for piece in pieces), whole_spec(bias.shape),
        ],
        out_specs=[
            rows_spec(units), rows_spec(units), wide, *(rows_spec(width // 2),) * 2, sums_spec(1, units),
        ],
        input_output_aliases={3: 2},
        scratch_shapes=[
            pltpu.VMEM((width, units), BF16),
            pltpu.VMEM((units, width), BF16),
            pltpu.VMEM((8, units), F32),
        ],
        cost_estimate=cost(8 * tokens * width * units, tokens * width * 28, tokens * units * 2),
        name="mlp_other",
    )(spots, a_second, dmlp, mlp_part, da_part, *pieces, bias)


def hidden_back_kernel(
    group, hidden_ref, mine_left, mine_right, peer_left, peer_right, cot_ref, kept_ref, vec_ref, out_own_ref, out_other_ref,
    dh_ref, dattn_ref, do_own_ref, do_other_ref, sums_out, out_weight, sums_ref,
):
    @pl.when(pl.program_id(0) == 0)
    def _():
        out_weight[pl.ds(0, group), :] = out_own_ref[...].astype(BF16)
        out_weight[pl.ds(group, group), :] = out_other_ref[...].astype(BF16)
        sums_ref[...] = jnp.zeros_like(sums_ref)

    hat, factor = normed(hidden_ref[...], 1)
    da = jnp.concatenate(
        [mine_left[...] + peer_left[...], mine_right[...] + peer_right[...]], axis=1
    )
    dy = cot_ref[...].astype(F32) * kept_ref[:, 0:1]
    dh = dy + normed_back(da * vec_ref[2:3, :], hat, factor, 1)
    dh_ref[...] = dh
    dattn = dh.astype(BF16)
    dattn_ref[...] = dattn
    grads = dot(out_weight[...], dattn, 1, 1).astype(BF16)
    do_own_ref[...] = grads[:group]
    do_other_ref[...] = grads[group:]
    sums_ref[0:8, :] += fold_rows(da * hat)
    sums_ref[8:16, :] += fold_rows(da)
    sums_ref[16:24, :] += fold_rows(dattn.astype(F32))
    sums_ref[24:32, :] += fold_rows(dy.astype(BF16).astype(F32))

    @pl.when(pl.program_id(0) == pl.num_programs(0) - 1)
    def _():
        for row in range(4):
            total = jnp.sum(sums_ref[8 * row : 8 * row + 8, :], axis=0, keepdims=True)
            sums_out[row : row + 1, :] = total


def hidden_back(hidden, mine, peer, cot, kept, vec_params, out_own, out_other):
    tokens, width = hidden.shape
    group = out_own.shape[0]
    wide = rows_spec(width)
    cols = pl.BlockSpec((group, BLOCK), lambda i: (0, i))
    struct = jax.ShapeDtypeStruct
    return pl.pallas_call(
        functools.partial(hidden_back_kernel, group),
        grid=(tokens // BLOCK,),
        out_shape=[
            struct((tokens, width), F32),
            struct((tokens, width), BF16),
            struct((group, tokens), BF16),
            struct((group, tokens), BF16),
            struct((4, width), F32),
        ],
        in_specs=[
            wide, *(rows_spec(width // 2),) * 4, wide, rows_spec(LANES), whole_spec(vec_params.shape),
            whole_spec(out_own.shape), whole_spec(out_other.shape),
        ],
        out_specs=[wide, wide, cols, cols, sums_spec(4, width)],
        scratch_shapes=[pltpu.VMEM((2 * group, width), BF16), pltpu.VMEM((32, width), F32)],
        compiler_params=pltpu.CompilerParams(vmem_limit_bytes=22 << 20),
        cost_estimate=cost(4 * tokens * width * group, tokens * width * 22),
        name="hidden_back",
    )(hidden, *mine, *peer, cot, kept, vec_params, out_own, out_other)


def input_back_kernel(
    core_ref, mine_ref, peer_ref, x_ref, dh_ref, vec_ref, left_ref, right_ref, sums_out, sums_ref
):
    @pl.when(pl.program_id(0) == 0)
    def _():
        sums_ref[...] = jnp.zeros_like(sums_ref)

    hat, factor = normed(x_ref[...].astype(F32), 1)
    da = mine_ref[...] + peer_ref[...]
    out = dh_ref[...] + normed_back(da * vec_ref[0:1, :], hat, factor, 1)
    cut = left_ref.shape[1]
    left_ref[...], right_ref[...] = out[:, :cut], out[:, cut:]
    sums_ref[0:8, :] += fold_rows(da * hat)
    sums_ref[8:16, :] += fold_rows(da)

    @pl.when(pl.program_id(0) == pl.num_programs(0) - 1)
    def _():
        for row in range(2):
            total = jnp.sum(sums_ref[8 * row : 8 * row + 8, :], axis=0, keepdims=True)
            sums_out[row : row + 1, :] = total


def input_back(core, mine, peer, x_win, dh, vec_params):
    half_rows, width = peer.shape
    step = LANES
    count = half_rows // step
    near = pl.BlockSpec((step, width), lambda i, core_ref: (i, 0))
    left = pl.BlockSpec((step, width // 2), lambda i, core_ref: (i, 0))
    window = pl.BlockSpec((step, width), lambda i, core_ref: (core_ref[0] * count + i, 0))
    struct = jax.ShapeDtypeStruct
    return pl.pallas_call(
        input_back_kernel,
        grid_spec=pltpu.PrefetchScalarGridSpec(
            num_scalar_prefetch=1,
            grid=(count,),
            in_specs=[window, near, window, window, whole_spec(vec_params.shape)],
            out_specs=[left, left, sums_spec(2, width)],
            scratch_shapes=[pltpu.VMEM((16, width), F32)],
        ),
        out_shape=[
            struct((half_rows, width // 2), F32),
            struct((half_rows, width // 2), F32),
            struct((2, width), F32),
        ],
        cost_estimate=cost(0, half_rows * width * 18),
        name="input_back",
    )(core, mine, peer, x_win, dh, vec_params)


def last_gradients_kernel(
    group, a_ref, dattn_ref, qk_ref, v_ref, o_own_ref, o_other_ref, qk_own_out, qk_other_out, vo_out
):
    a, dattn = a_ref[...], dattn_ref[...]
    query_key = jnp.transpose(dot(qk_ref[...], a, 1, 0))
    qk_own_out[...] = query_key[:, : 2 * group]
    qk_other_out[...] = query_key[:, 2 * group :]
    value = dot(v_ref[...], a, 1, 0)
    own, other = dot(o_own_ref[...], dattn, 1, 0), dot(o_other_ref[...], dattn, 1, 0)
    rows = jnp.concatenate([value[:group], own, value[group:], other], axis=0)
    vo_out[...] = jnp.transpose(rows)


def last_gradients(a_first, dattn, draw_qk, draw_v, o_own, o_other):
    tokens, width = a_first.shape
    group = o_own.shape[0]
    cols = pl.BlockSpec((tokens, BLOCK), lambda i: (0, i))
    narrow, wide = rows_spec(2 * group), rows_spec(4 * group)
    struct = jax.ShapeDtypeStruct
    inputs = (draw_qk, draw_v, o_own, o_other)
    return pl.pallas_call(
        functools.partial(last_gradients_kernel, group),
        grid=(width // BLOCK,),
        out_shape=[
            struct((width, 2 * group), F32),
            struct((width, 2 * group), F32),
            struct((width, 4 * group), F32),
        ],
        in_specs=[cols, cols, *(whole_spec(x.shape) for x in inputs)],
        out_specs=[narrow, narrow, wide],
        compiler_params=pltpu.CompilerParams(vmem_limit_bytes=20 << 20),
        cost_estimate=cost(16 * tokens * width * group, tokens * width * 12),
        name="last_gradients",
    )(a_first, dattn, *inputs)


def pack_kernel(
    core_ref, first_ref, second_ref, kept_ref, attn_ref, mlp_ref,
    own_ref, other_ref, own_bias_ref, other_bias_ref, mine_ref, away_ref,
):
    width = mine_ref.shape[1]
    once = jnp.where(core_ref[0] == 0, 1.0, 0.0)
    count = jnp.sum(kept_ref[...]) * (once / kept_ref.shape[1])
    attn = jnp.sum(attn_ref[...]) * once
    lane = lax.broadcasted_iota(jnp.int32, (1, width), 1)
    stats = jnp.where(lane == 0, count, jnp.where(lane == 1, attn, jnp.where(lane == 2, mlp_ref[0], 0.0)))
    sums, units = own_ref.shape[1], own_bias_ref.shape[1]
    for ref, head, bias in ((mine_ref, own_ref, own_bias_ref), (away_ref, other_ref, other_bias_ref)):
        ref[...] = jnp.zeros_like(ref)
        ref[0:2, :] = first_ref[...]
        ref[2:6, :] = second_ref[...] * once
        ref[6:7, :] = stats
        row = 8
        for source, size in ((head, sums), (bias, units)):
            for start in range(0, size, width):
                length = min(width, size - start)
                ref[row : row + 1, :length] = source[:, start : start + length]
                row += 1


def pack_small(core, first, second, kept, attn, mlp_sq, own, other, own_bias, other_bias):
    width = first.shape[1]
    inputs = (first, second, kept, attn)
    more = (own, other, own_bias, other_bias)
    rows = 8 + -(-own.shape[1] // width) + -(-own_bias.shape[1] // width)
    struct = jax.ShapeDtypeStruct((-(-rows // 8) * 8, width), F32)
    return pl.pallas_call(
        pack_kernel,
        out_shape=[struct, struct],
        in_specs=smem_specs(1) + vmem_specs(4) + smem_specs(1) + vmem_specs(4),
        out_specs=vmem_specs(2),
        compiler_params=pltpu.CompilerParams(vmem_limit_bytes=6 << 20),
        cost_estimate=cost(0, kept.size * 4),
        name="pack_small",
    )(core, *inputs, mlp_sq, *more)


def update_kernel(decays, *refs):
    scalars, count = refs[0], len(decays)
    inputs, outputs = refs[1 : 1 + 4 * count], refs[1 + 4 * count :]
    factor, corr_one, corr_two = scalars[0], scalars[1], scalars[2]
    for index, decay in enumerate(decays):
        weight_ref, grad_ref, first_ref, second_ref = inputs[4 * index : 4 * index + 4]
        shape = weight_ref.shape
        if index == 0:
            size = shape[2]
            spots = [(k, grad_ref[:, k * size : (k + 1) * size]) for k in range(shape[0])]
        elif index == 1:
            spots = [(slice(None), jnp.transpose(grad_ref[:, grad_ref.shape[1] - shape[0] :]))]
        elif index == 2:
            spots = [(slice(None), grad_ref[:, grad_ref.shape[1] - shape[1] :])]
        elif index == 3:
            spots = [(slice(None), grad_ref[:, : shape[1]])]
        else:
            spots = [(slice(None), grad_ref[...])]
        for spot, grad in spots:
            results = adam_step(
                weight_ref[spot], grad, first_ref[spot], second_ref[spot], factor, corr_one, corr_two, decay
            )
            for ref, value in zip(outputs[3 * index : 3 * index + 3], results):
                ref[spot] = value


def update(scalars, groups, decays):
    inputs = [array for group in groups for array in group]
    shapes = [
        jax.ShapeDtypeStruct(group[0].shape, F32) for group in groups for _ in range(3)
    ]
    results = pl.pallas_call(
        functools.partial(update_kernel, decays),
        out_shape=shapes,
        in_specs=smem_specs(1) + vmem_specs(len(inputs)),
        out_specs=vmem_specs(len(shapes)),
        cost_estimate=cost(0, sum(28 * group[0].size for group in groups)),
        name="update",
    )(scalars, *inputs)
    return [results[3 * k : 3 * k + 3] for k in range(len(groups))]


def join_kernel(half_rows, window, pieces, info_ref, factor_ref, shift_ref, *refs):
    out_ref = refs[-1]
    seq_len = out_ref.shape[1]
    core, half, parting = info_ref[0], info_ref[1], info_ref[2]
    factor = factor_ref[0]
    step = LANES
    offset = seq_len - window
    start = 0
    for piece in range(pieces):
        mine_ref, near_ref, far_ref, far_near_ref = refs[4 * piece : 4 * piece + 4]
        cols = slice(start, start + mine_ref.shape[1])
        start += mine_ref.shape[1]
        shift = shift_ref[:, cols]

        def rows_of(which, row, mine=mine_ref, near=near_ref, far=far_ref, far_near=far_near_ref):
            from_core = row // half_rows
            spot = pl.ds(pl.multiple_of(row - from_core * half_rows, step), step)
            same = core == from_core
            return jnp.where(
                half == which,
                jnp.where(same, mine[spot, :], near[spot, :]),
                jnp.where(same, far[spot, :], far_near[spot, :]),
            )

        def store(row, values, cols=cols, shift=shift):
            spot = pl.ds(pl.multiple_of(row, step), step)
            out_ref[0, spot, cols] = (values * factor + shift).astype(BF16)

        def first(block, carry, rows_of=rows_of, store=store):
            store(block * step, rows_of(0, block * step))
            return carry

        def middle(block, carry, rows_of=rows_of, store=store):
            row = block * step
            places = row + lax.broadcasted_iota(jnp.int32, (step, 1), 0)
            store(row, jnp.where(places < parting, rows_of(0, row), rows_of(1, row - offset)))
            return carry

        def second(block, carry, rows_of=rows_of, store=store):
            store(block * step, rows_of(1, block * step - offset))
            return carry

        lax.fori_loop(0, offset // step, first, 0)
        lax.fori_loop(offset // step, window // step, middle, 0)
        lax.fori_loop(window // step, seq_len // step, second, 0)


def join_sequence(links, pieces, parting, seq_len, window, factor, shift):
    half_rows = pieces[0][0].shape[0]
    width = shift.shape[1]
    info = jnp.stack([links.mp % 2, links.mp // 2, parting]).astype(jnp.int32)
    arrays = [array for piece in pieces for array in piece]
    return pl.pallas_call(
        functools.partial(join_kernel, half_rows, window, len(pieces)),
        out_shape=jax.ShapeDtypeStruct((1, seq_len, width), BF16),
        in_specs=smem_specs(2) + vmem_specs(1 + len(arrays)),
        out_specs=pl.BlockSpec(memory_space=pltpu.VMEM),
        cost_estimate=cost(0, half_rows * width * 16 + seq_len * width * 2),
        name="join_sequence",
    )(info, factor, shift, *arrays)


def local(
    patches, cotangent, keep_mask, segment_ids, step_count,
    qkv_weight, qkv_first, qkv_second,
    out_weight, out_first, out_second,
    up_weight, up_first, up_second,
    down_weight, down_first, down_second,
    head_params, head_first, head_second,
    up_bias, upb_first, upb_second,
    vec_params, vec_first, vec_second,
):
    links = Links()
    seq_len, width = patches.shape[1:]
    heads, dim = head_params.shape[1:]
    group = heads * dim
    units = up_weight.shape[1]
    window = seq_len // 2 + SEG_BOUND // 2
    half_rows = window // 2
    core = links.mp % 2
    start = (links.mp // 2) * (seq_len - window)

    qkv_flip = jnp.swapaxes(qkv_weight, 1, 2)
    qkv_base = links.half(quarter_of(links, qkv_flip, 1))
    small = jnp.concatenate([head_params.reshape(-1), up_bias])
    small_other = links.half(small)
    head_other = small_other[: head_params.size].reshape(head_params.shape)

    def columns(params):
        return jnp.pad(params.reshape(params.shape[0], group).T, ((0, 0), (0, 3)))

    head_cols = columns(head_params)
    other_cols = columns(head_other)
    upb_own = up_bias.reshape(1, units)
    upb_other = small_other[head_params.size :].reshape(1, units)

    plan, qseg, kcode, kept = make_plan(links, segment_ids, keep_mask, window)
    parting = plan[0, 2]
    x_win = lax.dynamic_slice_in_dim(patches[0], start, window, 0)
    cot_win = lax.dynamic_slice_in_dim(cotangent[0], start, window, 0)
    a_first, *own = own_heads(x_win, vec_params, qkv_flip, head_cols, heads, dim)

    qkv_base = hold(qkv_base, own[0])
    qkv_pieces = [qkv_base, links.data(qkv_base, 0), links.data(qkv_base, 1)]
    both = [(i, i ^ 3) for i in range(links.dp_size)]
    qkv_pieces.append(lax.ppermute(qkv_base, "dp", both))
    spots = quarter_spots(links)
    up_early, down_early, _, _ = lax.optimization_barrier(
        (up_weight, down_weight, qkv_base, small_other)
    )
    mlp_base = links.half(quarter_of(links, jnp.stack([up_early, down_early]), 1))
    own += attention(plan, hold(own[0], qkv_base), own[1], own[2], kcode, qseg, heads, dim)

    qkv_pieces = list(lax.optimization_barrier((*qkv_pieces, own[6]))[:4])
    *other, qk_cat, value_cat = other_heads(
        spots, hold(a_first, cot_win), qkv_flip, qkv_pieces, other_cols, heads, dim
    )
    mlp_base = hold(mlp_base, other[0])
    out_other = links.half(hold(out_weight, own[6]))
    eighth = mlp_base.shape[1] // 2
    part_a, part_b = mlp_base[:, :eighth], mlp_base[:, eighth:]
    near_a, near_b = links.data(part_a, 0), links.data(part_b, 1)
    other += attention(plan, hold(other[0], mlp_base), other[1], other[2], kcode, qseg, heads, dim)
    o_other, near_a, near_b = lax.optimization_barrier((other[6], near_a, near_b))
    attn_part = out_project(own[6], o_other, out_weight, out_other)
    pair_a, pair_b = jnp.stack([part_a, near_a]), jnp.stack([part_b, near_b])
    far_a, far_b = links.data(pair_a, 1), links.data(pair_b, 0)
    attn_peer = links.core(attn_part)
    hidden, a_second, dmlp, gated, grad_upper, mlp_part, da_part, upb_sums, attn_sums = own_mlp(
        x_win, attn_part, attn_peer, cot_win, kept, vec_params, up_weight, down_weight, upb_own
    )
    down, up = Reduction(links, dot(dmlp, gated, 0, 0)), Reduction(links, dot(a_second, grad_upper, 0, 0))
    down_sent, up_sent = down.send(0), up.send(1)
    down_got, up_got = links.data(down_sent, 0), links.data(up_sent, 1)
    gated, grad_upper, mlp_part, *da_parts, upb_sums_other = other_mlp(
        spots, hold(a_second, down_sent, up_sent), dmlp, mlp_part, da_part,
        (mlp_base, near_a, near_b, far_a, far_b), upb_other,
    )
    da_peers = [links.core(part) for part in da_parts]
    gated, grad_upper, down_got, up_got = lax.optimization_barrier(
        (gated, grad_upper, down_got, up_got)
    )
    down.take(down_got)
    up.take(up_got)
    down_other = Reduction(links, dot(dmlp, gated, 0, 0))
    up_other = Reduction(links, dot(a_second, grad_upper, 0, 0))
    down_sent, up_sent = down_other.send(0), up_other.send(1)
    down_got, up_got = links.data(down_sent, 0), links.data(up_sent, 1)
    def my_rows(array):
        return lax.dynamic_slice_in_dim(array, core * half_rows, half_rows, 0)

    def peer_rows(array):
        return lax.dynamic_slice_in_dim(array, (1 - core) * half_rows, half_rows, 0)

    mlp_sum = my_rows(mlp_part) + links.core(peer_rows(mlp_part))
    result_mine = my_rows(hidden) + mlp_sum
    result_far = links.half(result_mine)
    mlp_mine = mlp_sum + vec_params[5]
    mlp_sq = jnp.sum(my_rows(kept[:, :1]) * mlp_mine * mlp_mine)
    dh, dattn, do_own, do_other, row_sums = hidden_back(
        hold(hidden, down_sent, up_sent, result_mine), da_parts, da_peers, cot_win, kept, vec_params,
        out_weight, out_other,
    )

    *draws, own_sums = attention_back(plan, own, do_own, head_cols, kcode, qseg, heads, dim)
    down_other.take(hold(down_got, draws[1]))
    up_other.take(hold(up_got, draws[1]))
    down.array = jnp.concatenate([down.array, down_other.array], axis=-1)
    up.array = jnp.concatenate([up.array, up_other.array], axis=-1)
    down_sent, up_sent = down.send(1), up.send(0)
    down_got, up_got = links.data(down_sent, 1), links.data(up_sent, 0)
    result_near = links.core(result_mine)
    *draws, other_sums = attention_back(
        plan, other, hold(do_other, down_sent, up_sent, result_far, result_near), other_cols, kcode,
        qseg, heads, dim, draws,
    )
    down.take(hold(down_got, draws[1]))
    up.take(hold(up_got, draws[1]))
    mlp = Reduction(links, jnp.zeros((width, 1), F32))
    mlp.left = list(down.left)
    mlp_sent = jnp.concatenate([down.array[..., units:], up.array[..., units:]], axis=-1)
    mlp.kept = jnp.concatenate([down.array[..., :units], up.array[..., :units]], axis=-1)
    mlp_got = links.half(mlp_sent)
    result_far_near = links.core(hold(result_far, draws[1]))
    draws = lax.optimization_barrier((*draws, mlp_sent))[:2]
    qk_own, qk_other, value_out = last_gradients(a_first, dattn, *draws, own[6], other[6])
    last_bits = list(mlp.left)
    value_out = Reduction(links, value_out)
    value_out_sent = value_out.send(0)
    qk_got, value_out_got = links.half(qk_other), links.data(value_out_sent, 0)
    da1_part = dot(draws[0], qk_cat, 0, 0) + dot(draws[1], value_cat, 0, 0)
    da1_sent = peer_rows(da1_part)
    da1_peer = links.core(da1_sent)
    grad_left, grad_right, first_sums = input_back(
        jnp.full((1,), core, jnp.int32), hold(da1_part, result_far_near), da1_peer, x_win, dh, vec_params
    )
    grad_nears = [links.core(grad_left), links.core(grad_right)]
    far_left = links.half(grad_left)

    mlp.take(hold(mlp_got, grad_left))
    mlp_sent = mlp.send(last_bits[0])
    mlp_got = links.data(mlp_sent, last_bits[0])
    value_out.take(hold(value_out_got, grad_left))
    value_out_sent = value_out.send(1)
    value_out_got = links.data(value_out_sent, 1)
    rows = width // links.dp_size
    first_row = links.dp * rows
    old_shares = (
        lax.dynamic_slice_in_dim(qkv_weight, first_row, rows, 1),
        lax.dynamic_slice_in_dim(out_weight, first_row, rows, 1),
        lax.dynamic_slice_in_dim(up_weight, first_row, rows, 0),
        lax.dynamic_slice_in_dim(down_weight, first_row, rows, 1).T,
    )
    query_key = Reduction(links, qk_own + hold(qk_got, value_out_sent, *old_shares))
    query_key_sent = query_key.send(0)
    query_key_got = links.data(query_key_sent, 0)
    core_index = jnp.full((1,), core, jnp.int32)
    mine, away = pack_small(
        core_index, hold(first_sums, query_key_sent), row_sums, kept, attn_sums, mlp_sq.reshape(1),
        own_sums, other_sums, upb_sums, upb_sums_other,
    )
    summed = mine + links.half(away)
    value_out.take(hold(value_out_got, query_key_sent, mlp_got))
    value_out_sent = value_out.send("half")
    value_out_got = links.half(value_out_sent)
    one = jnp.ones((1,), F32)
    result = join_sequence(
        links, [(hold(result_mine, query_key_sent), result_near, result_far, result_far_near)], parting,
        seq_len, window, one, vec_params[5:6],
    )
    query_key.take(hold(query_key_got, summed, result, far_left))
    query_key_sent = query_key.send(1)
    query_key_got = links.data(query_key_sent, 1)
    summed = hold(summed, query_key_sent)
    shared = summed[:8]
    summed = jnp.concatenate([shared + links.core(shared), summed[8:]], axis=0)
    value_out_got = hold(value_out_got, query_key_sent)
    value_out.take(value_out_got)
    far_right = links.half(hold(grad_right, value_out_got))
    far_near_left = links.core(hold(far_left, value_out_got))
    query_key.take(hold(query_key_got, summed))
    last = Reduction(links, jnp.zeros((width, 1), F32))
    last.left = list(last_bits)
    last.array = jnp.concatenate([query_key.array, value_out.array], axis=-1)
    last_sent = last.send(last_bits[0])
    last_got = links.data(last_sent, last_bits[0])
    summed = hold(summed, last_sent)
    summed = links.sum_data(summed)
    mlp.take(mlp_got)
    for bit in last_bits[1:]:
        mlp.step(bit)
    last_got, summed = lax.optimization_barrier((last_got, summed))
    last.take(last_got)
    while last.left:
        last.step(last.left[0])
    last_share = last.array

    vec_grad = summed[:6]
    stats = summed[6, :3]
    tail = summed[8:].reshape(-1)
    head_grad = tail[: head_params.size].reshape(head_params.shape)
    head_rows = -(-own_sums.shape[1] // width)
    bup_grad = tail[head_rows * width : head_rows * width + units]
    count = stats[0]
    scale = seq_len * links.dp_size / count
    shares = (last_share, last_share, mlp.array, mlp.array)
    first_dp = links.dp == 0
    first_mp = links.mp == 0
    big_sq = jnp.sum(last_share * last_share) + jnp.sum(mlp.array * mlp.array)
    split_sq = jnp.sum(head_grad * head_grad) + jnp.sum(bup_grad * bup_grad)
    whole_sq = jnp.sum(vec_grad * vec_grad)
    raw_sq = (
        big_sq + jnp.where(first_dp, split_sq, 0.0) + jnp.where(first_dp & first_mp, whole_sq, 0.0)
    )
    sq_total = links.sum_all(raw_sq)
    grad_norm = scale * jnp.sqrt(sq_total)
    factor = jnp.minimum(1.0, CLIP_LIMIT / (grad_norm + 1e-06)) * scale
    steps_f = step_count[0].astype(F32)
    corr_one = 1.0 - BETA_ONE**steps_f
    corr_two = 1.0 - BETA_TWO**steps_f
    far_right = hold(far_right, sq_total)
    grad_input = join_sequence(
        links,
        [
            (grad_left, grad_nears[0], far_left, far_near_left),
            (grad_right, grad_nears[1], far_right, links.core(far_right)),
        ],
        parting, seq_len, window, scale.reshape(1), jnp.zeros((1, width), F32),
    )
    new_qkv, new_out, new_up, new_down, new_head, new_vec = update(
        jnp.stack([factor, corr_one, corr_two]),
        [
            (old_shares[0], shares[0], qkv_first, qkv_second),
            (old_shares[1], shares[1], out_first, out_second),
            (old_shares[2], shares[2], up_first, up_second),
            (old_shares[3], shares[3], down_first.T, down_second.T),
            (head_params, head_grad, head_first, head_second),
            (vec_params, vec_grad, vec_first, vec_second),
        ],
        (WEIGHT_DECAY,) * 4 + (0.0,) * 2,
    )
    new_down = [array.T for array in new_down]
    new_upb = adam_step(
        up_bias, bup_grad, upb_first, upb_second, factor, corr_one, corr_two, 0.0
    )
    rms = jnp.sqrt(stats[1:] / (count * width))
    return (
        result, grad_input, *new_qkv, *new_out, *new_up, *new_down, *new_head, *new_upb, *new_vec,
        grad_norm.reshape(1), rms,
    )


def solution(mesh):
    seq = P("dp", None, None)
    row = P("dp", None)
    qkv = P(None, "dp", "mp")
    out = P("mp", "dp")
    up = P("dp", "mp")
    head = P(None, "mp", None)
    unit = P("mp")
    whole = P()
    return jax.shard_map(
        local,
        mesh=mesh,
        in_specs=(
            *(seq, seq, row, row, whole),
            *(P(None, None, "mp"), qkv, qkv),
            *(P("mp", None), out, out),
            *(P(None, "mp"), up, up),
            *(P("mp", None), out, out),
            *(head, head, head),
            *(unit, unit, unit),
            *(whole, whole, whole),
        ),
        out_specs=(
            *(seq, seq),
            *(qkv, qkv, qkv),
            *(out, out, out),
            *(up, up, up),
            *(out, out, out),
            *(head, head, head),
            *(unit, unit, unit),
            *(whole, whole, whole),
            *(whole, whole),
        ),
        check_vma=False,
    )
```

```python
import functools

import jax
import jax.numpy as jnp
from jax import lax
from jax.experimental import pallas as pl
from jax.experimental.pallas import tpu as pltpu
from jax.sharding import PartitionSpec as P

NORM_EPS = 1e-06
CLIP_LIMIT = 1.0
LEARN_RATE = 0.1
BETA_ONE = 0.9
BETA_TWO = 0.95
ADAM_EPS = 1e-08
WEIGHT_DECAY = 0.1
SEG_BOUND = 512
BLOCK = 256
LANES = 128
F32 = jnp.float32
BF16 = jnp.bfloat16


def adam_step(weight, grad, first, second, factor, corr_one, corr_two, decay):
    grad = factor * grad
    first = BETA_ONE * first + (1.0 - BETA_ONE) * grad
    second = BETA_TWO * second + (1.0 - BETA_TWO) * grad * grad
    update = first / corr_one / (jnp.sqrt(second / corr_two) + ADAM_EPS)
    return (weight - LEARN_RATE * (update + decay * weight), first, second)


def dot(left, right, left_dim, right_dim):
    return lax.dot_general(
        left, right, (((left_dim,), (right_dim,)), ((), ())), preferred_element_type=F32
    )


class Links:
    def __init__(self):
        self.dp_size = lax.axis_size("dp")
        self.mp_size = lax.axis_size("mp")
        self.bits = self.dp_size.bit_length() - 1
        self.dp = lax.axis_index("dp")
        self.mp = lax.axis_index("mp")

    def core(self, array):
        return lax.ppermute(array, "mp", [(i, i ^ 1) for i in range(self.mp_size)])

    def half(self, array):
        return lax.ppermute(array, "mp", [(i, i ^ 2) for i in range(self.mp_size)])

    def data(self, array, bit):
        return lax.ppermute(array, "dp", [(i, i ^ (1 << bit)) for i in range(self.dp_size)])

    def bit(self, bit):
        return (self.dp >> bit) & 1

    def sum_all(self, array):
        array = array + self.core(array)
        array = array + self.half(array)
        return self.sum_data(array)

    def sum_data(self, array):
        for bit in range(self.bits):
            array = array + self.data(array, bit)
        return array


def hold(value, *after):
    return lax.optimization_barrier((value, *after))[0]


def quarter_of(links, weight, axis):
    rows = weight.shape[axis] // 4
    return lax.dynamic_slice_in_dim(weight, (links.dp & 3) * rows, rows, axis)


def quarter_spots(links):
    return jnp.stack([(links.dp & 3) ^ change for change in range(4)])


class Reduction:
    def __init__(self, links, grad):
        self.links = links
        self.left = list(range(links.bits - 1, -1, -1))
        self.array = grad.reshape((2,) * links.bits + (grad.shape[0] >> links.bits, grad.shape[1]))

    def send(self, step):
        if step == "half":
            own = self.array.shape[-1] // 2
            self.kept = self.array[..., :own]
            return self.array[..., own:]
        axis = self.left.index(step)
        self.left.remove(step)
        mine = self.links.bit(step)
        self.kept = lax.dynamic_index_in_dim(self.array, mine, axis, keepdims=False)
        return lax.dynamic_index_in_dim(self.array, 1 - mine, axis, keepdims=False)

    def take(self, arrived):
        self.array = self.kept + arrived

    def step(self, step, *after):
        sent = self.send(step)
        sent = hold(sent, *after) if after else sent
        self.take(self.links.half(sent) if step == "half" else self.links.data(sent, step))


def vmem_specs(count):
    return [pl.BlockSpec(memory_space=pltpu.VMEM)] * count


def smem_specs(count):
    return [pl.BlockSpec(memory_space=pltpu.SMEM)] * count


def cost(flops, bytes_accessed, transcendentals=0):
    return pl.CostEstimate(
        flops=int(flops), bytes_accessed=int(bytes_accessed), transcendentals=int(transcendentals)
    )


def normed(values, axis):
    scale = 1.0 / values.shape[axis]
    center = values - jnp.sum(values, axis=axis, keepdims=True) * scale
    spread = jnp.sum(center * center, axis=axis, keepdims=True) * scale
    factor = lax.rsqrt(spread + NORM_EPS)
    return center * factor, factor


def normed_back(grad_hat, hat, factor, axis):
    scale = 1.0 / hat.shape[axis]
    mean = jnp.sum(grad_hat, axis=axis, keepdims=True) * scale
    along = jnp.sum(grad_hat * hat, axis=axis, keepdims=True) * scale
    return factor * (grad_hat - mean - hat * along)


def fold_rows(values):
    return jnp.sum(values.reshape(values.shape[0] // 8, 8, values.shape[1]), axis=0)


def fold_lanes(values):
    total = values[:, :LANES]
    for start in range(LANES, values.shape[1], LANES):
        total = total + values[:, start : start + LANES]
    return total


def column(row, count):
    return jnp.transpose(jnp.broadcast_to(row, (count, row.shape[1])))


def plan_kernel(window, half_ref, seg_ref, keep_ref, plan_ref, qseg_ref, kcode_ref, kept_ref):
    seq_len = seg_ref.shape[1]
    seg = seg_ref[...]
    half = half_ref[0]
    places = lax.broadcasted_iota(jnp.int32, (1, seq_len), 1)
    starts = (seg != pltpu.roll(seg, 1, 1)) & (places > 0)
    ranking = jnp.where(starts, jnp.abs(places - seq_len // 2) * (4 * seq_len) + places, 1 << 30)
    parting = lax.rem(jnp.min(ranking), 4 * seq_len)
    start = pl.multiple_of(half * (seq_len - window), LANES)
    low_valid = jnp.where(half == 0, 0, parting - start)
    high_valid = jnp.where(half == 0, parting, window)
    seg_win = seg_ref[:, pl.ds(start, window)]
    keep_win = keep_ref[:, pl.ds(start, window)]
    spots = lax.broadcasted_iota(jnp.int32, (1, window), 1)
    valid = (spots >= low_valid) & (spots < high_valid)
    qseg_ref[...] = jnp.broadcast_to(seg_win, (8, window))
    kcode_ref[...] = column(jnp.where(keep_win == 1, seg_win, -1), LANES)
    kept_ref[...] = column(jnp.where(valid & (keep_win == 1), 1.0, 0.0), LANES)
    segs = jnp.broadcast_to(seg_win, (8, window))
    lanes = lax.broadcasted_iota(jnp.int32, (8, window), 1)
    block = lax.broadcasted_iota(jnp.int32, (8, window), 0) * BLOCK

    def total(values):
        return jnp.sum(values, axis=1, keepdims=True)

    first_seg = total(jnp.where(lanes == block, segs, 0))
    last_seg = total(jnp.where(lanes == block + (BLOCK - 1), segs, 0))
    low = total(jnp.where(segs < first_seg, 1, 0))
    high = total(jnp.where(segs <= last_seg, 1, 0))
    block_first = block[:, :1]
    low = jnp.maximum(low, low_valid)
    high = jnp.minimum(high, high_valid) + (BLOCK - 1)
    shift = BLOCK.bit_length() - 1
    low, high = low >> shift, high >> shift
    live = (block_first < high_valid) & (block_first + BLOCK > low_valid)
    high = jnp.where(live, high, low)
    lane = lax.broadcasted_iota(jnp.int32, (8, LANES), 1)
    plan = jnp.where(lane == 0, low, jnp.where(lane == 1, high, parting))
    plan_ref[...] = plan


def make_plan(links, seg_row, keep_row, window):
    half = jnp.full((1,), links.mp // 2, jnp.int32)
    return pl.pallas_call(
        functools.partial(plan_kernel, window),
        out_shape=(
            jax.ShapeDtypeStruct((8, LANES), jnp.int32),
            jax.ShapeDtypeStruct((8, window), jnp.int32),
            jax.ShapeDtypeStruct((window, LANES), jnp.int32),
            jax.ShapeDtypeStruct((window, LANES), F32),
        ),
        in_specs=smem_specs(1) + vmem_specs(2),
        out_specs=tuple(vmem_specs(4)),
        compiler_params=pltpu.CompilerParams(vmem_limit_bytes=6 << 20),
        cost_estimate=cost(0, window * 1100),
        name="plan_window",
    )(half, seg_row, keep_row)


def allowed_block(kcode_ref, qseg_ref, key_start, query_start):
    codes = kcode_ref[pl.ds(key_start, BLOCK), :]
    codes = jnp.concatenate([codes] * (BLOCK // LANES), axis=1)
    segs = qseg_ref[0:1, pl.ds(query_start, BLOCK)]
    rows = lax.broadcasted_iota(jnp.int32, (BLOCK, BLOCK), 0)
    cols = lax.broadcasted_iota(jnp.int32, (BLOCK, BLOCK), 1)
    return (codes == segs) | (rows - cols == query_start - key_start)


def project_heads(heads, dim, weight, a_ref, params_ref, qkv_refs, hat_refs, factor_ref):
    tokens = a_ref.shape[0]
    group = heads * dim

    def block(tb, carry):
        ts = pl.multiple_of(tb * BLOCK, BLOCK)
        here = pl.ds(ts, BLOCK)
        rows = a_ref[here, :]
        for which in range(3):
            raw = dot(weight[which][...], rows, 1, 1) + params_ref[:, which : which + 1]
            if which == 2:
                qkv_refs[2][:, here] = raw.astype(BF16)
                continue
            hat, factor = normed(raw.reshape(heads, dim, BLOCK), 1)
            hat = hat.reshape(group, BLOCK)
            gained = hat * params_ref[:, 3 + which : 4 + which]
            if which == 0:
                gained = gained * dim ** (-0.5)
            qkv_refs[which][:, here] = gained.astype(BF16)
            hat_refs[which][:, here] = hat.astype(BF16)
            for head in range(heads):
                spot = (which * heads + head) * 8
                factor_ref[pl.ds(spot, 8), here] = jnp.broadcast_to(factor[head], (8, BLOCK))
        return carry

    lax.fori_loop(0, tokens // BLOCK, block, 0)


def attend(heads, dim, plan_ref, q_ref, k_ref, v_ref, kcode_ref, qseg_ref, o_ref, inv_ref, acc, tot):
    tokens = q_ref.shape[1]

    def query_block(qb, carry):
        qs = pl.multiple_of(qb * BLOCK, BLOCK)
        acc[...] = jnp.zeros_like(acc)
        tot[...] = jnp.zeros_like(tot)

        def key_block(kb, carry):
            ks = pl.multiple_of(kb * BLOCK, BLOCK)
            allowed = allowed_block(kcode_ref, qseg_ref, ks, qs)
            lines = [pl.ds(head * dim, dim) for head in range(heads)]
            scores = [dot(k_ref[rows, pl.ds(ks, BLOCK)], q_ref[rows, pl.ds(qs, BLOCK)], 0, 0) for rows in lines]
            expos = [jnp.where(allowed, jnp.exp(score), 0.0) for score in scores]
            more = [dot(v_ref[rows, pl.ds(ks, BLOCK)], expo.astype(BF16), 1, 0) for rows, expo in zip(lines, expos)]
            for head, rows in enumerate(lines):
                tot[pl.ds(head * 8, 8), :] += fold_rows(expos[head])
                acc[rows, :] += more[head]
            return carry

        lax.fori_loop(plan_ref[qb, 0], plan_ref[qb, 1], key_block, 0)
        for head in range(heads):
            rows = pl.ds(head * dim, dim)
            total = jnp.sum(tot[pl.ds(head * 8, 8), :], axis=0, keepdims=True)
            inverse = jnp.where(total > 0.0, 1.0 / total, 0.0)
            o_ref[rows, pl.ds(qs, BLOCK)] = (acc[rows, :] * inverse).astype(BF16)
            inv_ref[pl.ds(head * 8, 8), pl.ds(qs, BLOCK)] = jnp.broadcast_to(inverse, (8, BLOCK))
        return carry

    lax.fori_loop(0, tokens // BLOCK, query_block, 0)


def own_heads_kernel(
    heads, dim, x_ref, vec_ref, weight_ref, params_ref,
    a_ref, q_ref, k_ref, v_ref, qh_ref, kh_ref, factor_ref, weight,
):
    weight[...] = weight_ref[...].astype(BF16)
    tokens = x_ref.shape[0]

    def norm_block(tb, carry):
        here = pl.ds(pl.multiple_of(tb * BLOCK, BLOCK), BLOCK)
        hat, _ = normed(x_ref[here, :].astype(F32), 1)
        a_ref[here, :] = (hat * vec_ref[0:1, :] + vec_ref[1:2, :]).astype(BF16)
        return carry

    lax.fori_loop(0, tokens // BLOCK, norm_block, 0)
    project_heads(
        heads, dim, [weight.at[k] for k in range(3)], a_ref, params_ref, (q_ref, k_ref, v_ref),
        (qh_ref, kh_ref), factor_ref,
    )


def other_heads_kernel(
    heads, dim, spots_ref, a_ref, own_ref, p0, p1, p2, p3, params_ref,
    q_ref, k_ref, v_ref, qh_ref, kh_ref, factor_ref, qk_ref, value_ref,
):
    group = heads * dim
    places = [
        (qk_ref.at[pl.ds(0, group)], qk_ref.at[pl.ds(2 * group, group)]),
        (qk_ref.at[pl.ds(group, group)], qk_ref.at[pl.ds(3 * group, group)]),
        (value_ref.at[pl.ds(0, group)], value_ref.at[pl.ds(group, group)]),
    ]
    for which, (own_place, place) in enumerate(places):
        own_place[...] = own_ref[which].astype(BF16)
        for index, piece in enumerate((p0, p1, p2, p3)):
            count = piece.shape[1]
            spot = pl.multiple_of(spots_ref[index] * count, 16)
            place[pl.ds(spot, count), :] = piece[which].astype(BF16)
    project_heads(
        heads, dim, [place for _, place in places], a_ref, params_ref, (q_ref, k_ref, v_ref), (qh_ref, kh_ref), factor_ref
    )


def attention_kernel(
    heads, dim, plan_ref, q_ref, k_ref, v_ref, kcode_ref, qseg_ref, o_ref, inv_ref, acc, tot
):
    attend(heads, dim, plan_ref, q_ref, k_ref, v_ref, kcode_ref, qseg_ref, o_ref, inv_ref, acc, tot)


def out_kernel(o_own_ref, o_other_ref, own_ref, other_ref, part_ref, weight, o_cat):
    group = own_ref.shape[0]

    @pl.when(pl.program_id(0) == 0)
    def _():
        weight[pl.ds(0, group), :] = own_ref[...].astype(BF16)
        weight[pl.ds(group, group), :] = other_ref[...].astype(BF16)

    o_cat[pl.ds(0, group), :] = o_own_ref[...]
    o_cat[pl.ds(group, group), :] = o_other_ref[...]
    part_ref[...] = dot(o_cat[...], weight[...], 0, 0)


def head_shapes(group, heads, tokens):
    narrow = jax.ShapeDtypeStruct((group, tokens), BF16)
    return [*(narrow,) * 5, jax.ShapeDtypeStruct((heads * 16, tokens), F32)]


def o_shapes(group, heads, tokens):
    return [
        jax.ShapeDtypeStruct((group, tokens), BF16),
        jax.ShapeDtypeStruct((heads * 8, tokens), F32),
    ]


def own_heads(x_win, vec_params, weight, params, heads, dim):
    tokens, width = x_win.shape
    group = heads * dim
    return pl.pallas_call(
        functools.partial(own_heads_kernel, heads, dim),
        out_shape=[
            jax.ShapeDtypeStruct((tokens, width), BF16),
            *head_shapes(group, heads, tokens),
        ],
        in_specs=vmem_specs(4),
        out_specs=vmem_specs(7),
        scratch_shapes=[pltpu.VMEM((3, group, width), BF16)],
        cost_estimate=cost(tokens * width * group * 6, tokens * width * 8),
        name="heads_own",
    )(x_win, vec_params, weight, params)


def other_heads(spots, a_first, own_weight, pieces, params, heads, dim):
    tokens, width = a_first.shape
    group = heads * dim
    return pl.pallas_call(
        functools.partial(other_heads_kernel, heads, dim),
        out_shape=[
            *head_shapes(group, heads, tokens),
            jax.ShapeDtypeStruct((4 * group, width), BF16),
            jax.ShapeDtypeStruct((2 * group, width), BF16),
        ],
        in_specs=smem_specs(1) + vmem_specs(7),
        out_specs=vmem_specs(8),
        cost_estimate=cost(tokens * width * group * 6, tokens * width * 8),
        name="heads_other",
    )(spots, a_first, own_weight, *pieces, params)


def attention(plan, query, key, value, kcode, qseg, heads, dim):
    group, tokens = query.shape
    pairs = heads * tokens * 3 * BLOCK
    return pl.pallas_call(
        functools.partial(attention_kernel, heads, dim),
        out_shape=o_shapes(group, heads, tokens),
        in_specs=smem_specs(1) + vmem_specs(5),
        out_specs=vmem_specs(2),
        scratch_shapes=[pltpu.VMEM((group, BLOCK), F32), pltpu.VMEM((heads * 8, BLOCK), F32)],
        cost_estimate=cost(pairs * dim * 4, group * tokens * 8, pairs),
        name="attention",
    )(plan, query, key, value, kcode, qseg)


def out_project(o_own, o_other, out_own, out_other):
    group, tokens = o_own.shape
    width = out_own.shape[1]
    cols = pl.BlockSpec((group, BLOCK), lambda i: (0, i))
    return pl.pallas_call(
        out_kernel,
        grid=(tokens // BLOCK,),
        out_shape=jax.ShapeDtypeStruct((tokens, width), F32),
        in_specs=[cols, cols, whole_spec(out_own.shape), whole_spec(out_other.shape)],
        out_specs=rows_spec(width),
        scratch_shapes=[
            pltpu.VMEM((2 * group, width), BF16),
            pltpu.VMEM((2 * group, BLOCK), BF16),
        ],
        compiler_params=pltpu.CompilerParams(vmem_limit_bytes=12 << 20),
        cost_estimate=cost(tokens * width * group * 4, tokens * width * 6),
        name="out_project",
    )(o_own, o_other, out_own, out_other)


def attention_back_kernel(
    heads, dim, plan_ref, q_ref, k_ref, v_ref, qh_ref, kh_ref, factor_ref, o_ref, inv_ref, do_ref,
    params_ref, kcode_ref, qseg_ref, *rest,
):
    draw_qk_ref, draw_v_ref = rest[-7:-5]
    out_sums_ref, dq_ref, dk_ref, dv_ref, sums_ref = rest[-5:]
    group, tokens = q_ref.shape
    for ref in (dq_ref, dk_ref, dv_ref, sums_ref):
        ref[...] = jnp.zeros_like(ref)

    def query_block(qb, carry):
        qs = pl.multiple_of(qb * BLOCK, BLOCK)
        here = pl.ds(qs, BLOCK)
        deltas = []
        inverses = []
        for head in range(heads):
            rows = pl.ds(head * dim, dim)
            products = do_ref[rows, here].astype(F32) * o_ref[rows, here].astype(F32)
            deltas.append(jnp.sum(products, axis=0, keepdims=True))
            inverses.append(inv_ref[pl.ds(head * 8, 1), here])

        def key_block(kb, carry):
            ks = pl.multiple_of(kb * BLOCK, BLOCK)
            there = pl.ds(ks, BLOCK)
            allowed = allowed_block(kcode_ref, qseg_ref, ks, qs)
            lines = [pl.ds(head * dim, dim) for head in range(heads)]
            keys = [k_ref[rows, there] for rows in lines]
            queries = [q_ref[rows, here] for rows in lines]
            grads = [do_ref[rows, here] for rows in lines]
            scores = [dot(key, query, 0, 0) for key, query in zip(keys, queries)]
            grad_probs = [dot(v_ref[rows, there], grad, 0, 0) for rows, grad in zip(lines, grads)]
            added = []
            for head in range(heads):
                probs = jnp.where(allowed, jnp.exp(scores[head]), 0.0) * inverses[head]
                grad_scores = (probs * (grad_probs[head] - deltas[head])).astype(BF16)
                added.append((
                    dot(grads[head], probs.astype(BF16), 1, 1),
                    dot(queries[head], grad_scores, 1, 1),
                    dot(keys[head], grad_scores, 1, 0),
                ))
            for rows, (more_v, more_k, more_q) in zip(lines, added):
                dv_ref[rows, there] += more_v
                dk_ref[rows, there] += more_k
                dq_ref[rows, here] += more_q
            return carry

        lax.fori_loop(plan_ref[qb, 0], plan_ref[qb, 1], key_block, 0)
        return carry

    lax.fori_loop(0, tokens // BLOCK, query_block, 0)

    def token_block(tb, carry):
        here = pl.ds(pl.multiple_of(tb * BLOCK, BLOCK), BLOCK)
        for which, (grad_ref, hat_ref) in enumerate(((dq_ref, qh_ref), (dk_ref, kh_ref), (dv_ref, None))):
            rows = pl.ds(which * group, group)
            grad = grad_ref[:, here]
            if hat_ref is not None:
                if which == 0:
                    grad = grad * dim ** (-0.5)
                hat = hat_ref[:, here].astype(F32)
                sums_ref[pl.ds((3 + which) * group, group), :] += fold_lanes(grad * hat)
                grad = grad * params_ref[:, 3 + which : 4 + which]
                parts = []
                for head in range(heads):
                    lines = slice(head * dim, (head + 1) * dim)
                    factor = factor_ref[pl.ds((which * heads + head) * 8, 1), here]
                    parts.append(normed_back(grad[lines], hat[lines], factor, 0))
                grad = jnp.concatenate(parts, axis=0)
            rounded = grad.astype(BF16)
            if which < 2:
                draw_qk_ref[rows, here] = rounded
            else:
                draw_v_ref[:, here] = rounded
            sums_ref[rows, :] += fold_lanes(rounded.astype(F32))
        return carry

    lax.fori_loop(0, tokens // BLOCK, token_block, 0)
    out_sums_ref[...] = jnp.sum(jnp.transpose(sums_ref[...]), axis=0, keepdims=True)


def attention_back(plan, saved, grad_o, params, kcode, qseg, heads, dim, draws=None):
    group, tokens = saved[0].shape
    pairs = heads * tokens * 3 * BLOCK
    which = 0 if draws is None else 1
    sums = -(-5 * group // LANES) * LANES
    inputs = [*saved, grad_o, params, kcode, qseg]
    in_specs = smem_specs(1) + [whole_spec(x.shape) for x in inputs]
    aliases = {}
    if draws is not None:
        aliases = {1 + len(inputs) + k: k for k in range(2)}
        inputs += draws
        in_specs += [pl.BlockSpec(memory_space=pl.ANY)] * 2
    return pl.pallas_call(
        functools.partial(attention_back_kernel, heads, dim),
        grid=(1,),
        out_shape=[
            jax.ShapeDtypeStruct((4 * group, tokens), BF16),
            jax.ShapeDtypeStruct((2 * group, tokens), BF16),
            jax.ShapeDtypeStruct((1, sums), F32),
        ],
        in_specs=in_specs,
        out_specs=[
            pl.BlockSpec((2 * group, tokens), lambda i: (which, 0)),
            pl.BlockSpec((group, tokens), lambda i: (which, 0)),
            whole_spec((1, sums)),
        ],
        scratch_shapes=[
            *(pltpu.VMEM((group, tokens), F32),) * 3,
            pltpu.VMEM((sums, LANES), F32),
        ],
        input_output_aliases=aliases,
        compiler_params=pltpu.CompilerParams(vmem_limit_bytes=16 << 20),
        cost_estimate=cost(pairs * dim * 10, group * tokens * 30, pairs),
        name="attention_back",
    )(plan, *inputs)


ERFC_TERMS = (
    0.16918800576031592, 0.17071521752915575, 0.14833923939584578, 0.2149257797248009,
    -0.09465005158893602, 0.5477190245253036, -0.5122771874066157, 0.4855627631921905,
    -0.1295228107166713,
)


def gelu_and_slope(values):
    t = 1.0 / (1.0 + (0.3 * 0.5**0.5) * jnp.abs(values))
    poly = ERFC_TERMS[-1]
    for term in ERFC_TERMS[-2::-1]:
        poly = poly * t + term
    bell = jnp.exp(values * values * -0.5)
    low_tail = 0.5 * (t * poly) * bell
    below = jnp.where(values > 0.0, 1.0 - low_tail, low_tail)
    return values * below, below + values * bell * 0.3989422804014327


def mlp_half(a, dmlp, up, down, bias):
    upper = dot(a, up, 1, 0) + bias
    gated, slope = gelu_and_slope(upper)
    gated = gated.astype(BF16)
    grad_gated = dot(dmlp, down, 1, 1)
    grad_upper = (grad_gated * slope).astype(BF16)
    return gated, grad_upper, dot(gated, down, 1, 0), dot(grad_upper, up, 1, 1)


def own_mlp_kernel(
    x_ref, mine_ref, peer_ref, cot_ref, kept_ref, vec_ref, up_ref, down_ref, bias_ref,
    hidden_ref, a_ref, dmlp_ref, g_ref, du_ref, mlp_ref, da_ref, bias_out, attn_out, up, down, bias_sums, attn_sums,
):
    @pl.when(pl.program_id(0) == 0)
    def _():
        up[...] = up_ref[...].astype(BF16)
        down[...] = down_ref[...].astype(BF16)
        bias_sums[...] = jnp.zeros_like(bias_sums)
        attn_sums[...] = jnp.zeros_like(attn_sums)

    kept = kept_ref[:, 0:1]
    attn = mine_ref[...] + peer_ref[...] + vec_ref[4:5, :]
    attn_sums[...] += fold_rows(kept * attn * attn)
    hidden = x_ref[...].astype(F32) + attn
    hidden_ref[...] = hidden
    hat, _ = normed(hidden, 1)
    a = (hat * vec_ref[2:3, :] + vec_ref[3:4, :]).astype(BF16)
    a_ref[...] = a
    dmlp = (cot_ref[...].astype(F32) * kept).astype(BF16)
    dmlp_ref[...] = dmlp
    gated, grad_upper, mlp, da = mlp_half(a, dmlp, up[...], down[...], bias_ref[...])
    g_ref[...] = gated
    du_ref[...] = grad_upper
    mlp_ref[...] = mlp
    da_ref[...] = da
    bias_sums[...] += fold_rows(grad_upper.astype(F32))

    @pl.when(pl.program_id(0) == pl.num_programs(0) - 1)
    def _():
        bias_out[...] = jnp.sum(bias_sums[...], axis=0, keepdims=True)
        attn_out[...] = jnp.sum(attn_sums[...], axis=0, keepdims=True)


def other_mlp_kernel(
    spots_ref, a_ref, dmlp_ref, mlp_in_ref, da_in_ref, base, near_a, near_b, far_a, far_b, bias_ref,
    g_ref, du_ref, mlp_ref, da_left_ref, da_right_ref, bias_out, up, down, bias_sums,
):
    @pl.when(pl.program_id(0) == 0)
    def _():
        count = near_a.shape[1]
        for change, first, second in (
            (0, base.at[:, pl.ds(0, count)], base.at[:, pl.ds(count, count)]),
            (1, near_a, far_b.at[0]),
            (2, far_a.at[0], near_b),
            (3, far_a.at[1], far_b.at[1]),
        ):
            for which, piece in enumerate((first, second)):
                spot = pl.multiple_of((spots_ref[change] * 2 + which) * count, 16)
                up[pl.ds(spot, count), :] = piece[0].astype(BF16)
                down[pl.ds(spot, count), :] = piece[1].astype(BF16)
        bias_sums[...] = jnp.zeros_like(bias_sums)

    gated, grad_upper, mlp, da = mlp_half(
        a_ref[...], dmlp_ref[...], up[...], down[...], bias_ref[...]
    )
    g_ref[...] = gated
    du_ref[...] = grad_upper
    mlp_ref[...] = mlp_in_ref[...] + mlp
    da = da_in_ref[...] + da
    cut = da_left_ref.shape[1]
    da_left_ref[...], da_right_ref[...] = da[:, :cut], da[:, cut:]
    bias_sums[...] += fold_rows(grad_upper.astype(F32))

    @pl.when(pl.program_id(0) == pl.num_programs(0) - 1)
    def _():
        bias_out[...] = jnp.sum(bias_sums[...], axis=0, keepdims=True)


def rows_spec(width):
    return pl.BlockSpec((BLOCK, width), lambda i: (i, 0))


def whole_spec(shape):
    return pl.BlockSpec(shape, lambda *_: (0,) * len(shape), pipeline_mode=pl.Buffered(1))


def sums_spec(rows, width):
    return pl.BlockSpec((rows, width), lambda *_: (0, 0))


def own_mlp(x_win, mine, peer, cot, kept, vec_params, up_weight, down_weight, bias):
    tokens, width = x_win.shape
    units = up_weight.shape[1]
    wide = rows_spec(width)
    struct = jax.ShapeDtypeStruct
    return pl.pallas_call(
        own_mlp_kernel,
        grid=(tokens // BLOCK,),
        out_shape=[
            struct((tokens, width), F32),
            struct((tokens, width), BF16),
            struct((tokens, width), BF16),
            struct((tokens, units), BF16),
            struct((tokens, units), BF16),
            struct((tokens, width), F32),
            struct((tokens, width), F32),
            struct((1, units), F32),
            struct((1, width), F32),
        ],
        in_specs=[
            wide, wide, wide, wide, rows_spec(LANES), whole_spec(vec_params.shape),
            whole_spec(up_weight.shape), whole_spec(down_weight.shape), whole_spec(bias.shape),
        ],
        out_specs=[
            wide, wide, wide, rows_spec(units), rows_spec(units), wide, wide,
            sums_spec(1, units), sums_spec(1, width),
        ],
        scratch_shapes=[
            pltpu.VMEM(up_weight.shape, BF16),
            pltpu.VMEM(down_weight.shape, BF16),
            pltpu.VMEM((8, units), F32),
            pltpu.VMEM((8, width), F32),
        ],
        cost_estimate=cost(8 * tokens * width * units, tokens * width * 40, tokens * units * 2),
        name="mlp_own",
    )(x_win, mine, peer, cot, kept, vec_params, up_weight, down_weight, bias)


def other_mlp(spots, a_second, dmlp, mlp_part, da_part, pieces, bias):
    tokens, width = a_second.shape
    units = bias.shape[1]
    wide = rows_spec(width)
    struct = jax.ShapeDtypeStruct
    return pl.pallas_call(
        other_mlp_kernel,
        grid=(tokens // BLOCK,),
        out_shape=[
            struct((tokens, units), BF16),
            struct((tokens, units), BF16),
            struct((tokens, width), F32),
            struct((tokens, width // 2), F32),
            struct((tokens, width // 2), F32),
            struct((1, units), F32),
        ],
        in_specs=[
            *smem_specs(1), wide, wide, wide, wide,
            *(whole_spec(piece.shape) for piece in pieces), whole_spec(bias.shape),
        ],
        out_specs=[
            rows_spec(units), rows_spec(units), wide, *(rows_spec(width // 2),) * 2, sums_spec(1, units),
        ],
        input_output_aliases={3: 2},
        scratch_shapes=[
            pltpu.VMEM((width, units), BF16),
            pltpu.VMEM((units, width), BF16),
            pltpu.VMEM((8, units), F32),
        ],
        cost_estimate=cost(8 * tokens * width * units, tokens * width * 28, tokens * units * 2),
        name="mlp_other",
    )(spots, a_second, dmlp, mlp_part, da_part, *pieces, bias)


def hidden_back_kernel(
    group, hidden_ref, mine_left, mine_right, peer_left, peer_right, cot_ref, kept_ref, vec_ref, out_own_ref, out_other_ref,
    dh_ref, dattn_ref, do_own_ref, do_other_ref, sums_out, out_weight, sums_ref,
):
    @pl.when(pl.program_id(0) == 0)
    def _():
        out_weight[pl.ds(0, group), :] = out_own_ref[...].astype(BF16)
        out_weight[pl.ds(group, group), :] = out_other_ref[...].astype(BF16)
        sums_ref[...] = jnp.zeros_like(sums_ref)

    hat, factor = normed(hidden_ref[...], 1)
    da = jnp.concatenate(
        [mine_left[...] + peer_left[...], mine_right[...] + peer_right[...]], axis=1
    )
    dy = cot_ref[...].astype(F32) * kept_ref[:, 0:1]
    dh = dy + normed_back(da * vec_ref[2:3, :], hat, factor, 1)
    dh_ref[...] = dh
    dattn = dh.astype(BF16)
    dattn_ref[...] = dattn
    grads = dot(out_weight[...], dattn, 1, 1).astype(BF16)
    do_own_ref[...] = grads[:group]
    do_other_ref[...] = grads[group:]
    sums_ref[0:8, :] += fold_rows(da * hat)
    sums_ref[8:16, :] += fold_rows(da)
    sums_ref[16:24, :] += fold_rows(dattn.astype(F32))
    sums_ref[24:32, :] += fold_rows(dy.astype(BF16).astype(F32))

    @pl.when(pl.program_id(0) == pl.num_programs(0) - 1)
    def _():
        for row in range(4):
            total = jnp.sum(sums_ref[8 * row : 8 * row + 8, :], axis=0, keepdims=True)
            sums_out[row : row + 1, :] = total


def hidden_back(hidden, mine, peer, cot, kept, vec_params, out_own, out_other):
    tokens, width = hidden.shape
    group = out_own.shape[0]
    wide = rows_spec(width)
    cols = pl.BlockSpec((group, BLOCK), lambda i: (0, i))
    struct = jax.ShapeDtypeStruct
    return pl.pallas_call(
        functools.partial(hidden_back_kernel, group),
        grid=(tokens // BLOCK,),
        out_shape=[
            struct((tokens, width), F32),
            struct((tokens, width), BF16),
            struct((group, tokens), BF16),
            struct((group, tokens), BF16),
            struct((4, width), F32),
        ],
        in_specs=[
            wide, *(rows_spec(width // 2),) * 4, wide, rows_spec(LANES), whole_spec(vec_params.shape),
            whole_spec(out_own.shape), whole_spec(out_other.shape),
        ],
        out_specs=[wide, wide, cols, cols, sums_spec(4, width)],
        scratch_shapes=[pltpu.VMEM((2 * group, width), BF16), pltpu.VMEM((32, width), F32)],
        compiler_params=pltpu.CompilerParams(vmem_limit_bytes=22 << 20),
        cost_estimate=cost(4 * tokens * width * group, tokens * width * 22),
        name="hidden_back",
    )(hidden, *mine, *peer, cot, kept, vec_params, out_own, out_other)


def input_back_kernel(
    core_ref, mine_ref, peer_ref, x_ref, dh_ref, vec_ref, left_ref, right_ref, sums_out, sums_ref
):
    @pl.when(pl.program_id(0) == 0)
    def _():
        sums_ref[...] = jnp.zeros_like(sums_ref)

    hat, factor = normed(x_ref[...].astype(F32), 1)
    da = mine_ref[...] + peer_ref[...]
    out = dh_ref[...] + normed_back(da * vec_ref[0:1, :], hat, factor, 1)
    cut = left_ref.shape[1]
    left_ref[...], right_ref[...] = out[:, :cut], out[:, cut:]
    sums_ref[0:8, :] += fold_rows(da * hat)
    sums_ref[8:16, :] += fold_rows(da)

    @pl.when(pl.program_id(0) == pl.num_programs(0) - 1)
    def _():
        for row in range(2):
            total = jnp.sum(sums_ref[8 * row : 8 * row + 8, :], axis=0, keepdims=True)
            sums_out[row : row + 1, :] = total


def input_back(core, mine, peer, x_win, dh, vec_params):
    half_rows, width = peer.shape
    step = LANES
    count = half_rows // step
    near = pl.BlockSpec((step, width), lambda i, core_ref: (i, 0))
    left = pl.BlockSpec((step, width // 2), lambda i, core_ref: (i, 0))
    window = pl.BlockSpec((step, width), lambda i, core_ref: (core_ref[0] * count + i, 0))
    struct = jax.ShapeDtypeStruct
    return pl.pallas_call(
        input_back_kernel,
        grid_spec=pltpu.PrefetchScalarGridSpec(
            num_scalar_prefetch=1,
            grid=(count,),
            in_specs=[window, near, window, window, whole_spec(vec_params.shape)],
            out_specs=[left, left, sums_spec(2, width)],
            scratch_shapes=[pltpu.VMEM((16, width), F32)],
        ),
        out_shape=[
            struct((half_rows, width // 2), F32),
            struct((half_rows, width // 2), F32),
            struct((2, width), F32),
        ],
        cost_estimate=cost(0, half_rows * width * 18),
        name="input_back",
    )(core, mine, peer, x_win, dh, vec_params)


def last_gradients_kernel(
    group, a_ref, dattn_ref, qk_ref, v_ref, o_own_ref, o_other_ref, qk_own_out, qk_other_out, vo_out
):
    a, dattn = a_ref[...], dattn_ref[...]
    query_key = jnp.transpose(dot(qk_ref[...], a, 1, 0))
    qk_own_out[...] = query_key[:, : 2 * group]
    qk_other_out[...] = query_key[:, 2 * group :]
    value = dot(v_ref[...], a, 1, 0)
    own, other = dot(o_own_ref[...], dattn, 1, 0), dot(o_other_ref[...], dattn, 1, 0)
    rows = jnp.concatenate([value[:group], own, value[group:], other], axis=0)
    vo_out[...] = jnp.transpose(rows)


def last_gradients(a_first, dattn, draw_qk, draw_v, o_own, o_other):
    tokens, width = a_first.shape
    group = o_own.shape[0]
    cols = pl.BlockSpec((tokens, BLOCK), lambda i: (0, i))
    narrow, wide = rows_spec(2 * group), rows_spec(4 * group)
    struct = jax.ShapeDtypeStruct
    inputs = (draw_qk, draw_v, o_own, o_other)
    return pl.pallas_call(
        functools.partial(last_gradients_kernel, group),
        grid=(width // BLOCK,),
        out_shape=[
            struct((width, 2 * group), F32),
            struct((width, 2 * group), F32),
            struct((width, 4 * group), F32),
        ],
        in_specs=[cols, cols, *(whole_spec(x.shape) for x in inputs)],
        out_specs=[narrow, narrow, wide],
        compiler_params=pltpu.CompilerParams(vmem_limit_bytes=20 << 20),
        cost_estimate=cost(16 * tokens * width * group, tokens * width * 12),
        name="last_gradients",
    )(a_first, dattn, *inputs)


def pack_kernel(
    core_ref, first_ref, second_ref, kept_ref, attn_ref, mlp_ref,
    own_ref, other_ref, own_bias_ref, other_bias_ref, mine_ref, away_ref,
):
    width = mine_ref.shape[1]
    once = jnp.where(core_ref[0] == 0, 1.0, 0.0)
    count = jnp.sum(kept_ref[...]) * (once / kept_ref.shape[1])
    attn = jnp.sum(attn_ref[...]) * once
    lane = lax.broadcasted_iota(jnp.int32, (1, width), 1)
    stats = jnp.where(lane == 0, count, jnp.where(lane == 1, attn, jnp.where(lane == 2, mlp_ref[0], 0.0)))
    sums, units = own_ref.shape[1], own_bias_ref.shape[1]
    for ref, head, bias in ((mine_ref, own_ref, own_bias_ref), (away_ref, other_ref, other_bias_ref)):
        ref[...] = jnp.zeros_like(ref)
        ref[0:2, :] = first_ref[...]
        ref[2:6, :] = second_ref[...] * once
        ref[6:7, :] = stats
        row = 8
        for source, size in ((head, sums), (bias, units)):
            for start in range(0, size, width):
                length = min(width, size - start)
                ref[row : row + 1, :length] = source[:, start : start + length]
                row += 1


def pack_small(core, first, second, kept, attn, mlp_sq, own, other, own_bias, other_bias):
    width = first.shape[1]
    inputs = (first, second, kept, attn)
    more = (own, other, own_bias, other_bias)
    rows = 8 + -(-own.shape[1] // width) + -(-own_bias.shape[1] // width)
    struct = jax.ShapeDtypeStruct((-(-rows // 8) * 8, width), F32)
    return pl.pallas_call(
        pack_kernel,
        out_shape=[struct, struct],
        in_specs=smem_specs(1) + vmem_specs(4) + smem_specs(1) + vmem_specs(4),
        out_specs=vmem_specs(2),
        compiler_params=pltpu.CompilerParams(vmem_limit_bytes=6 << 20),
        cost_estimate=cost(0, kept.size * 4),
        name="pack_small",
    )(core, *inputs, mlp_sq, *more)


def update_kernel(decays, *refs):
    scalars, count = refs[0], len(decays)
    inputs, outputs = refs[1 : 1 + 4 * count], refs[1 + 4 * count :]
    factor, corr_one, corr_two = scalars[0], scalars[1], scalars[2]
    for index, decay in enumerate(decays):
        weight_ref, grad_ref, first_ref, second_ref = inputs[4 * index : 4 * index + 4]
        shape = weight_ref.shape
        if index == 0:
            size = shape[2]
            spots = [(k, grad_ref[:, k * size : (k + 1) * size]) for k in range(shape[0])]
        elif index == 1:
            spots = [(slice(None), jnp.transpose(grad_ref[:, grad_ref.shape[1] - shape[0] :]))]
        elif index == 2:
            spots = [(slice(None), grad_ref[:, grad_ref.shape[1] - shape[1] :])]
        elif index == 3:
            spots = [(slice(None), grad_ref[:, : shape[1]])]
        else:
            spots = [(slice(None), grad_ref[...])]
        for spot, grad in spots:
            results = adam_step(
                weight_ref[spot], grad, first_ref[spot], second_ref[spot], factor, corr_one, corr_two, decay
            )
            for ref, value in zip(outputs[3 * index : 3 * index + 3], results):
                ref[spot] = value


def update(scalars, groups, decays):
    inputs = [array for group in groups for array in group]
    shapes = [
        jax.ShapeDtypeStruct(group[0].shape, F32) for group in groups for _ in range(3)
    ]
    results = pl.pallas_call(
        functools.partial(update_kernel, decays),
        out_shape=shapes,
        in_specs=smem_specs(1) + vmem_specs(len(inputs)),
        out_specs=vmem_specs(len(shapes)),
        cost_estimate=cost(0, sum(28 * group[0].size for group in groups)),
        name="update",
    )(scalars, *inputs)
    return [results[3 * k : 3 * k + 3] for k in range(len(groups))]


def join_kernel(half_rows, window, pieces, info_ref, factor_ref, shift_ref, *refs):
    out_ref = refs[-1]
    seq_len = out_ref.shape[1]
    core, half, parting = info_ref[0], info_ref[1], info_ref[2]
    factor = factor_ref[0]
    step, small = LANES, LANES // 4
    offset = seq_len - window
    start = 0
    for piece in range(pieces):
        far_cols = refs[4 * piece + 2].shape[-1]
        cols = slice(start, start + far_cols)
        start += far_cols
        shift = shift_ref[:, cols]

        def view(ref, piece=piece, cols=cols):
            if len(ref.shape) == 3:
                return ref.at[piece]
            return ref if ref.shape[1] == cols.stop - cols.start else ref.at[:, cols]

        mine_ref, near_ref, far_ref, far_near_ref = (
            view(ref) for ref in refs[4 * piece : 4 * piece + 4]
        )

        def rows_of(which, row, step, views=(mine_ref, near_ref, far_ref, far_near_ref)):
            mine, near, far, far_near = views
            from_core = row // half_rows
            spot = pl.ds(pl.multiple_of(row - from_core * half_rows, step), step)
            same = core == from_core
            return jnp.where(
                half == which,
                jnp.where(same, mine[spot, :], near[spot, :]),
                jnp.where(same, far[spot, :], far_near[spot, :]),
            )

        def store(row, step, values, cols=cols, shift=shift):
            spot = pl.ds(pl.multiple_of(row, step), step)
            out_ref[0, spot, cols] = (values * factor + shift).astype(BF16)

        def first(block, carry, rows_of=rows_of, store=store):
            store(block * step, step, rows_of(0, block * step, step))
            return carry

        def middle(block, carry, rows_of=rows_of, store=store):
            row = block * small
            places = row + lax.broadcasted_iota(jnp.int32, (small, 1), 0)
            one, two = rows_of(0, row, small), rows_of(1, row - offset, small)
            store(row, small, jnp.where(places < parting, one, two))
            return carry

        def second(block, carry, rows_of=rows_of, store=store):
            store(block * step, step, rows_of(1, block * step - offset, step))
            return carry

        lax.fori_loop(0, offset // step, first, 0)
        lax.fori_loop(offset // small, window // small, middle, 0)
        lax.fori_loop(window // step, seq_len // step, second, 0)


def join_sequence(links, pieces, parting, seq_len, window, factor, shift):
    half_rows = pieces[0][0].shape[0]
    width = shift.shape[1]
    info = jnp.stack([links.mp % 2, links.mp // 2, parting]).astype(jnp.int32)
    arrays = [array for piece in pieces for array in piece]
    return pl.pallas_call(
        functools.partial(join_kernel, half_rows, window, len(pieces)),
        out_shape=jax.ShapeDtypeStruct((1, seq_len, width), BF16),
        in_specs=smem_specs(2) + vmem_specs(1 + len(arrays)),
        out_specs=pl.BlockSpec(memory_space=pltpu.VMEM),
        cost_estimate=cost(0, half_rows * width * 16 + seq_len * width * 2),
        name="join_sequence",
    )(info, factor, shift, *arrays)


def local(
    patches, cotangent, keep_mask, segment_ids, step_count,
    qkv_weight, qkv_first, qkv_second,
    out_weight, out_first, out_second,
    up_weight, up_first, up_second,
    down_weight, down_first, down_second,
    head_params, head_first, head_second,
    up_bias, upb_first, upb_second,
    vec_params, vec_first, vec_second,
):
    links = Links()
    seq_len, width = patches.shape[1:]
    heads, dim = head_params.shape[1:]
    group = heads * dim
    units = up_weight.shape[1]
    window = seq_len // 2 + SEG_BOUND // 2
    half_rows = window // 2
    core = links.mp % 2
    start = (links.mp // 2) * (seq_len - window)

    qkv_flip = jnp.swapaxes(qkv_weight, 1, 2)
    qkv_base = links.half(quarter_of(links, qkv_flip, 1))
    small = jnp.concatenate([head_params.reshape(-1), up_bias])
    small_other = links.half(small)
    head_other = small_other[: head_params.size].reshape(head_params.shape)

    def columns(params):
        return jnp.pad(params.reshape(params.shape[0], group).T, ((0, 0), (0, 3)))

    head_cols = columns(head_params)
    other_cols = columns(head_other)
    upb_own = up_bias.reshape(1, units)
    upb_other = small_other[head_params.size :].reshape(1, units)

    plan, qseg, kcode, kept = make_plan(links, segment_ids, keep_mask, window)
    parting = plan[0, 2]
    x_win = lax.dynamic_slice_in_dim(patches[0], start, window, 0)
    cot_win = lax.dynamic_slice_in_dim(cotangent[0], start, window, 0)
    a_first, *own = own_heads(x_win, vec_params, qkv_flip, head_cols, heads, dim)

    qkv_base = hold(qkv_base, own[0])
    qkv_pieces = [qkv_base, links.data(qkv_base, 0), links.data(qkv_base, 1)]
    both = [(i, i ^ 3) for i in range(links.dp_size)]
    qkv_pieces.append(lax.ppermute(qkv_base, "dp", both))
    spots = quarter_spots(links)
    up_early, down_early, _, _ = lax.optimization_barrier(
        (up_weight, down_weight, qkv_base, small_other)
    )
    mlp_base = links.half(quarter_of(links, jnp.stack([up_early, down_early]), 1))
    own += attention(plan, hold(own[0], qkv_base), own[1], own[2], kcode, qseg, heads, dim)

    qkv_pieces = list(lax.optimization_barrier((*qkv_pieces, own[6]))[:4])
    *other, qk_cat, value_cat = other_heads(
        spots, hold(a_first, cot_win), qkv_flip, qkv_pieces, other_cols, heads, dim
    )
    mlp_base = hold(mlp_base, other[0])
    out_other = links.half(hold(out_weight, own[6]))
    eighth = mlp_base.shape[1] // 2
    part_a, part_b = mlp_base[:, :eighth], mlp_base[:, eighth:]
    near_a, near_b = links.data(part_a, 0), links.data(part_b, 1)
    other += attention(plan, hold(other[0], mlp_base), other[1], other[2], kcode, qseg, heads, dim)
    o_other, near_a, near_b = lax.optimization_barrier((other[6], near_a, near_b))
    attn_part = out_project(own[6], o_other, out_weight, out_other)
    pair_a, pair_b = jnp.stack([part_a, near_a]), jnp.stack([part_b, near_b])
    far_a, far_b = links.data(pair_a, 1), links.data(pair_b, 0)
    attn_peer = links.core(attn_part)
    hidden, a_second, dmlp, gated, grad_upper, mlp_part, da_part, upb_sums, attn_sums = own_mlp(
        x_win, attn_part, attn_peer, cot_win, kept, vec_params, up_weight, down_weight, upb_own
    )
    down, up = Reduction(links, dot(dmlp, gated, 0, 0)), Reduction(links, dot(a_second, grad_upper, 0, 0))
    down_sent, up_sent = down.send(0), up.send(1)
    down_got, up_got = links.data(down_sent, 0), links.data(up_sent, 1)
    gated, grad_upper, mlp_part, *da_parts, upb_sums_other = other_mlp(
        spots, hold(a_second, down_sent, up_sent), dmlp, mlp_part, da_part,
        (mlp_base, near_a, near_b, far_a, far_b), upb_other,
    )
    da_peers = [links.core(part) for part in da_parts]
    gated, grad_upper, down_got, up_got = lax.optimization_barrier(
        (gated, grad_upper, down_got, up_got)
    )
    down.take(down_got)
    up.take(up_got)
    down_other = Reduction(links, dot(dmlp, gated, 0, 0))
    up_other = Reduction(links, dot(a_second, grad_upper, 0, 0))
    down_sent, up_sent = down_other.send(0), up_other.send(1)
    down_got, up_got = links.data(down_sent, 0), links.data(up_sent, 1)
    def my_rows(array):
        return lax.dynamic_slice_in_dim(array, core * half_rows, half_rows, 0)

    def peer_rows(array):
        return lax.dynamic_slice_in_dim(array, (1 - core) * half_rows, half_rows, 0)

    mlp_sum = my_rows(mlp_part) + links.core(peer_rows(mlp_part))
    result_mine = my_rows(hidden) + mlp_sum
    cut = width // 2
    result_far = [links.half(result_mine[:, :cut])]
    mlp_mine = mlp_sum + vec_params[5]
    mlp_sq = jnp.sum(my_rows(kept[:, :1]) * mlp_mine * mlp_mine)
    dh, dattn, do_own, do_other, row_sums = hidden_back(
        hold(hidden, down_sent, up_sent, result_mine), da_parts, da_peers, cot_win, kept, vec_params,
        out_weight, out_other,
    )

    *draws, own_sums = attention_back(plan, own, do_own, head_cols, kcode, qseg, heads, dim)
    down_other.take(hold(down_got, draws[1]))
    up_other.take(hold(up_got, draws[1]))
    down.array = jnp.concatenate([down.array, down_other.array], axis=-1)
    up.array = jnp.concatenate([up.array, up_other.array], axis=-1)
    down_sent, up_sent = down.send(1), up.send(0)
    down_got, up_got = links.data(down_sent, 1), links.data(up_sent, 0)
    result_near = links.core(result_mine)
    result_far.append(links.half(hold(result_mine, draws[1])[:, cut:]))
    *draws, other_sums = attention_back(
        plan, other, hold(do_other, down_sent, up_sent, result_far[0], result_near), other_cols, kcode,
        qseg, heads, dim, draws,
    )
    down.take(hold(down_got, draws[1]))
    up.take(hold(up_got, draws[1]))
    mlp = Reduction(links, jnp.zeros((width, 1), F32))
    mlp.left = list(down.left)
    mlp_sent = jnp.concatenate([down.array[..., units:], up.array[..., units:]], axis=-1)
    mlp.kept = jnp.concatenate([down.array[..., :units], up.array[..., :units]], axis=-1)
    mlp_got = links.half(mlp_sent)
    *draws, _, result_right = lax.optimization_barrier((*draws, mlp_sent, result_far[1]))
    result_far[1] = result_right
    result_far_near = links.core(jnp.stack(result_far))
    qk_own, qk_other, value_out = last_gradients(a_first, dattn, *draws, own[6], other[6])
    last_bits = list(mlp.left)
    value_out = Reduction(links, value_out)
    value_out_sent = value_out.send(0)
    qk_got, value_out_got = links.half(qk_other), links.data(value_out_sent, 0)
    da1_part = dot(draws[0], qk_cat, 0, 0) + dot(draws[1], value_cat, 0, 0)
    da1_sent = peer_rows(da1_part)
    da1_peer = links.core(da1_sent)
    grad_left, grad_right, first_sums = input_back(
        jnp.full((1,), core, jnp.int32), hold(da1_part, result_far_near), da1_peer, x_win, dh, vec_params
    )
    grad_nears = [links.core(grad_left), links.core(grad_right)]
    far_left = links.half(grad_left)

    mlp.take(hold(mlp_got, grad_left))
    mlp_sent = mlp.send(last_bits[0])
    mlp_got = links.data(mlp_sent, last_bits[0])
    value_out.take(hold(value_out_got, grad_left))
    value_out_sent = value_out.send(1)
    value_out_got = links.data(value_out_sent, 1)
    rows = width // links.dp_size
    first_row = links.dp * rows
    old_shares = (
        lax.dynamic_slice_in_dim(qkv_weight, first_row, rows, 1),
        lax.dynamic_slice_in_dim(out_weight, first_row, rows, 1),
        lax.dynamic_slice_in_dim(up_weight, first_row, rows, 0),
        lax.dynamic_slice_in_dim(down_weight, first_row, rows, 1).T,
    )
    query_key = Reduction(links, qk_own + hold(qk_got, value_out_sent, *old_shares))
    query_key_sent = query_key.send(0)
    query_key_got = links.data(query_key_sent, 0)
    core_index = jnp.full((1,), core, jnp.int32)
    mine, away = pack_small(
        core_index, hold(first_sums, query_key_sent), row_sums, kept, attn_sums, mlp_sq.reshape(1),
        own_sums, other_sums, upb_sums, upb_sums_other,
    )
    summed = mine + links.half(away)
    value_out.take(hold(value_out_got, query_key_sent, mlp_got))
    value_out_sent = value_out.send("half")
    value_out_got = links.half(value_out_sent)
    one = jnp.ones((1,), F32)
    result_mine = hold(result_mine, query_key_sent)
    result = join_sequence(
        links, [(result_mine, result_near, far, result_far_near) for far in result_far], parting,
        seq_len, window, one, vec_params[5:6],
    )
    query_key.take(hold(query_key_got, summed, result, far_left))
    query_key_sent = query_key.send(1)
    query_key_got = links.data(query_key_sent, 1)
    summed = hold(summed, query_key_sent)
    shared = summed[:8]
    summed = jnp.concatenate([shared + links.core(shared), summed[8:]], axis=0)
    value_out_got = hold(value_out_got, query_key_sent)
    value_out.take(value_out_got)
    far_right = links.half(hold(grad_right, value_out_got))
    far_near_left = links.core(hold(far_left, value_out_got))
    query_key.take(hold(query_key_got, summed))
    last = Reduction(links, jnp.zeros((width, 1), F32))
    last.left = list(last_bits)
    last.array = jnp.concatenate([query_key.array, value_out.array], axis=-1)
    last_sent = last.send(last_bits[0])
    last_got = links.data(last_sent, last_bits[0])
    summed = hold(summed, last_sent)
    summed = links.sum_data(summed)
    mlp.take(mlp_got)
    for bit in last_bits[1:]:
        mlp.step(bit)
    last_got, summed = lax.optimization_barrier((last_got, summed))
    last.take(last_got)
    while last.left:
        last.step(last.left[0])
    last_share = last.array

    vec_grad = summed[:6]
    stats = summed[6, :3]
    tail = summed[8:].reshape(-1)
    head_grad = tail[: head_params.size].reshape(head_params.shape)
    head_rows = -(-own_sums.shape[1] // width)
    bup_grad = tail[head_rows * width : head_rows * width + units]
    count = stats[0]
    scale = seq_len * links.dp_size / count
    shares = (last_share, last_share, mlp.array, mlp.array)
    first_dp = links.dp == 0
    first_mp = links.mp == 0
    big_sq = jnp.sum(last_share * last_share) + jnp.sum(mlp.array * mlp.array)
    split_sq = jnp.sum(summed[8:] * summed[8:])
    whole_sq = jnp.sum(summed[:6] * summed[:6])
    raw_sq = (
        big_sq + jnp.where(first_dp, split_sq, 0.0) + jnp.where(first_dp & first_mp, whole_sq, 0.0)
    )
    raw_sq = raw_sq + links.core(raw_sq)
    raw_sq = raw_sq + links.half(raw_sq)
    far_right = hold(far_right, raw_sq)
    far_near_right = links.core(far_right)
    sq_total = links.sum_data(raw_sq)
    grad_norm = scale * jnp.sqrt(sq_total)
    factor = jnp.minimum(1.0, CLIP_LIMIT / (grad_norm + 1e-06)) * scale
    steps_f = step_count[0].astype(F32)
    corr_one = 1.0 - BETA_ONE**steps_f
    corr_two = 1.0 - BETA_TWO**steps_f
    grad_input = join_sequence(
        links,
        [
            (grad_left, grad_nears[0], far_left, far_near_left),
            (grad_right, grad_nears[1], far_right, far_near_right),
        ],
        parting, seq_len, window, scale.reshape(1), jnp.zeros((1, width), F32),
    )
    new_qkv, new_out, new_up, new_down, new_head, new_vec = update(
        jnp.stack([factor, corr_one, corr_two]),
        [
            (old_shares[0], shares[0], qkv_first, qkv_second),
            (old_shares[1], shares[1], out_first, out_second),
            (old_shares[2], shares[2], up_first, up_second),
            (old_shares[3], shares[3], down_first.T, down_second.T),
            (head_params, head_grad, head_first, head_second),
            (vec_params, vec_grad, vec_first, vec_second),
        ],
        (WEIGHT_DECAY,) * 4 + (0.0,) * 2,
    )
    new_down = [array.T for array in new_down]
    new_upb = adam_step(
        up_bias, bup_grad, upb_first, upb_second, factor, corr_one, corr_two, 0.0
    )
    rms = jnp.sqrt(stats[1:] / (count * width))
    return (
        result, grad_input, *new_qkv, *new_out, *new_up, *new_down, *new_head, *new_upb, *new_vec,
        grad_norm.reshape(1), rms,
    )


def solution(mesh):
    seq = P("dp", None, None)
    row = P("dp", None)
    qkv = P(None, "dp", "mp")
    out = P("mp", "dp")
    up = P("dp", "mp")
    head = P(None, "mp", None)
    unit = P("mp")
    whole = P()
    return jax.shard_map(
        local,
        mesh=mesh,
        in_specs=(
            *(seq, seq, row, row, whole),
            *(P(None, None, "mp"), qkv, qkv),
            *(P("mp", None), out, out),
            *(P(None, "mp"), up, up),
            *(P("mp", None), out, out),
            *(head, head, head),
            *(unit, unit, unit),
            *(whole, whole, whole),
        ),
        out_specs=(
            *(seq, seq),
            *(qkv, qkv, qkv),
            *(out, out, out),
            *(up, up, up),
            *(out, out, out),
            *(head, head, head),
            *(unit, unit, unit),
            *(whole, whole, whole),
            *(whole, whole),
        ),
        check_vma=False,
    )
```
